32 devices in a mesh: seq: 4 (over y, x), tp: 8 (over z, core).
Axes of the slice: x: 2, y: 2, z: 4, core: 2. Of those that a mesh axis runs over, the one named last changes fastest.
Arguments:
- tokens: bfloat16 [4096, 4096], P('seq'), may hold values from -32 to 32
- w_query: bfloat16 [4096, 2048], P(None, 'tp'), may hold values from -0.109375 to 0.109375
- w_key: bfloat16 [4096, 512], P(None, 'tp'), may hold values from -0.078125 to 0.078125
- w_value: bfloat16 [4096, 512], P(None, 'tp'), may hold values from -0.09375 to 0.09375
- w_out: bfloat16 [2048, 4096], P('tp'), may hold values from -0.1875 to 0.1875
- seg_ids: int32 [4096], replicated, may hold values from 0 to 31, as said below
- owner_counts: int32 [8], replicated, may hold values from 1 to 8, 32 in all
- centroids: bfloat16 [16384, 4096], P('seq', 'tp'), may hold values from -1.5 to 1.5
- pool_gain: float32 [4096], P('tp'), may hold values from 0.1 to 1.9
- assign: int32 [32], replicated, may hold values from 0 to 16383
Outputs:
- distances: float32 [64, 16384], P('tp', 'seq')
- updated: float32 [16384, 4096], P('seq', 'tp')
The draws below stay inside these ranges and needn't reach their ends.
Inputs may be any that keep to these rules, and one draw needn't show every extreme that they name: `seg_ids`: ids never fall along the sequence; every id occurs; one instruction spans exactly 4065 tokens. `owner_counts`: the counts sum to 32; one owner holds exactly 8 rows.
All inputs are finite; a program needn't handle non-finite values.
Results may differ from the reference program's by a relative error of at most 0.0007.
Values may be sent and summed in bfloat16 or wider, within the bound.
No kernel may reach another device: no remote copies, remote signals or barrier semaphores. Data moves between devices by JAX's collectives and lax.ppermute only.
A program may use at most 192 MiB of HBM per device.

```python
import math
import jax
import jax.numpy as jnp
import numpy as np
from jax import lax

D = 4096
HD = 128
WINDOW = 4096
QBLOCK = 512
NC = 16384
HEADS = 16
KVH = 4
SEQLEN = 4096
NI = 32
MOST = 4065
OWNERS = 8
CAP = 8


def draw_tokens(key, part):
    base_key = jax.random.fold_in(key, 101)
    col_scale = jnp.exp(jax.random.uniform(jax.random.fold_in(key, 102), (D,), jnp.float32, math.log(0.3), math.log(3.0)))
    base_draw = jnp.clip(jax.random.normal(base_key, (SEQLEN, D), jnp.float32), -4.0, 4.0)
    return jnp.clip(base_draw * col_scale[None, :], -32.0, 32.0).astype(jnp.bfloat16)


def linked_weights(key):
    key_draw = jnp.clip(jax.random.normal(jax.random.fold_in(key, 201), (D, KVH * HD), jnp.float32), -5.0, 5.0) * D ** (-0.5)
    noise_draw = jnp.clip(jax.random.normal(jax.random.fold_in(key, 202), (D, HEADS * HD), jnp.float32), -5.0, 5.0) * D ** (-0.5)
    return (key_draw, noise_draw)


def draw_w_key(key, part):
    return linked_weights(key)[0].astype(jnp.bfloat16)


def draw_w_query(key, part):
    key_draw, noise_draw = linked_weights(key)
    return noise_draw.astype(jnp.bfloat16)


def draw_seg_ids(key, part):
    rest_len = SEQLEN - MOST
    spacing = rest_len // (NI - 1)
    jitter = jax.random.randint(jax.random.fold_in(key, 301), (NI - 2,), 0, max(spacing, 1))
    cuts = (jnp.arange(1, NI - 1, dtype=jnp.int32) * spacing + jitter).astype(jnp.int32)
    long_id = jax.random.randint(jax.random.fold_in(key, 302), (), 0, NI).astype(jnp.int32)
    bounds = jnp.concatenate([jnp.zeros((1,), jnp.int32), cuts, jnp.full((1,), rest_len, jnp.int32)], 0)
    long_start = jnp.sum(jnp.where(jnp.arange(NI, dtype=jnp.int32) == long_id, bounds, 0)).astype(jnp.int32)
    where_at = jnp.arange(SEQLEN, dtype=jnp.int32)
    before = jnp.sum((cuts[None, :] <= where_at[:, None]).astype(jnp.int32), axis=1)
    shifted = where_at - MOST
    after = 1 + jnp.sum((cuts[None, :] <= shifted[:, None]).astype(jnp.int32), axis=1)
    ids = jnp.where(where_at < long_start, before, jnp.where(where_at < long_start + MOST, long_id, after))
    return ids.astype(jnp.int32)


def touch_ends(result, key, smallest, top_value):
    spot = [jax.random.randint(jax.random.fold_in(key, axis), (), 0, length) for axis, length in enumerate(result.shape)]
    main_axis = result.shape.index(max(result.shape))
    neighbour = spot[:main_axis] + [(spot[main_axis] + 1) % result.shape[main_axis]] + spot[main_axis + 1:]
    return result.at[tuple(spot)].set(smallest).at[tuple(neighbour)].set(top_value)


def spiked(result, key, source, target, shards_of, factor):
    owner, partner = [(jnp.arange(result.shape[dim]) // (result.shape[dim] // shards_of)).reshape([-1 if axis == dim else 1 for axis in range(result.ndim)]) for dim in (source, target)]
    chosen = jax.random.permutation(key, shards_of)[partner]
    strong = (owner == chosen) | (owner == (partner + shards_of // 2) % shards_of)
    return jnp.where(strong, factor * result, result)


def block_levels(stream_key, dims, cuts, smallest, top_value):
    gain, own = 1.0, jax.random.fold_in(stream_key, 6)
    for position, shards_of in cuts:
        draws = jnp.exp(jax.random.uniform(jax.random.fold_in(own, position), (shards_of,), jnp.float32, smallest / len(cuts), top_value / len(cuts)))
        gain = gain * jnp.repeat(draws, dims[position] // shards_of).reshape([-1 if axis == position else 1 for axis in range(len(dims))])
    return gain


def profile(amount, total, limit, skew):
    loads = [(1 << 20) // math.isqrt(grade ** skew) + 1 for grade in range(2, amount + 1)]
    surplus, holding = total - limit - (amount - 1), [1] * (amount - 1)
    while surplus > 0:
        free = [i for i in range(amount - 1) if holding[i] < limit]
        mass, budget = sum([loads[i] for i in free]), surplus
        for i in free:
            extra = min(limit - holding[i], max(1, budget * loads[i] // mass), surplus)
            holding[i] = holding[i] + extra
            surplus = surplus - extra
    return np.array([limit] + holding)


def uneven(stream_key, number_of, total, bound, lean):
    if number_of == 2:
        one = jax.random.randint(stream_key, (), max(1, total - bound), min(bound, total - 1) + 1)
        return jnp.stack([one, total - one])
    tallies = jnp.asarray(profile(number_of, total, bound, lean), jnp.int32)
    pairs = (number_of - 1) // 2
    giver, taker = tallies[1:1 + 2 * pairs:2], tallies[2:2 + 2 * pairs:2]
    slack = jnp.minimum(giver - 1, bound - taker)
    moved = jax.random.randint(jax.random.fold_in(stream_key, 1), (pairs,), 0, 1 << 20) % (slack + 1)
    tallies = tallies.at[1:1 + 2 * pairs:2].set(giver - moved).at[2:2 + 2 * pairs:2].set(taker + moved)
    return tallies[jax.random.permutation(jax.random.fold_in(stream_key, 2), number_of)]


def centred(rng, shape, deviation, limit, split=(), held_as=jnp.bfloat16):
    drawn = deviation * jax.random.normal(rng, shape, jnp.float32)
    if split:
        drawn = drawn * block_levels(rng, shape, split, -0.22, 0.18)
    return jnp.clip(drawn, -limit, limit).astype(held_as)


def heavy_noise(key, extent, spread, bound, pieces, heavy, kind=jnp.bfloat16):
    entries = spread * jax.random.normal(key, extent, jnp.float32)
    if pieces:
        entries = entries * block_levels(key, extent, pieces, -0.22, 0.18)
    return jnp.clip(spiked(entries, jax.random.fold_in(key, 3), *heavy), -bound, bound).astype(kind)


def setup_inputs(seed: int = 0) -> dict:
    seeds = jax.random.split(jax.random.key(seed), 11)
    tokens = draw_tokens(jax.random.fold_in(seeds[10], 71), 0)
    w_query = draw_w_query(jax.random.fold_in(seeds[10], 71), 0)
    w_key = draw_w_key(jax.random.fold_in(seeds[10], 71), 0)
    w_value = centred(seeds[3], (D, KVH * HD), D ** -0.5, 0.09375, ((1, 8),))
    w_out = heavy_noise(seeds[4], (HEADS * HD, D), (HEADS * HD) ** -0.5, 0.1875, ((0, 8),), (0, 1, 8, 2.0))
    seg_ids = draw_seg_ids(jax.random.fold_in(seeds[10], 71), 0)
    owner_counts = uneven(seeds[6], OWNERS, NI, CAP, 2).astype(jnp.int32)
    centroids = centred(seeds[7], (NC, D), 0.25, 1.5, ((0, 4), (1, 8)))
    pool_gain = jnp.clip(1.0 + 0.18 * jax.random.normal(seeds[8], (D,), jnp.float32), 0.1, 1.9)
    assign = touch_ends(jax.random.randint(seeds[9], (NI,), 0, NC), jax.random.fold_in(seeds[9], 1), 0, NC - 1).astype(jnp.int32)
    return {"tokens": tokens, "w_query": w_query, "w_key": w_key, "w_value": w_value, "w_out": w_out, "seg_ids": seg_ids, "owner_counts": owner_counts, "centroids": centroids, "pool_gain": pool_gain, "assign": assign}


rope_theta = 10000.0
norm_eps = 1e-06

def rotate_pairs(vectors, positions, first_pair, head_size):
    cols = vectors.shape[-1]
    pair_index = (first_pair + jnp.arange(cols // 2)).astype(jnp.float32)
    inverse = jnp.exp(-(2.0 * pair_index / head_size) * math.log(rope_theta))
    angles = positions.astype(jnp.float32)[:, None] * inverse[None, :]
    cosine = jnp.cos(angles)[:, None, :]
    sine = jnp.sin(angles)[:, None, :]
    paired = vectors.reshape(vectors.shape[:-1] + (cols // 2, 2))
    even_part = paired[..., 0]
    odd_part = paired[..., 1]
    turned = jnp.stack([even_part * cosine - odd_part * sine, even_part * sine + odd_part * cosine], -1)
    return turned.reshape(vectors.shape)

def reference(tokens, w_query, w_key, w_value, w_out, seg_ids, owner_counts, centroids, pool_gain, assign):
    seq_len, model_width = tokens.shape
    head_total = w_query.shape[1] // HD
    kv_total = w_key.shape[1] // HD
    group_size = head_total // kv_total
    positions = jnp.arange(seq_len, dtype=jnp.int32)
    queries = rotate_pairs(jnp.dot(tokens, w_query, preferred_element_type=jnp.float32).reshape(seq_len, head_total, HD), positions, 0, HD).astype(jnp.bfloat16)
    key_rows = rotate_pairs(jnp.dot(tokens, w_key, preferred_element_type=jnp.float32).reshape(seq_len, kv_total, HD), positions, 0, HD).astype(jnp.bfloat16)
    value_rows = jnp.dot(tokens, w_value, preferred_element_type=jnp.float32).astype(jnp.bfloat16).reshape(seq_len, kv_total, HD)
    key_rows = jnp.repeat(key_rows, group_size, axis=1)
    value_rows = jnp.repeat(value_rows, group_size, axis=1)
    pad_keys = jnp.concatenate([jnp.zeros((WINDOW, head_total, HD), jnp.bfloat16), key_rows], 0)
    pad_values = jnp.concatenate([jnp.zeros((WINDOW, head_total, HD), jnp.bfloat16), value_rows], 0)
    pad_ids = jnp.concatenate([jnp.full((WINDOW,), -1, jnp.int32), seg_ids.astype(jnp.int32)], 0)
    distance_grid = jnp.arange(QBLOCK)[:, None] + WINDOW - jnp.arange(WINDOW + QBLOCK)[None, :]

    def attend_block(block_index):
        q_start = (block_index * QBLOCK).astype(jnp.int32)
        q_block = lax.dynamic_slice_in_dim(queries, q_start, QBLOCK, 0)
        k_block = lax.dynamic_slice_in_dim(pad_keys, q_start, WINDOW + QBLOCK, 0)
        v_block = lax.dynamic_slice_in_dim(pad_values, q_start, WINDOW + QBLOCK, 0)
        q_ids = lax.dynamic_slice_in_dim(seg_ids.astype(jnp.int32), q_start, QBLOCK, 0)
        k_ids = lax.dynamic_slice_in_dim(pad_ids, q_start, WINDOW + QBLOCK, 0)
        allowed = (distance_grid >= 0) & (distance_grid < WINDOW) & (q_ids[:, None] == k_ids[None, :])
        scores = jnp.einsum('qhd,khd->hqk', q_block.astype(jnp.float32), k_block.astype(jnp.float32)) * HD ** (-0.5)
        scores = jnp.where(allowed[None], scores, -1e+30)
        highest = lax.optimization_barrier(jnp.max(scores, axis=-1, keepdims=True))
        weights = jnp.exp(scores - highest)
        soft_weights = (weights / lax.optimization_barrier(jnp.sum(weights, axis=-1, keepdims=True))).astype(jnp.bfloat16)
        head_out = jnp.einsum('hqk,khd->qhd', soft_weights.astype(jnp.float32), v_block.astype(jnp.float32)).astype(jnp.bfloat16)
        return head_out.reshape(QBLOCK, head_total * HD)
    attention = lax.map(attend_block, jnp.arange(seq_len // QBLOCK, dtype=jnp.int32)).reshape(seq_len, head_total * HD)
    hidden = tokens.astype(jnp.float32) + jnp.dot(attention, w_out, preferred_element_type=jnp.float32)
    seg_total = assign.shape[0]
    seg_sums = jax.ops.segment_sum(hidden, seg_ids, seg_total)
    counts = jax.ops.segment_sum(jnp.ones((seq_len,), jnp.float32), seg_ids, seg_total)
    pooled = seg_sums / counts[:, None]
    mean_square = lax.optimization_barrier(jnp.mean(pooled * pooled, axis=1, keepdims=True))
    embedding = pooled * lax.rsqrt(mean_square + norm_eps) * pool_gain.astype(jnp.float32)[None, :]
    cross_term = jnp.dot(embedding.astype(jnp.bfloat16), centroids.T, preferred_element_type=jnp.float32)
    cent_float = centroids.astype(jnp.float32)
    cent_norm = lax.optimization_barrier(jnp.sum(cent_float * cent_float, axis=1))
    row_terms = (cent_norm[None, :] - 2.0 * cross_term) / model_width ** 0.5
    owners = owner_counts.shape[0]
    capacity = 2 * seg_total // owners
    starts = (jnp.cumsum(owner_counts) - owner_counts).astype(jnp.int32)
    slot_index = jnp.arange(capacity, dtype=jnp.int32)
    slot_rows = (starts[:, None] + slot_index[None, :]).reshape(-1)
    slot_valid = (slot_index[None, :] < owner_counts[:, None]).reshape(-1)
    picked = jnp.take(row_terms, jnp.clip(slot_rows, 0, seg_total - 1).astype(jnp.int32), axis=0)
    distances = jnp.where(slot_valid[:, None], picked, 0.0)
    cent_sums = jax.ops.segment_sum(embedding, assign, cent_float.shape[0])
    cent_counts = jax.ops.segment_sum(jnp.ones((seg_total,), jnp.float32), assign, cent_float.shape[0])
    updated = (cent_float + cent_sums) / (1.0 + cent_counts)[:, None]
    return (distances, updated)
```

```python
import math

import jax
import jax.numpy as jnp
import numpy as np
from jax import lax
from jax.experimental import pallas as pl
from jax.experimental.pallas import tpu as pltpu
from jax.sharding import PartitionSpec as P

HD = 128
WINDOW = 4096
QB = 256
KB = 512
LANES = 128
GROUP = 16

rope_theta = 10000.0
norm_eps = 1e-06
VMEM_LIMIT = 56 * 1024 * 1024

f32 = jnp.float32
bf16 = jnp.bfloat16
i32 = jnp.int32


def swapped(x, axis, mask):
    count = lax.axis_size(axis)
    return lax.ppermute(x, axis, [(i, i ^ mask) for i in range(count)])


def angle_tables(seq_len):
    inverse = np.exp(-(2.0 * np.arange(HD // 2) / HD) * math.log(rope_theta))
    inverse = np.repeat(inverse, 2)[None, :]
    fine = np.arange(LANES)[:, None] * inverse
    coarse = LANES * np.arange(seq_len // LANES)[:, None] * inverse
    fine_tab = np.stack([np.cos(fine), np.sin(fine)]).astype(np.float32)
    coarse_tab = np.stack([np.cos(coarse), np.sin(coarse)]).astype(np.float32)
    return fine_tab, coarse_tab


def turn(fine, coarse, which):
    ca = coarse[0, pl.ds(which, 1), :]
    sa = coarse[1, pl.ds(which, 1), :]
    cb = fine[0]
    sb = fine[1]
    return ca * cb - sa * sb, sa * cb + ca * sb


def pair_swap(x, even):
    up = pltpu.roll(x, x.shape[1] - 1, 1)
    down = pltpu.roll(x, 1, 1)
    return jnp.where(even, up, down)


def kv_body(tok, wk, wv, fine, coarse, k_out, v_out, w_both):
    step = pl.program_id(0)
    half = wk.shape[1]
    rows = tok.shape[0]
    subs = rows // LANES

    @pl.when(step == 0)
    def _():
        w_both[:, :half] = wk[...]
        w_both[:, half:] = wv[...]

    both = jnp.dot(tok[...], w_both[...], preferred_element_type=f32)
    lane = lax.broadcasted_iota(i32, (LANES, LANES), 1)
    even = lane % 2 == 0
    upper = lax.axis_index("tp") % 2 == 1
    first = lax.axis_index("seq") * (pl.num_programs(0) * subs) + step * subs
    for sub in range(subs):
        cos, sin = turn(fine, coarse, first + sub)
        cos = jnp.where(upper, pltpu.roll(cos, half, 1), cos)
        sin = jnp.where(upper, pltpu.roll(sin, half, 1), sin)
        cos = jnp.where(lane < half, cos, 1.0)
        sin = jnp.where(lane < half, jnp.where(even, -sin, sin), 0.0)
        x = both[sub * LANES : (sub + 1) * LANES]
        x = x * cos + pair_swap(x, even) * sin
        x = x.T
        k_out[:, sub * LANES : (sub + 1) * LANES] = x[:half].astype(bf16)
        v_out[:, sub * LANES : (sub + 1) * LANES] = x[half:].astype(bf16)


def project_kv(tokens, w_key, w_value, fine, coarse):
    rows, width = tokens.shape
    half = w_key.shape[1]
    block = 256
    whole = lambda a: pl.BlockSpec(a.shape, lambda i: (0,) * a.ndim)
    out = jax.ShapeDtypeStruct((half, rows), bf16)
    return pl.pallas_call(
        kv_body,
        grid=(rows // block,),
        in_specs=[
            pl.BlockSpec((block, width), lambda i: (i, 0)),
            whole(w_key),
            whole(w_value),
            whole(fine),
            whole(coarse),
        ],
        out_specs=[pl.BlockSpec((half, block), lambda i: (0, i))] * 2,
        out_shape=[out, out],
        scratch_shapes=[pltpu.VMEM((width, 2 * half), bf16)],
        compiler_params=pltpu.CompilerParams(vmem_limit_bytes=VMEM_LIMIT),
        name="project_kv",
    )(tokens, w_key, w_value, fine, coarse)


def q_body(tok, wq, fine, coarse, q_out):
    step = pl.program_id(0)
    rows = tok.shape[0]
    subs = rows // LANES
    heads = wq.shape[1] // HD
    x_all = jnp.dot(tok[...], wq[...], preferred_element_type=f32)
    lane = lax.broadcasted_iota(i32, (LANES, LANES), 1)
    even = lane % 2 == 0
    first = lax.axis_index("seq") * (pl.num_programs(0) * subs) + step * subs
    scale = HD ** (-0.5) * math.log2(math.e)
    for sub in range(subs):
        cos, sin = turn(fine, coarse, first + sub)
        cos = cos * scale
        sin = jnp.where(even, -sin, sin) * scale
        for h in range(heads):
            x = x_all[sub * LANES : (sub + 1) * LANES, h * HD : (h + 1) * HD]
            x = x * cos + pair_swap(x, even) * sin
            q_out[sub * LANES : (sub + 1) * LANES, h * HD : (h + 1) * HD] = x.astype(bf16)


def project_q(tokens, w_query, fine, coarse):
    rows, width = tokens.shape
    cols = w_query.shape[1]
    block = 256
    whole = lambda a: pl.BlockSpec(a.shape, lambda i: (0,) * a.ndim)
    return pl.pallas_call(
        q_body,
        grid=(rows // block,),
        in_specs=[
            pl.BlockSpec((block, width), lambda i: (i, 0)),
            whole(w_query),
            whole(fine),
            whole(coarse),
        ],
        out_specs=pl.BlockSpec((block, cols), lambda i: (i, 0)),
        out_shape=jax.ShapeDtypeStruct((rows, cols), bf16),
        compiler_params=pltpu.CompilerParams(vmem_limit_bytes=VMEM_LIMIT),
        name="project_q",
    )(tokens, w_query, fine, coarse)


def cent_body(base, cent, cent_any, wide, norms, picked, sems):
    step = pl.program_id(0)
    count = base.shape[0]

    def fetch(r):
        start = pl.multiple_of(base[r], GROUP)
        return pltpu.make_async_copy(
            cent_any.at[pl.ds(start, GROUP), :], picked.at[pl.ds(r * GROUP, GROUP), :], sems.at[r]
        )

    @pl.when(step == 0)
    def _():
        for r in range(count):
            fetch(r).start()

    c = cent[...].astype(f32)
    wide[...] = c
    square = c * c
    high = square.astype(bf16)
    low = (square - high.astype(f32)).astype(bf16)
    ones = jnp.ones((8, c.shape[1]), bf16)
    contract = (((1,), (1,)), ((), ()))
    total = lax.dot_general(ones, high, contract, preferred_element_type=f32)
    total = total + lax.dot_general(ones, low, contract, preferred_element_type=f32)
    norms[pl.ds(step, 1), :] = total[:1]

    @pl.when(step == pl.num_programs(0) - 1)
    def _():
        for r in range(count):
            fetch(r).wait()


def widen_centroids(base, centroids):
    rows, feat = centroids.shape
    count = base.shape[0]
    block = rows // 8
    spec = pltpu.PrefetchScalarGridSpec(
        num_scalar_prefetch=1,
        grid=(8,),
        in_specs=[
            pl.BlockSpec((block, feat), lambda i, b: (i, 0)),
            pl.BlockSpec(memory_space=pl.ANY),
        ],
        out_specs=[
            pl.BlockSpec((block, feat), lambda i, b: (i, 0)),
            pl.BlockSpec((8, block), lambda i, b: (0, 0)),
            pl.BlockSpec((count * GROUP, feat), lambda i, b: (0, 0)),
        ],
        scratch_shapes=[pltpu.SemaphoreType.DMA((count,))],
    )
    return pl.pallas_call(
        cent_body,
        grid_spec=spec,
        out_shape=[
            jax.ShapeDtypeStruct((rows, feat), f32),
            jax.ShapeDtypeStruct((8, block), f32),
            jax.ShapeDtypeStruct((count * GROUP, feat), bf16),
        ],
        compiler_params=pltpu.CompilerParams(vmem_limit_bytes=VMEM_LIMIT),
        name="widen_centroids",
    )(base, centroids, centroids)


def attend_body(pieces, seg_total, seg, q_ref, seg_row, *refs):
    keys_in = refs[: 2 * pieces]
    values_in = refs[2 * pieces : 4 * pieces]
    out, counts, kt, vt, sc, col, lhs, sems = refs[4 * pieces :]
    rows = q_ref.shape[0]
    heads = q_ref.shape[1] // HD
    half = HD // 2
    seq_len = kt.shape[1]
    rank = lax.axis_index("seq")
    parity = lax.axis_index("tp") % 2

    def copies(sources, target, first):
        result = []
        for k in range(2):
            for m in range(pieces):
                row0 = pl.multiple_of((parity ^ k) * half, half)
                col0 = pl.multiple_of((rank ^ m) * rows, rows)
                index = k * pieces + m
                result.append(
                    pltpu.make_async_copy(
                        sources[index],
                        target.at[pl.ds(row0, half), pl.ds(col0, rows)],
                        sems.at[first + index],
                    )
                )
        return result

    key_copies = copies(keys_in, kt, 0)
    value_copies = copies(values_in, vt, 2 * pieces)
    for c in key_copies:
        c.start()
    for c in value_copies:
        c.start()
    col[...] = jnp.zeros(col.shape, f32)
    for c in key_copies:
        c.wait()

    def q_step(b, carry):
        base = rank * rows + b * QB
        last_seg = seg[base + QB - 1]
        first_seg = seg[base]
        end = (base + QB - 1) // KB + 1
        clear_end = base // KB
        begin = jnp.int32(0)
        clear = jnp.int32(0)
        for t in range(seq_len // KB):
            begin = begin + (seg[t * KB + KB - 1] < first_seg).astype(i32)
            outside = (seg[t * KB] != last_seg) | (base + QB - 1 - t * KB >= WINDOW)
            clear = clear + (outside & (t < clear_end)).astype(i32)
        begin = jnp.maximum(begin, jnp.maximum(base - (WINDOW - 1), 0) // KB)
        begin = jnp.minimum(begin, clear_end)
        clear = jnp.clip(clear, begin, clear_end)
        own = jnp.broadcast_to(seg_row[:, pl.ds(base, QB)].astype(f32), (LANES, QB)).T
        i_pos = base + lax.broadcasted_iota(i32, (QB, LANES), 0)

        for h in range(heads):
            q = q_ref[pl.ds(b * QB, QB), h * HD : (h + 1) * HD]

            def score(masked, kb, top):
                start = pl.multiple_of(kb * KB, KB)
                s = jnp.dot(q, kt[:, pl.ds(start, KB)], preferred_element_type=f32)
                for g in range(KB // LANES):
                    part = s[:, g * LANES : (g + 1) * LANES]
                    at = pl.multiple_of(start + g * LANES, LANES)
                    if masked:
                        j_pos = at + lax.broadcasted_iota(i32, (QB, LANES), 1)
                        ids = seg_row[:, pl.ds(at, LANES)].astype(f32)
                        allowed = (j_pos <= i_pos) & (own == ids)
                        if seq_len > WINDOW:
                            allowed = allowed & (i_pos - j_pos < WINDOW)
                        part = jnp.where(allowed, part, -1e30)
                    sc[:, pl.ds(at, LANES)] = part
                    top = jnp.maximum(top, part)
                return top

            top = jnp.full((QB, LANES), -1e30, f32)
            top = lax.fori_loop(begin, clear, lambda kb, t: score(True, kb, t), top)
            top = lax.fori_loop(clear, clear_end, lambda kb, t: score(False, kb, t), top)
            top = lax.fori_loop(clear_end, end, lambda kb, t: score(True, kb, t), top)
            top = jnp.max(top, axis=1, keepdims=True)

            def weigh(kb, total):
                start = pl.multiple_of(kb * KB, KB)
                for g in range(KB // LANES):
                    at = pl.multiple_of(start + g * LANES, LANES)
                    p = jnp.exp2(sc[:, pl.ds(at, LANES)] - top)
                    sc[:, pl.ds(at, LANES)] = p
                    total = total + p
                return total

            total = lax.fori_loop(begin, end, weigh, jnp.zeros((QB, LANES), f32))
            share = 1.0 / jnp.sum(total, axis=1, keepdims=True)
            share = jnp.broadcast_to(share, (QB, LANES))

            def gather(kb, carry):
                start = pl.multiple_of(kb * KB, KB)
                for g in range(KB // LANES):
                    at = pl.multiple_of(start + g * LANES, LANES)
                    p = sc[:, pl.ds(at, LANES)] * share
                    p = jnp.sum(p.reshape(QB // 8, 8, LANES), axis=0)
                    col[h, :, pl.ds(at, LANES)] = col[h, :, pl.ds(at, LANES)] + p
                return carry

            lax.fori_loop(begin, end, gather, 0)
        return carry

    lax.fori_loop(0, rows // QB, q_step, 0)

    number = jnp.zeros((seg_total, LANES), f32)
    for g in range(seq_len // LANES):
        at = slice(g * LANES, (g + 1) * LANES)
        ids = seg_row[:, at]
        member = ids == lax.broadcasted_iota(i32, (seg_total, LANES), 0)
        number = number + member.astype(f32)
        for h in range(heads):
            w = jnp.sum(col[h, :, at], axis=0, keepdims=True)
            w = jnp.where(member, w, 0.0)
            high = w.astype(bf16)
            lhs[h * seg_total : (h + 1) * seg_total, at] = high
            low = (w - high.astype(f32)).astype(bf16)
            lhs[(heads + h) * seg_total : (heads + h + 1) * seg_total, at] = low
    counts[...] = jnp.broadcast_to(jnp.sum(number, axis=1, keepdims=True), counts.shape)
    for c in value_copies:
        c.wait()
    pooled = lax.dot_general(
        lhs[...], vt[...], (((1,), (1,)), ((), ())), preferred_element_type=f32
    )
    for h in range(heads):
        high = pooled[h * seg_total : (h + 1) * seg_total]
        low = pooled[(heads + h) * seg_total : (heads + h + 1) * seg_total]
        out[:, h * HD : (h + 1) * HD] = high + low


def attend(seg_ids, queries, keys, values, seg_total):
    rows, cols = queries.shape
    seq_len = seg_ids.shape[0]
    pieces = len(keys) // 2
    heads = cols // HD
    whole = pl.BlockSpec(memory_space=pltpu.VMEM)
    anywhere = pl.BlockSpec(memory_space=pl.ANY)

    def body(*refs):
        attend_body(pieces, seg_total, *refs)

    return pl.pallas_call(
        body,
        in_specs=[pl.BlockSpec(memory_space=pltpu.SMEM), whole, whole] + [anywhere] * (4 * pieces),
        out_specs=[whole, whole],
        out_shape=[
            jax.ShapeDtypeStruct((seg_total, cols), f32),
            jax.ShapeDtypeStruct((seg_total, LANES), f32),
        ],
        scratch_shapes=[
            pltpu.VMEM((HD, seq_len), bf16),
            pltpu.VMEM((HD, seq_len), bf16),
            pltpu.VMEM((QB, seq_len), f32),
            pltpu.VMEM((heads, 8, seq_len), f32),
            pltpu.VMEM((2 * heads * seg_total, seq_len), bf16),
            pltpu.SemaphoreType.DMA((4 * pieces,)),
        ],
        compiler_params=pltpu.CompilerParams(vmem_limit_bytes=VMEM_LIMIT),
        name="attend",
    )(seg_ids, queries, seg_ids.reshape(1, seq_len), *keys, *values)


def mix_body(pieces, *refs):
    parts = refs[:pieces]
    norms, w_out, keep, send = refs[pieces:]
    groups, _, feat = keep.shape
    seg_total = parts[0].shape[0]
    mixed = parts[0][...]
    for p in parts[1:]:
        mixed = mixed + p[...]
    high = mixed.astype(bf16)
    low = (mixed - high.astype(f32)).astype(bf16)
    lhs = jnp.concatenate([high, low], 0)
    rank = lax.axis_index("tp")
    for k, target in enumerate((keep, send)):
        for m in range(groups):
            owner = rank ^ (2 * m + k)
            cols = pl.ds(pl.multiple_of(owner * feat, feat), feat)
            y = jnp.dot(lhs, w_out[:, cols], preferred_element_type=f32)
            target[m, :seg_total, :] = y[:seg_total] + y[seg_total:]
            target[m, seg_total:, :] = norms[...]


def mix(parts, norms, w_out, feat, groups):
    seg_total = parts[0].shape[0]
    whole = pl.BlockSpec(memory_space=pltpu.VMEM)
    out = jax.ShapeDtypeStruct((groups, seg_total + 8, feat), f32)

    def body(*refs):
        mix_body(len(parts), *refs)

    return pl.pallas_call(
        body,
        in_specs=[whole] * (len(parts) + 2),
        out_specs=[whole, whole],
        out_shape=[out, out],
        compiler_params=pltpu.CompilerParams(vmem_limit_bytes=VMEM_LIMIT),
        name="mix",
    )(*parts, norms, w_out)


def owner_span(owner_counts, owner):
    start = jnp.int32(0)
    for o in range(owner_counts.shape[0]):
        start = start + jnp.where(o < owner, owner_counts[o], 0)
    return start, owner_counts[owner]


def cross_body(groups, pieces, model_width, owner_counts, *refs):
    mixed = refs[:groups]
    pooled_in = refs[groups : groups + pieces]
    counts, gain, cent = refs[groups + pieces : groups + pieces + 3]
    keep, send, emb, norms, lhs = refs[groups + pieces + 3 :]
    step = pl.program_id(0)
    seg_total, feat = emb.shape
    block = cent.shape[0]
    slots = keep.shape[1]
    per_side = groups * slots
    rank = lax.axis_index("tp")

    @pl.when(step == 0)
    def _():
        total = mixed[0][...]
        for p in mixed[1:]:
            total = total + p[...]
        norms[...] = total[seg_total:]
        sums = total[:seg_total]
        for p in pooled_in:
            sums = sums + p[...]
        pooled = sums / counts[:, :1]
        square = jnp.sum(pooled * pooled, axis=1, keepdims=True)
        row = lax.broadcasted_iota(i32, (seg_total, LANES), 0)
        lane = lax.broadcasted_iota(i32, (seg_total, LANES), 1)
        square = jnp.sum(jnp.where(row == lane, square, 0.0), axis=0, keepdims=True)
        square = jnp.broadcast_to(square, (slots, LANES))
        scaled = pooled * gain[...]
        emb[...] = scaled
        high = scaled.astype(bf16)
        low = (scaled - high.astype(f32)).astype(bf16)
        slot = lax.broadcasted_iota(i32, (slots, seg_total), 0)
        column = lax.broadcasted_iota(i32, (slots, seg_total), 1)
        chosen = []
        for k, target in enumerate((keep, send)):
            for m in range(groups):
                start, number = owner_span(owner_counts, rank ^ (2 * m + k))
                hit = (slot + start == column) & (slot < number)
                chosen.append(jnp.where(hit, 1.0, 0.0))
                target[m, :, block * pl.num_programs(0) :] = square
        chosen = jnp.concatenate(chosen, 0).astype(bf16)
        factor = -2.0 / model_width**0.5
        lhs[: 2 * per_side] = (
            jnp.dot(chosen, high, preferred_element_type=f32) * factor
        ).astype(bf16)
        lhs[2 * per_side :] = (
            jnp.dot(chosen, low, preferred_element_type=f32) * factor
        ).astype(bf16)

    y = lax.dot_general(
        lhs[...], cent[...], (((1,), (1,)), ((), ())), preferred_element_type=f32
    )
    y = y[: 2 * per_side] + y[2 * per_side :]
    cols = pl.ds(pl.multiple_of(step * block, block), block)
    for k, target in enumerate((keep, send)):
        for m in range(groups):
            first = k * per_side + m * slots
            target[m, :, cols] = y[first : first + slots]


def cross(owner_counts, mixed, pooled_in, counts, gain, centroids, slots, model_width):
    rows, feat = centroids.shape
    groups = len(mixed)
    pieces = len(pooled_in)
    seg_total = counts.shape[0]
    block = rows // 8
    fixed = lambda shape: pl.BlockSpec(shape, lambda i, o: (0,) * len(shape))
    side = (groups, slots, rows + LANES)
    spec = pltpu.PrefetchScalarGridSpec(
        num_scalar_prefetch=1,
        grid=(8,),
        in_specs=[fixed(a.shape) for a in mixed]
        + [fixed(a.shape) for a in pooled_in]
        + [
            fixed(counts.shape),
            fixed(gain.shape),
            pl.BlockSpec((block, feat), lambda i, o: (i, 0)),
        ],
        out_specs=[fixed(side), fixed(side), fixed((seg_total, feat)), fixed((8, block))],
        scratch_shapes=[pltpu.VMEM((4 * groups * slots, feat), bf16)],
    )

    def body(*refs):
        cross_body(groups, pieces, model_width, *refs)

    return pl.pallas_call(
        body,
        grid_spec=spec,
        out_shape=[
            jax.ShapeDtypeStruct(side, f32),
            jax.ShapeDtypeStruct(side, f32),
            jax.ShapeDtypeStruct((seg_total, feat), f32),
            jax.ShapeDtypeStruct((8, block), f32),
        ],
        compiler_params=pltpu.CompilerParams(vmem_limit_bytes=VMEM_LIMIT),
        name="cross",
    )(owner_counts, *mixed, *pooled_in, counts, gain, centroids)


def finish_body(groups, model_width, owner_counts, place, *refs):
    terms = refs[:groups]
    norms, emb, assign_row, picked, wide_in, dist, wide, moved, sems = refs[groups:]
    seg_total, feat = emb.shape
    block = norms.shape[1]
    slots = dist.shape[0]
    rows = dist.shape[1]
    total = terms[0][:, rows:]
    for t in terms[1:]:
        total = total + t[:, rows:]
    scale = lax.rsqrt(total / model_width + norm_eps)
    slot = lax.broadcasted_iota(i32, (slots, LANES), 0)
    lane = lax.broadcasted_iota(i32, (slots, LANES), 1)
    start, number = owner_span(owner_counts, lax.axis_index("tp"))
    hit = (slot + start == lane) & (slot < number)
    own_scale = jnp.sum(jnp.where(hit, scale, 0.0), axis=1, keepdims=True)

    spread = jnp.broadcast_to(scale[:1], (seg_total, LANES))
    r_row = lax.broadcasted_iota(i32, (seg_total, LANES), 0)
    r_lane = lax.broadcasted_iota(i32, (seg_total, LANES), 1)
    row_scale = jnp.sum(jnp.where(r_row == r_lane, spread, 0.0), axis=1, keepdims=True)
    value = emb[...] * row_scale
    high = value.astype(bf16)
    rest = value - high.astype(f32)
    middle = rest.astype(bf16)
    low = (rest - middle.astype(f32)).astype(bf16)
    stacked = jnp.concatenate([high, middle, low], 0)
    member = lax.broadcasted_iota(i32, (GROUP, 3 * seg_total), 0)
    once = lax.broadcasted_iota(i32, (GROUP, 3 * seg_total), 1) < seg_total
    for r in range(seg_total):
        match = assign_row[...] == member + place[1, r]
        match = jnp.where(match, 1.0, 0.0)
        number_r = jnp.sum(jnp.where(once, match, 0.0), axis=1, keepdims=True)
        added = jnp.dot(match.astype(bf16), stacked, preferred_element_type=f32)
        at = slice(r * GROUP, (r + 1) * GROUP)
        moved[at, :] = (picked[at, :].astype(f32) + added) / (1.0 + number_r)

    def write(r):
        first = pl.multiple_of(place[0, r], GROUP)
        return pltpu.make_async_copy(
            moved.at[pl.ds(r * GROUP, GROUP), :], wide.at[pl.ds(first, GROUP), :], sems.at[r]
        )

    for r in range(seg_total):
        pl.when(place[2, r] == 1)(lambda r=r: write(r).start())

    valid = lax.broadcasted_iota(i32, (slots, block), 0) < number
    for g in range(rows // block):
        at = slice(g * block, (g + 1) * block)
        y = terms[0][:, at]
        for t in terms[1:]:
            y = y + t[:, at]
        y = norms[g : g + 1, :] * (1.0 / model_width**0.5) + y * own_scale
        dist[:, at] = jnp.where(valid, y, 0.0)

    for r in range(seg_total):
        pl.when(place[2, r] == 1)(lambda r=r: write(r).wait())


def finish(owner_counts, place, terms, norms, emb, assign_row, picked, wide, model_width):
    groups = len(terms)
    seg_total = emb.shape[0]
    slots, rows = terms[0].shape
    rows = rows - LANES
    whole = pl.BlockSpec(memory_space=pltpu.VMEM)
    anywhere = pl.BlockSpec(memory_space=pl.ANY)
    scalar = pl.BlockSpec(memory_space=pltpu.SMEM)

    def body(*refs):
        finish_body(groups, model_width, *refs)

    return pl.pallas_call(
        body,
        in_specs=[scalar, scalar] + [whole] * (groups + 4) + [anywhere],
        out_specs=[whole, anywhere],
        out_shape=[
            jax.ShapeDtypeStruct((slots, rows), f32),
            jax.ShapeDtypeStruct(wide.shape, f32),
        ],
        scratch_shapes=[
            pltpu.VMEM((seg_total * GROUP, emb.shape[1]), f32),
            pltpu.SemaphoreType.DMA((seg_total,)),
        ],
        input_output_aliases={2 + groups + 4: 1},
        compiler_params=pltpu.CompilerParams(vmem_limit_bytes=VMEM_LIMIT),
        name="finish",
    )(owner_counts, place, *terms, norms, emb, assign_row, picked, wide)


def shards(
    tokens, w_query, w_key, w_value, w_out, seg_ids, owner_counts, centroids, pool_gain, assign
):
    tok_rows, model_width = tokens.shape
    seq_len = seg_ids.shape[0]
    seg_total = assign.shape[0]
    rank_seq = lax.axis_index("seq")
    rank_tp = lax.axis_index("tp")
    seq_total = lax.axis_size("seq")
    tp_total = lax.axis_size("tp")
    groups = tp_total // 2
    feat = model_width // tp_total
    cent_rows = centroids.shape[0]
    slots = 2 * seg_total // owner_counts.shape[0]
    fine_np, coarse_np = angle_tables(seq_len)
    fine = jnp.asarray(fine_np)
    coarse = jnp.asarray(coarse_np)

    key_half, value_half = project_kv(tokens, w_key, w_value, fine, coarse)
    masks = range(1, seq_total)
    keys = [key_half] + [swapped(key_half, "seq", m) for m in masks]
    keys = keys + [swapped(k, "tp", 1) for k in keys]
    values = [value_half] + [swapped(value_half, "seq", m) for m in masks]
    values = values + [swapped(v, "tp", 1) for v in values]

    queries = project_q(tokens, w_query, fine, coarse)

    local = assign - rank_seq * cent_rows
    mine = (local >= 0) & (local < cent_rows)
    first_row = jnp.where(mine, local // GROUP * GROUP, 0)
    line = assign // GROUP
    order = jnp.arange(seg_total, dtype=i32)
    repeat = jnp.any((line[:, None] == line[None, :]) & (order[None, :] < order[:, None]), axis=1)
    place = jnp.stack([first_row, line * GROUP, (mine & ~repeat).astype(i32)])
    wide, norms, picked = widen_centroids(first_row, centroids)

    member = (
        lax.dynamic_slice_in_dim(seg_ids, rank_seq * tok_rows, tok_rows, 0)[:, None]
        == jnp.arange(seg_total, dtype=i32)[None, :]
    ).astype(bf16)
    token_cols = lax.dynamic_slice_in_dim(tokens, rank_tp * feat, feat, 1)
    pooled_tokens = lax.dot_general(
        member, token_cols, (((0,), (0,)), ((), ())), preferred_element_type=f32
    )
    pooled_tokens = [pooled_tokens] + [swapped(pooled_tokens, "seq", m) for m in masks]

    attended, counts = attend(seg_ids, queries, keys, values, seg_total)
    attended = [attended] + [swapped(attended, "seq", m) for m in masks]

    keep, send = mix(attended, norms, w_out, feat, groups)
    both = keep + swapped(send, "tp", 1)
    mixed = [both[0]] + [swapped(both[m], "tp", 2 * m) for m in range(1, groups)]

    keep, send, emb, norms = cross(
        owner_counts,
        mixed,
        pooled_tokens,
        counts,
        pool_gain.reshape(1, feat),
        centroids,
        slots,
        model_width,
    )
    both = keep + swapped(send, "tp", 1)
    terms = [both[0]] + [swapped(both[m], "tp", 2 * m) for m in range(1, groups)]
    assign_row = jnp.tile(assign, 3).reshape(1, 3 * seg_total)
    distances, updated = finish(
        owner_counts, place, terms, norms, emb, assign_row, picked, wide, model_width
    )
    return (distances, updated)


def solution(mesh):
    in_specs = (
        P("seq", None),
        P(None, "tp"),
        P(None, "tp"),
        P(None, "tp"),
        P("tp", None),
        P(),
        P(),
        P("seq", "tp"),
        P("tp"),
        P(),
    )
    out_specs = (P("tp", "seq"), P("seq", "tp"))
    return jax.shard_map(shards, mesh=mesh, in_specs=in_specs, out_specs=out_specs, check_vma=False)
```

```python
import math

import jax
import jax.numpy as jnp
import numpy as np
from jax import lax
from jax.experimental import pallas as pl
from jax.experimental.pallas import tpu as pltpu
from jax.sharding import PartitionSpec as P

HD = 128
WINDOW = 4096
QB = 256
KB = 512
LANES = 128
GROUP = 16
PROJECT_STEPS = 4

rope_theta = 10000.0
norm_eps = 1e-06
VMEM_LIMIT = 56 * 1024 * 1024

f32 = jnp.float32
bf16 = jnp.bfloat16
i32 = jnp.int32


def swapped(x, axis, mask):
    count = lax.axis_size(axis)
    return lax.ppermute(x, axis, [(i, i ^ mask) for i in range(count)])


def angle_tables(seq_len):
    inverse = np.exp(-(2.0 * np.arange(HD // 2) / HD) * math.log(rope_theta))
    inverse = np.repeat(inverse, 2)[None, :]
    fine = np.arange(LANES)[:, None] * inverse
    coarse = LANES * np.arange(seq_len // LANES)[:, None] * inverse
    fine_tab = np.stack([np.cos(fine), np.sin(fine)]).astype(np.float32)
    coarse_tab = np.stack([np.cos(coarse), np.sin(coarse)]).astype(np.float32)
    return fine_tab, coarse_tab


def turn(fine, coarse, which):
    ca = coarse[0, pl.ds(which, 1), :]
    sa = coarse[1, pl.ds(which, 1), :]
    cb = fine[0]
    sb = fine[1]
    return ca * cb - sa * sb, sa * cb + ca * sb


def pair_swap(x, even):
    up = pltpu.roll(x, x.shape[1] - 1, 1)
    down = pltpu.roll(x, 1, 1)
    return jnp.where(even, up, down)


def kv_body(tok, wk, wv, fine, coarse, out, acc):
    step = pl.program_id(0)
    half = wk.shape[0]
    subs = out.shape[0] // LANES
    weight = jnp.concatenate([wk[...], wv[...]], 0)
    part = lax.dot_general(
        tok[...], weight, (((1,), (1,)), ((), ())), preferred_element_type=f32
    )

    @pl.when(step == 0)
    def _():
        acc[...] = part

    @pl.when(step > 0)
    def _():
        acc[...] = acc[...] + part

    @pl.when(step == pl.num_programs(0) - 1)
    def _():
        lane = lax.broadcasted_iota(i32, (LANES, LANES), 1)
        even = lane % 2 == 0
        upper = lax.axis_index("tp") % 2 == 1
        first = lax.axis_index("seq") * subs
        for sub in range(subs):
            at = slice(sub * LANES, (sub + 1) * LANES)
            cos, sin = turn(fine, coarse, first + sub)
            cos = jnp.where(upper, pltpu.roll(cos, half, 1), cos)
            sin = jnp.where(upper, pltpu.roll(sin, half, 1), sin)
            cos = jnp.where(lane < half, cos, 1.0)
            sin = jnp.where(lane < half, jnp.where(even, -sin, sin), 0.0)
            x = acc[at]
            out[at, :] = (x * cos + pair_swap(x, even) * sin).astype(bf16)


def project_kv(tokens, w_key, w_value, fine, coarse):
    rows, width = tokens.shape
    half = w_key.shape[1]
    block = width // PROJECT_STEPS
    whole = lambda a: pl.BlockSpec(a.shape, lambda i: (0,) * a.ndim)
    return pl.pallas_call(
        kv_body,
        grid=(PROJECT_STEPS,),
        in_specs=[
            pl.BlockSpec((rows, block), lambda i: (0, i)),
            pl.BlockSpec((half, block), lambda i: (0, i)),
            pl.BlockSpec((half, block), lambda i: (0, i)),
            whole(fine),
            whole(coarse),
        ],
        out_specs=pl.BlockSpec((rows, 2 * half), lambda i: (0, 0)),
        out_shape=jax.ShapeDtypeStruct((rows, 2 * half), bf16),
        scratch_shapes=[pltpu.VMEM((rows, 2 * half), f32)],
        compiler_params=pltpu.CompilerParams(vmem_limit_bytes=VMEM_LIMIT),
        name="project_kv",
    )(tokens, w_key.T, w_value.T, fine, coarse)


def q_body(tok, wq, fine, coarse, *refs):
    outs = refs[:-1]
    acc = refs[-1]
    step = pl.program_id(0)
    subs = acc.shape[0] // LANES
    per_out = subs // len(outs)
    heads = wq.shape[1] // HD
    part = jnp.dot(tok[...], wq[...], preferred_element_type=f32)

    @pl.when(step == 0)
    def _():
        acc[...] = part

    @pl.when(step > 0)
    def _():
        acc[...] = acc[...] + part

    @pl.when(step == pl.num_programs(0) - 1)
    def _():
        lane = lax.broadcasted_iota(i32, (LANES, LANES), 1)
        even = lane % 2 == 0
        upper = lax.axis_index("tp") % 2 == 1
        first = lax.axis_index("seq") * subs
        scale = HD ** (-0.5) * math.log2(math.e)
        for sub in range(subs):
            cos, sin = turn(fine, coarse, first + sub)
            cos = cos * scale
            sin = jnp.where(even, -sin, sin) * scale
            out = outs[sub // per_out]
            row = (sub % per_out) * LANES
            for h in range(heads):
                x = acc[sub * LANES : (sub + 1) * LANES, h * HD : (h + 1) * HD]
                x = x * cos + pair_swap(x, even) * sin
                x = jnp.where(upper, pltpu.roll(x, HD // 2, 1), x)
                out[row : row + LANES, h * HD : (h + 1) * HD] = x.astype(bf16)


def project_q(tokens, w_query, fine, coarse):
    rows, width = tokens.shape
    cols = w_query.shape[1]
    block = width // PROJECT_STEPS
    whole = lambda a: pl.BlockSpec(a.shape, lambda i: (0,) * a.ndim)
    out = jax.ShapeDtypeStruct((rows // 2, cols), bf16)
    return pl.pallas_call(
        q_body,
        grid=(PROJECT_STEPS,),
        in_specs=[
            pl.BlockSpec((rows, block), lambda i: (0, i)),
            pl.BlockSpec((block, cols), lambda i: (i, 0)),
            whole(fine),
            whole(coarse),
        ],
        out_specs=[pl.BlockSpec((rows // 2, cols), lambda i: (0, 0))] * 2,
        out_shape=[out, out],
        scratch_shapes=[pltpu.VMEM((rows, cols), f32)],
        compiler_params=pltpu.CompilerParams(vmem_limit_bytes=VMEM_LIMIT),
        name="project_q",
    )(tokens, w_query, fine, coarse)


def cent_body(base, cent, cent_any, wide, norms, picked, sems):
    step = pl.program_id(0)
    count = base.shape[0]

    def fetch(r):
        start = pl.multiple_of(base[r], GROUP)
        return pltpu.make_async_copy(
            cent_any.at[pl.ds(start, GROUP), :], picked.at[pl.ds(r * GROUP, GROUP), :], sems.at[r]
        )

    @pl.when(step == 0)
    def _():
        for r in range(count):
            fetch(r).start()

    c = cent[...].astype(f32)
    wide[...] = c
    square = c * c
    part = square[:, :LANES]
    for g in range(1, c.shape[1] // LANES):
        part = part + square[:, g * LANES : (g + 1) * LANES]
    norms[pl.ds(step, 1), :] = jnp.sum(part.T, axis=0, keepdims=True)

    @pl.when(step == pl.num_programs(0) - 1)
    def _():
        for r in range(count):
            fetch(r).wait()


def widen_centroids(base, centroids):
    rows, feat = centroids.shape
    count = base.shape[0]
    block = rows // 8
    spec = pltpu.PrefetchScalarGridSpec(
        num_scalar_prefetch=1,
        grid=(8,),
        in_specs=[
            pl.BlockSpec((block, feat), lambda i, b: (i, 0)),
            pl.BlockSpec(memory_space=pl.ANY),
        ],
        out_specs=[
            pl.BlockSpec((block, feat), lambda i, b: (i, 0)),
            pl.BlockSpec((8, block), lambda i, b: (0, 0)),
            pl.BlockSpec((count * GROUP, feat), lambda i, b: (0, 0)),
        ],
        scratch_shapes=[pltpu.SemaphoreType.DMA((count,))],
    )
    return pl.pallas_call(
        cent_body,
        grid_spec=spec,
        out_shape=[
            jax.ShapeDtypeStruct((rows, feat), f32),
            jax.ShapeDtypeStruct((8, block), f32),
            jax.ShapeDtypeStruct((count * GROUP, feat), bf16),
        ],
        compiler_params=pltpu.CompilerParams(vmem_limit_bytes=VMEM_LIMIT),
        name="widen_centroids",
    )(base, centroids, centroids)


def segment_starts(ids):
    rows = ids.shape[0]
    row = lax.broadcasted_iota(i32, ids.shape, 0)
    lane = lax.broadcasted_iota(i32, ids.shape, 1)
    left = pltpu.roll(ids, 1, 1)
    left = jnp.where(lane == 0, pltpu.roll(left, 1, 0), left)
    token = row * LANES + lane
    first = jnp.where((ids != left) & (token > 0), token, 0)
    shift = 1
    while shift < LANES:
        first = jnp.maximum(first, jnp.where(lane >= shift, pltpu.roll(first, shift, 1), 0))
        shift = shift * 2
    above = jnp.broadcast_to(jnp.max(first, axis=1, keepdims=True), ids.shape)
    above = jnp.where(row >= 1, pltpu.roll(above, 1, 0), 0)
    shift = 1
    while shift < rows:
        above = jnp.maximum(above, jnp.where(row >= shift, pltpu.roll(above, shift, 0), 0))
        shift = shift * 2
    return jnp.maximum(first, above)


def attend_body(pieces, seg_total, balanced, seg, ids, *refs):
    queries = refs[: 3 if balanced else 2]
    refs = refs[len(queries) :]
    own_in = refs[:pieces]
    other_in = refs[pieces : 2 * pieces]
    out, counts, q_all, own, other, kn, vn, starts, weights, tops, col, lhs, sems = refs[
        2 * pieces :
    ]
    q_rows, q_cols = queries[0].shape
    rows = own_in[0].shape[0]
    heads = q_cols // HD
    half = HD // 2
    seq_len = own.shape[0]
    wide = heads * QB
    own_blocks = rows // QB
    rank = lax.axis_index("seq")
    upper = lax.axis_index("tp") % 2 == 1

    copies = []
    for k, source in enumerate(queries):
        target = q_all.at[pl.ds(k * q_rows, q_rows), :]
        copies.append(pltpu.make_async_copy(source, target, sems.at[len(copies)]))
    for sources, target in ((own_in, own), (other_in, other)):
        for m in range(pieces):
            row0 = pl.multiple_of((rank ^ m) * rows, rows)
            place = target.at[pl.ds(row0, rows), :]
            copies.append(pltpu.make_async_copy(sources[m], place, sems.at[len(copies)]))
    for c in copies:
        c.start()
    col[...] = jnp.zeros(col.shape, f32)
    starts[...] = segment_starts(ids[...])
    for c in copies:
        c.wait()

    def join(t, carry):
        at = pl.ds(pl.multiple_of(t * KB, KB), KB)
        a = own[at, :]
        b = other[at, :]
        kn[at, :] = jnp.concatenate([a[:, :half], b[:, :half]], 1)
        vn[at, :] = jnp.concatenate([a[:, half:], b[:, half:]], 1)
        return carry

    lax.fori_loop(0, seq_len // KB, join, 0)

    def q_step(n, carry):
        home = n < own_blocks
        base = jnp.where(home, rank, rank ^ 3) * rows + jnp.where(home, n, n - own_blocks) * QB
        base = pl.multiple_of(base, QB)
        last_seg = seg[base + QB - 1]
        first_seg = seg[base]
        end = (base + QB - 1) // KB + 1
        clear_end = base // KB
        begin = jnp.int32(0)
        clear = jnp.int32(0)
        for t in range(seq_len // KB):
            begin = begin + (seg[t * KB + KB - 1] < first_seg).astype(i32)
            outside = (seg[t * KB] != last_seg) | (base + QB - 1 - t * KB >= WINDOW)
            clear = clear + (outside & (t < clear_end)).astype(i32)
        begin = jnp.maximum(begin, jnp.maximum(base - (WINDOW - 1), 0) // KB)
        begin = jnp.minimum(begin, clear_end)
        clear = jnp.clip(clear, begin, clear_end)

        q_at = pl.ds(pl.multiple_of(n * QB, QB), QB)
        q = jnp.concatenate([q_all[q_at, h * HD : (h + 1) * HD] for h in range(heads)], 0)
        low = [starts[pl.ds(base // LANES + g, 1), :] for g in range(QB // LANES)]
        low = jnp.concatenate(low * heads, 1)
        i_pos = base + lax.broadcasted_iota(i32, (1, wide), 1) % QB
        if seq_len > WINDOW:
            low = jnp.maximum(low, i_pos - (WINDOW - 1))

        def score(masked, kb, carry):
            top, total = carry
            start = pl.multiple_of(kb * KB, KB)
            s = lax.dot_general(
                kn[pl.ds(start, KB), :],
                q,
                (((1,), (1,)), ((), ())),
                preferred_element_type=f32,
            )
            if masked:
                j_pos = start + lax.broadcasted_iota(i32, (KB, wide), 0)
                s = jnp.where((j_pos <= i_pos) & (j_pos >= low), s, -1e30)
            new_top = jnp.maximum(top, jnp.max(s, axis=0, keepdims=True))
            p = jnp.exp2(s - new_top)
            weights[pl.ds(start, KB), :] = p.astype(bf16)
            tops[pl.ds(kb, 1), :] = new_top
            p = jnp.sum(p.reshape(KB // 8, 8, wide), axis=0)
            return new_top, total * jnp.exp2(top - new_top) + p

        state = (jnp.full((1, wide), -1e30, f32), jnp.zeros((8, wide), f32))
        state = lax.fori_loop(begin, clear, lambda kb, c: score(True, kb, c), state)
        state = lax.fori_loop(clear, clear_end, lambda kb, c: score(False, kb, c), state)
        top, total = lax.fori_loop(clear_end, end, lambda kb, c: score(True, kb, c), state)
        share = 1.0 / jnp.sum(total, axis=0, keepdims=True)
        row = lax.broadcasted_iota(i32, (16, wide), 0)
        head = lax.broadcasted_iota(i32, (16, wide), 1) // QB

        def gather(kb, carry):
            start = pl.multiple_of(kb * KB, KB)
            r = share * jnp.exp2(tops[pl.ds(kb, 1), :] - top)
            high = r.astype(bf16).astype(f32)
            r = jnp.where(row == head, high, jnp.where(row == heads + head, r - high, 0.0))
            add = lax.dot_general(
                weights[pl.ds(start, KB), :],
                r.astype(bf16),
                (((1,), (1,)), ((), ())),
                preferred_element_type=f32,
            )
            at = pl.ds(start, KB)
            col[at, :16] = col[at, :16] + add
            return carry

        lax.fori_loop(begin, end, gather, 0)
        return carry

    if balanced:
        low_n = jnp.where(rank == 3, 2, jnp.where(rank == 2, 1, 0))
        high_n = own_blocks + jnp.where(rank == 0, 2, jnp.where(rank == 1, 1, 0))
    else:
        low_n = 0
        high_n = own_blocks
    lax.fori_loop(low_n, high_n, q_step, 0)

    number = jnp.zeros((seg_total, LANES), f32)
    for g in range(seq_len // LANES):
        at = slice(g * LANES, (g + 1) * LANES)
        member = ids[g : g + 1, :] == lax.broadcasted_iota(i32, (seg_total, LANES), 0)
        number = number + member.astype(f32)
        turned = col[at, :].T
        for h in range(heads):
            w = turned[h : h + 1] + turned[heads + h : heads + h + 1]
            w = jnp.where(member, w, 0.0)
            high = w.astype(bf16)
            lhs[h * seg_total : (h + 1) * seg_total, at] = high
            rest = (w - high.astype(f32)).astype(bf16)
            lhs[(heads + h) * seg_total : (heads + h + 1) * seg_total, at] = rest
    counts[...] = jnp.broadcast_to(jnp.sum(number, axis=1, keepdims=True), counts.shape)
    pooled = jnp.dot(lhs[...], vn[...], preferred_element_type=f32)
    for h in range(heads):
        x = pooled[h * seg_total : (h + 1) * seg_total]
        x = x + pooled[(heads + h) * seg_total : (heads + h + 1) * seg_total]
        out[:, h * HD : (h + 1) * HD] = jnp.where(upper, pltpu.roll(x, half, 1), x)


def attend(seg_ids, queries, own, other, seg_total, balanced):
    q_rows, cols = queries[0].shape
    rows = own[0].shape[0]
    seq_len = seg_ids.shape[0]
    pieces = len(own)
    heads = cols // HD
    whole = pl.BlockSpec(memory_space=pltpu.VMEM)
    anywhere = pl.BlockSpec(memory_space=pl.ANY)
    inputs = len(queries) + 2 * pieces

    def body(*refs):
        attend_body(pieces, seg_total, balanced, *refs)

    return pl.pallas_call(
        body,
        in_specs=[pl.BlockSpec(memory_space=pltpu.SMEM), whole] + [anywhere] * inputs,
        out_specs=[whole, whole],
        out_shape=[
            jax.ShapeDtypeStruct((seg_total, cols), f32),
            jax.ShapeDtypeStruct((seg_total, LANES), f32),
        ],
        scratch_shapes=[
            pltpu.VMEM((len(queries) * q_rows, cols), bf16),
            pltpu.VMEM((seq_len, HD), bf16),
            pltpu.VMEM((seq_len, HD), bf16),
            pltpu.VMEM((seq_len, HD), bf16),
            pltpu.VMEM((seq_len, HD), bf16),
            pltpu.VMEM((seq_len // LANES, LANES), i32),
            pltpu.VMEM((seq_len, heads * QB), bf16),
            pltpu.VMEM((max(8, seq_len // KB), heads * QB), f32),
            pltpu.VMEM((seq_len, LANES), f32),
            pltpu.VMEM((2 * heads * seg_total, seq_len), bf16),
            pltpu.SemaphoreType.DMA((inputs,)),
        ],
        compiler_params=pltpu.CompilerParams(vmem_limit_bytes=VMEM_LIMIT),
        name="attend",
    )(seg_ids, seg_ids.reshape(seq_len // LANES, LANES), *queries, *own, *other)


def mix_body(pieces, *refs):
    parts = refs[:pieces]
    norms, w_out, keep, send = refs[pieces:]
    groups, _, feat = keep.shape
    seg_total = parts[0].shape[0]
    mixed = parts[0][...]
    for p in parts[1:]:
        mixed = mixed + p[...]
    high = mixed.astype(bf16)
    low = (mixed - high.astype(f32)).astype(bf16)
    lhs = jnp.concatenate([high, low], 0)
    rank = lax.axis_index("tp")
    for k, target in enumerate((keep, send)):
        for m in range(groups):
            owner = rank ^ (2 * m + k)
            cols = pl.ds(pl.multiple_of(owner * feat, feat), feat)
            y = jnp.dot(lhs, w_out[:, cols], preferred_element_type=f32)
            target[m, :seg_total, :] = y[:seg_total] + y[seg_total:]
            target[m, seg_total:, :] = norms[...]


def mix(parts, norms, w_out, feat, groups):
    seg_total = parts[0].shape[0]
    whole = pl.BlockSpec(memory_space=pltpu.VMEM)
    out = jax.ShapeDtypeStruct((groups, seg_total + 8, feat), f32)

    def body(*refs):
        mix_body(len(parts), *refs)

    return pl.pallas_call(
        body,
        in_specs=[whole] * (len(parts) + 2),
        out_specs=[whole, whole],
        out_shape=[out, out],
        compiler_params=pltpu.CompilerParams(vmem_limit_bytes=VMEM_LIMIT),
        name="mix",
    )(*parts, norms, w_out)


def owner_span(owner_counts, owner):
    start = jnp.int32(0)
    for o in range(owner_counts.shape[0]):
        start = start + jnp.where(o < owner, owner_counts[o], 0)
    return start, owner_counts[owner]


def cross_body(groups, pieces, model_width, owner_counts, *refs):
    mixed = refs[:groups]
    pooled_in = refs[groups : groups + pieces]
    counts, gain, cent = refs[groups + pieces : groups + pieces + 3]
    keep, send, emb, norms, lhs = refs[groups + pieces + 3 :]
    step = pl.program_id(0)
    seg_total, feat = emb.shape
    block = cent.shape[0]
    slots = keep.shape[1]
    per_side = groups * slots
    rank = lax.axis_index("tp")

    @pl.when(step == 0)
    def _():
        total = mixed[0][...]
        for p in mixed[1:]:
            total = total + p[...]
        norms[...] = total[seg_total:]
        sums = total[:seg_total]
        for p in pooled_in:
            sums = sums + p[...]
        pooled = sums / counts[:, :1]
        square = jnp.sum(pooled * pooled, axis=1, keepdims=True)
        row = lax.broadcasted_iota(i32, (seg_total, LANES), 0)
        lane = lax.broadcasted_iota(i32, (seg_total, LANES), 1)
        square = jnp.sum(jnp.where(row == lane, square, 0.0), axis=0, keepdims=True)
        square = jnp.broadcast_to(square, (slots, LANES))
        scaled = pooled * gain[...]
        emb[...] = scaled
        high = scaled.astype(bf16)
        low = (scaled - high.astype(f32)).astype(bf16)
        slot = lax.broadcasted_iota(i32, (slots, seg_total), 0)
        column = lax.broadcasted_iota(i32, (slots, seg_total), 1)
        chosen = []
        for k, target in enumerate((keep, send)):
            for m in range(groups):
                start, number = owner_span(owner_counts, rank ^ (2 * m + k))
                hit = (slot + start == column) & (slot < number)
                chosen.append(jnp.where(hit, 1.0, 0.0))
                target[m, :, block * pl.num_programs(0) :] = square
        chosen = jnp.concatenate(chosen, 0).astype(bf16)
        factor = -2.0 / model_width**0.5
        lhs[: 2 * per_side] = (
            jnp.dot(chosen, high, preferred_element_type=f32) * factor
        ).astype(bf16)
        lhs[2 * per_side :] = (
            jnp.dot(chosen, low, preferred_element_type=f32) * factor
        ).astype(bf16)

    y = lax.dot_general(
        cent[...], lhs[...], (((1,), (1,)), ((), ())), preferred_element_type=f32
    ).T
    y = y[: 2 * per_side] + y[2 * per_side :]
    cols = pl.ds(pl.multiple_of(step * block, block), block)
    for k, target in enumerate((keep, send)):
        for m in range(groups):
            first = k * per_side + m * slots
            target[m, :, cols] = y[first : first + slots]


def cross(owner_counts, mixed, pooled_in, counts, gain, centroids, slots, model_width):
    rows, feat = centroids.shape
    groups = len(mixed)
    pieces = len(pooled_in)
    seg_total = counts.shape[0]
    block = rows // 8
    fixed = lambda shape: pl.BlockSpec(shape, lambda i, o: (0,) * len(shape))
    side = (groups, slots, rows + LANES)
    spec = pltpu.PrefetchScalarGridSpec(
        num_scalar_prefetch=1,
        grid=(8,),
        in_specs=[fixed(a.shape) for a in mixed]
        + [fixed(a.shape) for a in pooled_in]
        + [
            fixed(counts.shape),
            fixed(gain.shape),
            pl.BlockSpec((block, feat), lambda i, o: (i, 0)),
        ],
        out_specs=[fixed(side), fixed(side), fixed((seg_total, feat)), fixed((8, block))],
        scratch_shapes=[pltpu.VMEM((4 * groups * slots, feat), bf16)],
    )

    def body(*refs):
        cross_body(groups, pieces, model_width, *refs)

    return pl.pallas_call(
        body,
        grid_spec=spec,
        out_shape=[
            jax.ShapeDtypeStruct(side, f32),
            jax.ShapeDtypeStruct(side, f32),
            jax.ShapeDtypeStruct((seg_total, feat), f32),
            jax.ShapeDtypeStruct((8, block), f32),
        ],
        compiler_params=pltpu.CompilerParams(vmem_limit_bytes=VMEM_LIMIT),
        name="cross",
    )(owner_counts, *mixed, *pooled_in, counts, gain, centroids)


def finish_body(groups, model_width, owner_counts, place, *refs):
    terms = refs[:groups]
    norms, emb, assign_row, picked, wide_in, dist, wide, moved, sems = refs[groups:]
    seg_total, feat = emb.shape
    block = norms.shape[1]
    slots = dist.shape[0]
    rows = dist.shape[1]
    total = terms[0][:, rows:]
    for t in terms[1:]:
        total = total + t[:, rows:]
    scale = lax.rsqrt(total / model_width + norm_eps)
    slot = lax.broadcasted_iota(i32, (slots, LANES), 0)
    lane = lax.broadcasted_iota(i32, (slots, LANES), 1)
    start, number = owner_span(owner_counts, lax.axis_index("tp"))
    hit = (slot + start == lane) & (slot < number)
    own_scale = jnp.sum(jnp.where(hit, scale, 0.0), axis=1, keepdims=True)

    spread = jnp.broadcast_to(scale[:1], (seg_total, LANES))
    r_row = lax.broadcasted_iota(i32, (seg_total, LANES), 0)
    r_lane = lax.broadcasted_iota(i32, (seg_total, LANES), 1)
    row_scale = jnp.sum(jnp.where(r_row == r_lane, spread, 0.0), axis=1, keepdims=True)
    value = emb[...] * row_scale
    high = value.astype(bf16)
    rest = value - high.astype(f32)
    middle = rest.astype(bf16)
    low = (rest - middle.astype(f32)).astype(bf16)
    stacked = jnp.concatenate([high, middle, low], 0)
    member = lax.broadcasted_iota(i32, (GROUP, 3 * seg_total), 0)
    once = lax.broadcasted_iota(i32, (GROUP, 3 * seg_total), 1) < seg_total
    for r in range(seg_total):
        match = assign_row[...] == member + place[1, r]
        match = jnp.where(match, 1.0, 0.0)
        number_r = jnp.sum(jnp.where(once, match, 0.0), axis=1, keepdims=True)
        added = jnp.dot(match.astype(bf16), stacked, preferred_element_type=f32)
        at = slice(r * GROUP, (r + 1) * GROUP)
        moved[at, :] = (picked[at, :].astype(f32) + added) / (1.0 + number_r)

    def write(r):
        first = pl.multiple_of(place[0, r], GROUP)
        return pltpu.make_async_copy(
            moved.at[pl.ds(r * GROUP, GROUP), :], wide.at[pl.ds(first, GROUP), :], sems.at[r]
        )

    for r in range(seg_total):
        pl.when(place[2, r] == 1)(lambda r=r: write(r).start())

    valid = lax.broadcasted_iota(i32, (slots, block), 0) < number
    for g in range(rows // block):
        at = slice(g * block, (g + 1) * block)
        y = terms[0][:, at]
        for t in terms[1:]:
            y = y + t[:, at]
        y = norms[g : g + 1, :] * (1.0 / model_width**0.5) + y * own_scale
        dist[:, at] = jnp.where(valid, y, 0.0)

    for r in range(seg_total):
        pl.when(place[2, r] == 1)(lambda r=r: write(r).wait())


def finish(owner_counts, place, terms, norms, emb, assign_row, picked, wide, model_width):
    groups = len(terms)
    seg_total = emb.shape[0]
    slots, rows = terms[0].shape
    rows = rows - LANES
    whole = pl.BlockSpec(memory_space=pltpu.VMEM)
    anywhere = pl.BlockSpec(memory_space=pl.ANY)
    scalar = pl.BlockSpec(memory_space=pltpu.SMEM)

    def body(*refs):
        finish_body(groups, model_width, *refs)

    return pl.pallas_call(
        body,
        in_specs=[scalar, scalar] + [whole] * (groups + 4) + [anywhere],
        out_specs=[whole, anywhere],
        out_shape=[
            jax.ShapeDtypeStruct((slots, rows), f32),
            jax.ShapeDtypeStruct(wide.shape, f32),
        ],
        scratch_shapes=[
            pltpu.VMEM((seg_total * GROUP, emb.shape[1]), f32),
            pltpu.SemaphoreType.DMA((seg_total,)),
        ],
        input_output_aliases={2 + groups + 4: 1},
        compiler_params=pltpu.CompilerParams(vmem_limit_bytes=VMEM_LIMIT),
        name="finish",
    )(owner_counts, place, *terms, norms, emb, assign_row, picked, wide)


def shards(
    tokens, w_query, w_key, w_value, w_out, seg_ids, owner_counts, centroids, pool_gain, assign
):
    tok_rows, model_width = tokens.shape
    seq_len = seg_ids.shape[0]
    seg_total = assign.shape[0]
    rank_seq = lax.axis_index("seq")
    rank_tp = lax.axis_index("tp")
    seq_total = lax.axis_size("seq")
    tp_total = lax.axis_size("tp")
    groups = tp_total // 2
    feat = model_width // tp_total
    cent_rows = centroids.shape[0]
    slots = 2 * seg_total // owner_counts.shape[0]
    fine_np, coarse_np = angle_tables(seq_len)
    fine = jnp.asarray(fine_np)
    coarse = jnp.asarray(coarse_np)

    own = project_kv(tokens, w_key, w_value, fine, coarse)
    masks = range(1, seq_total)
    own = [own] + [swapped(own, "seq", m) for m in masks]
    other = [swapped(x, "tp", 1) for x in own]

    queries = list(project_q(tokens, w_query, fine, coarse))
    balanced = seq_total == 4 and seq_len <= WINDOW and tok_rows == 4 * QB
    if balanced:
        queries = queries + [lax.ppermute(queries[0], "seq", [(3, 0), (2, 1)])]

    local = assign - rank_seq * cent_rows
    mine = (local >= 0) & (local < cent_rows)
    first_row = jnp.where(mine, local // GROUP * GROUP, 0)
    line = assign // GROUP
    order = jnp.arange(seg_total, dtype=i32)
    repeat = jnp.any((line[:, None] == line[None, :]) & (order[None, :] < order[:, None]), axis=1)
    place = jnp.stack([first_row, line * GROUP, (mine & ~repeat).astype(i32)])
    wide, norms, picked = widen_centroids(first_row, centroids)

    member = (
        lax.dynamic_slice_in_dim(seg_ids, rank_seq * tok_rows, tok_rows, 0)[:, None]
        == jnp.arange(seg_total, dtype=i32)[None, :]
    ).astype(bf16)
    token_cols = lax.dynamic_slice_in_dim(tokens, rank_tp * feat, feat, 1)
    pooled_tokens = lax.dot_general(
        member, token_cols, (((0,), (0,)), ((), ())), preferred_element_type=f32
    )
    pooled_tokens = [pooled_tokens] + [swapped(pooled_tokens, "seq", m) for m in masks]

    queries, wide, norms, picked, pooled_first = lax.optimization_barrier(
        (queries, wide, norms, picked, pooled_tokens[0])
    )
    pooled_tokens[0] = pooled_first
    attended, counts = attend(seg_ids, queries, own, other, seg_total, balanced)
    attended = [attended] + [swapped(attended, "seq", m) for m in masks]

    keep, send = mix(attended, norms, w_out, feat, groups)
    both = keep + swapped(send, "tp", 1)
    mixed = [both[0]] + [swapped(both[m], "tp", 2 * m) for m in range(1, groups)]

    keep, send, emb, norms = cross(
        owner_counts,
        mixed,
        pooled_tokens,
        counts,
        pool_gain.reshape(1, feat),
        centroids,
        slots,
        model_width,
    )
    both = keep + swapped(send, "tp", 1)
    terms = [both[0]] + [swapped(both[m], "tp", 2 * m) for m in range(1, groups)]
    assign_row = jnp.tile(assign, 3).reshape(1, 3 * seg_total)
    distances, updated = finish(
        owner_counts, place, terms, norms, emb, assign_row, picked, wide, model_width
    )
    return (distances, updated)


def solution(mesh):
    in_specs = (
        P("seq", None),
        P(None, "tp"),
        P(None, "tp"),
        P(None, "tp"),
        P("tp", None),
        P(),
        P(),
        P("seq", "tp"),
        P("tp"),
        P(),
    )
    out_specs = (P("tp", "seq"), P("seq", "tp"))
    return jax.shard_map(shards, mesh=mesh, in_specs=in_specs, out_specs=out_specs, check_vma=False)
```

```python
import math

import jax
import jax.numpy as jnp
import numpy as np
from jax import lax
from jax.experimental import pallas as pl
from jax.experimental.pallas import tpu as pltpu
from jax.sharding import PartitionSpec as P

HD = 128
WINDOW = 4096
QB = 256
KB = 512
LANES = 128
GROUP = 16
TOKEN_CHUNKS = 8
AHEAD = 3
COLUMNS_AS_ROWS = True

rope_theta = 10000.0
norm_eps = 1e-06
MIB = 1024 * 1024

f32 = jnp.float32
bf16 = jnp.bfloat16
i32 = jnp.int32


def swapped(x, axis, mask):
    count = lax.axis_size(axis)
    return lax.ppermute(x, axis, [(i, i ^ mask) for i in range(count)])


def angle_tables(seq_len):
    inverse = np.exp(-(2.0 * np.arange(HD // 2) / HD) * math.log(rope_theta))
    inverse = np.repeat(inverse, 2)[None, :]
    fine = np.arange(LANES)[:, None] * inverse
    coarse = LANES * np.arange(seq_len // LANES)[:, None] * inverse
    fine_tab = np.stack([np.cos(fine), np.sin(fine)]).astype(np.float32)
    coarse_tab = np.stack([np.cos(coarse), np.sin(coarse)]).astype(np.float32)
    return fine_tab, coarse_tab


def turn(fine, coarse, which):
    ca = coarse[0, pl.ds(which, 1), :]
    sa = coarse[1, pl.ds(which, 1), :]
    cb = fine[0]
    sb = fine[1]
    return ca * cb - sa * sb, sa * cb + ca * sb


def pair_swap(x, even):
    up = pltpu.roll(x, x.shape[1] - 1, 1)
    down = pltpu.roll(x, 1, 1)
    return jnp.where(even, up, down)


def far(x):
    return pltpu.with_memory_space_constraint(x, pltpu.HBM)


def near(x):
    return pltpu.with_memory_space_constraint(x, pltpu.VMEM)


def stream(source, buffer, sems, chunks, axis):
    size = source.shape[axis] // chunks
    result = []
    for i in range(chunks):
        part = pl.ds(i * size, size)
        at = (part, slice(None)) if axis == 0 else (slice(None), part)
        result.append(pltpu.make_async_copy(source.at[at], buffer.at[at], sems.at[i]))
    return result


def kv_body(chunks, seg_total, *refs):
    ids_in, wk_in, wv_in, fine_in, coarse_in, tok_in = refs[:6]
    out, pooled, tables, tok, key_tables, weight, ids, fine, coarse, acc, small, sems = refs[6:]
    rows, width = tok.shape
    half = wk_in.shape[0]
    subs = rows // LANES
    size = width // chunks
    rest = [
        pltpu.make_async_copy(wk_in, weight.at[pl.ds(0, half), :], small.at[0]),
        pltpu.make_async_copy(wv_in, weight.at[pl.ds(half, half), :], small.at[1]),
        pltpu.make_async_copy(fine_in, fine, small.at[2]),
        pltpu.make_async_copy(coarse_in, coarse, small.at[3]),
        pltpu.make_async_copy(ids_in, ids, small.at[4]),
    ]
    for c in rest:
        c.start()
    copies = stream(tok_in, tok, sems, chunks, 1)
    for c in copies[:AHEAD]:
        c.start()
    for c in rest:
        c.wait()
    lane = lax.broadcasted_iota(i32, (LANES, LANES), 1)
    even = lane % 2 == 0
    upper = lax.axis_index("tp") % 2 == 1
    first = lax.axis_index("seq") * subs
    members = []
    for sub in range(subs):
        at = slice(sub * LANES, (sub + 1) * LANES)
        cos, sin = turn(fine, coarse, first + sub)
        sin = jnp.where(even, -sin, sin)
        tables[0, at, :] = cos
        tables[1, at, :] = sin
        cos = jnp.where(upper, pltpu.roll(cos, half, 1), cos)
        sin = jnp.where(upper, pltpu.roll(sin, half, 1), sin)
        key_tables[0, at, :] = jnp.where(lane < half, cos, 1.0)
        key_tables[1, at, :] = jnp.where(lane < half, sin, 0.0)
        member = ids[pl.ds(first + sub, 1), :] == lax.broadcasted_iota(i32, (seg_total, LANES), 0)
        members.append(jnp.where(member, 1.0, 0.0))
    for i in range(chunks):
        at = slice(i * size, (i + 1) * size)
        copies[i].wait()
        if i + AHEAD < chunks:
            copies[i + AHEAD].start()
        part = lax.dot_general(
            tok[:, at], weight[:, at], (((1,), (1,)), ((), ())), preferred_element_type=f32
        )
        acc[...] = part if i == 0 else acc[...] + part
    for sub in range(subs):
        at = slice(sub * LANES, (sub + 1) * LANES)
        x = acc[at]
        x = x * key_tables[0, at, :] + pair_swap(x, even) * key_tables[1, at, :]
        out[at, :] = x.astype(bf16)
    feat = pooled.shape[1]
    cols = pl.ds(pl.multiple_of(lax.axis_index("tp") * feat, feat), feat)
    member = jnp.concatenate(members, 1).astype(bf16)
    pooled[...] = jnp.dot(member, tok[:, cols], preferred_element_type=f32)


def project_kv(tokens, w_key, w_value, fine, coarse, ids, seg_total, feat):
    rows, width = tokens.shape
    half = w_key.shape[1]
    whole = pl.BlockSpec(memory_space=pltpu.VMEM)

    def body(*refs):
        kv_body(TOKEN_CHUNKS, seg_total, *refs)

    return pl.pallas_call(
        body,
        in_specs=[pl.BlockSpec(memory_space=pltpu.HBM)] * 6,
        out_specs=[whole] * 3,
        out_shape=[
            jax.ShapeDtypeStruct((rows, 2 * half), bf16),
            jax.ShapeDtypeStruct((seg_total, feat), f32),
            jax.ShapeDtypeStruct((2, rows, LANES), f32),
        ],
        scratch_shapes=[
            pltpu.VMEM((rows, width), bf16),
            pltpu.VMEM((2, rows, LANES), f32),
            pltpu.VMEM((2 * half, width), bf16),
            pltpu.VMEM(ids.shape, i32),
            pltpu.VMEM(fine.shape, f32),
            pltpu.VMEM(coarse.shape, f32),
            pltpu.VMEM((rows, 2 * half), f32),
            pltpu.SemaphoreType.DMA((5,)),
            pltpu.SemaphoreType.DMA((TOKEN_CHUNKS,)),
        ],
        compiler_params=pltpu.CompilerParams(vmem_limit_bytes=20 * MIB),
        name="project_kv",
    )(*[far(x) for x in (ids, w_key.T, w_value.T, fine, coarse, tokens)])


def q_body(tok, weight, tables, *refs):
    outs = refs[:2]
    acc = refs[2]
    rows = tok.shape[0]
    subs = rows // LANES
    per_out = subs // len(outs)
    heads = weight.shape[1] // HD
    acc[...] = jnp.dot(tok[...], weight[...], preferred_element_type=f32)
    even = lax.broadcasted_iota(i32, (LANES, LANES), 1) % 2 == 0
    upper = lax.axis_index("tp") % 2 == 1
    scale = HD ** (-0.5) * math.log2(math.e)
    for sub in range(subs):
        at = slice(sub * LANES, (sub + 1) * LANES)
        cos = tables[0, at, :] * scale
        sin = tables[1, at, :] * scale
        out = outs[sub // per_out]
        row = (sub % per_out) * LANES
        for h in range(heads):
            x = acc[at, h * HD : (h + 1) * HD]
            x = x * cos + pair_swap(x, even) * sin
            x = jnp.where(upper, pltpu.roll(x, HD // 2, 1), x)
            out[row : row + LANES, h * HD : (h + 1) * HD] = x.astype(bf16)


def project_q(tokens, w_query, tables):
    rows = tokens.shape[0]
    cols = w_query.shape[1]
    whole = pl.BlockSpec(memory_space=pltpu.VMEM)
    out = jax.ShapeDtypeStruct((rows // 2, cols), bf16)
    return pl.pallas_call(
        q_body,
        in_specs=[whole] * 3,
        out_specs=[whole, whole],
        out_shape=[out, out],
        scratch_shapes=[pltpu.VMEM((rows, cols), f32)],
        compiler_params=pltpu.CompilerParams(vmem_limit_bytes=20 * MIB),
        name="project_q",
    )(near(tokens), near(w_query), near(tables))


def cent_body(chunks, groups, place, owner_counts, gain_in, cent_in, *refs):
    wide, norms, picked, gain, chosen, hit, match = refs[:7]
    cent, wide_buf, in_sems, out_sems = refs[7:]
    rows, feat = cent.shape
    size = rows // chunks
    block = norms.shape[1]
    loads = stream(cent_in, cent, in_sems, chunks, 0)
    stores = []
    for i in range(chunks):
        at = pl.ds(i * size, size)
        stores.append(pltpu.make_async_copy(wide_buf.at[at, :], wide.at[at, :], out_sems.at[i]))
    for c in loads:
        c.start()
    gain[...] = gain_in[...]
    slots = hit.shape[0]
    seg_total = chosen.shape[1]
    rank = lax.axis_index("tp")
    slot = lax.broadcasted_iota(i32, (slots, seg_total), 0)
    column = lax.broadcasted_iota(i32, (slots, seg_total), 1)
    for k in range(2):
        for m in range(groups):
            start, number = owner_span(owner_counts, rank ^ (2 * m + k))
            row = (k * groups + m) * slots
            taken = (slot + start == column) & (slot < number)
            chosen[row : row + slots, :] = jnp.where(taken, 1.0, 0.0)
    start, number = owner_span(owner_counts, rank)
    slot = lax.broadcasted_iota(i32, (slots, LANES), 0)
    column = lax.broadcasted_iota(i32, (slots, LANES), 1)
    hit[...] = jnp.where((slot + start == column) & (slot < number), 1.0, 0.0)
    third = lax.broadcasted_iota(i32, (1, match.shape[1]), 1) % seg_total
    assigned = jnp.zeros((1, match.shape[1]), i32)
    for r in range(seg_total):
        assigned = jnp.where(third == r, place[3, r], assigned)
    member = lax.broadcasted_iota(i32, (GROUP, match.shape[1]), 0)
    for r in range(seg_total):
        same = jnp.where(assigned == member + place[1, r], 1.0, 0.0)
        match[r * GROUP : (r + 1) * GROUP, :] = same.astype(bf16)

    def widen(b, carry):
        at = pl.ds(pl.multiple_of(b * block, block), block)
        c = cent[at, :].astype(f32)
        wide_buf[at, :] = c
        square = c * c
        part = square[:, :LANES]
        for g in range(1, feat // LANES):
            part = part + square[:, g * LANES : (g + 1) * LANES]
        norms[pl.ds(b, 1), :] = jnp.sum(part.T, axis=0, keepdims=True)
        return carry

    per_chunk = size // block
    for i in range(chunks):
        loads[i].wait()
        lax.fori_loop(i * per_chunk, (i + 1) * per_chunk, widen, 0)
        stores[i].start()
    for r in range(seg_total):
        first = pl.multiple_of(place[0, r], GROUP)
        picked[r * GROUP : (r + 1) * GROUP, :] = cent[pl.ds(first, GROUP), :]
    for c in stores:
        c.wait()


def widen_centroids(place, owner_counts, gain, centroids, groups, slots):
    rows, feat = centroids.shape
    count = place.shape[1]
    chunks = 4
    whole = pl.BlockSpec(memory_space=pltpu.VMEM)
    scalar = pl.BlockSpec(memory_space=pltpu.SMEM)
    in_hbm = pl.BlockSpec(memory_space=pltpu.HBM)

    def body(*refs):
        cent_body(chunks, groups, *refs)

    return pl.pallas_call(
        body,
        in_specs=[scalar, scalar, whole, in_hbm],
        out_specs=[in_hbm] + [whole] * 6,
        out_shape=[
            jax.ShapeDtypeStruct((rows, feat), f32),
            jax.ShapeDtypeStruct((8, rows // 8), f32),
            jax.ShapeDtypeStruct((count * GROUP, feat), bf16),
            jax.ShapeDtypeStruct((1, feat), f32),
            jax.ShapeDtypeStruct((2 * groups * slots, count), f32),
            jax.ShapeDtypeStruct((slots, LANES), f32),
            jax.ShapeDtypeStruct((count * GROUP, 3 * count), bf16),
        ],
        scratch_shapes=[
            pltpu.VMEM((rows, feat), bf16),
            pltpu.VMEM((rows, feat), f32),
            pltpu.SemaphoreType.DMA((chunks,)),
            pltpu.SemaphoreType.DMA((chunks,)),
        ],
        compiler_params=pltpu.CompilerParams(vmem_limit_bytes=24 * MIB),
        name="widen_centroids",
    )(place, owner_counts, gain, far(centroids))


def segment_starts(ids):
    rows = ids.shape[0]
    row = lax.broadcasted_iota(i32, ids.shape, 0)
    lane = lax.broadcasted_iota(i32, ids.shape, 1)
    left = pltpu.roll(ids, 1, 1)
    left = jnp.where(lane == 0, pltpu.roll(left, 1, 0), left)
    token = row * LANES + lane
    first = jnp.where((ids != left) & (token > 0), token, 0)
    shift = 1
    while shift < LANES:
        first = jnp.maximum(first, jnp.where(lane >= shift, pltpu.roll(first, shift, 1), 0))
        shift = shift * 2
    above = jnp.broadcast_to(jnp.max(first, axis=1, keepdims=True), ids.shape)
    above = jnp.where(row >= 1, pltpu.roll(above, 1, 0), 0)
    shift = 1
    while shift < rows:
        above = jnp.maximum(above, jnp.where(row >= shift, pltpu.roll(above, shift, 0), 0))
        shift = shift * 2
    return jnp.maximum(first, above)


def attend_body(pieces, seg_total, balanced, seg, ids, *refs):
    queries = refs[: 3 if balanced else 2]
    refs = refs[len(queries) :]
    own_in = refs[:pieces]
    other_in = refs[pieces : 2 * pieces]
    token_sums = refs[2 * pieces : 3 * pieces]
    out, counts, tokens_out, q_all, kv, starts, weights, tops, col, lhs, sems = refs[
        3 * pieces :
    ]
    q_rows, q_cols = queries[0].shape
    rows = own_in[0].shape[0]
    heads = q_cols // HD
    half = HD // 2
    seq_len = kv.shape[0]
    wide = heads * QB
    own_blocks = rows // QB
    rank = lax.axis_index("seq")
    upper = lax.axis_index("tp") % 2 == 1

    copies = []
    for k, source in enumerate(queries):
        target = q_all.at[pl.ds(k * q_rows, q_rows), :]
        copies.append(pltpu.make_async_copy(source, target, sems.at[len(copies)]))
    for k, sources in enumerate((own_in, other_in)):
        for m in range(pieces):
            row0 = pl.multiple_of((rank ^ m) * rows, rows)
            place = kv.at[pl.ds(row0, rows), pl.ds(k * HD, HD)]
            copies.append(pltpu.make_async_copy(sources[m], place, sems.at[len(copies)]))
    for c in copies:
        c.start()
    col[...] = jnp.zeros(col.shape, f32)
    starts[...] = segment_starts(ids[...])
    for c in copies:
        c.wait()

    def q_step(n, carry):
        home = n < own_blocks
        base = jnp.where(home, rank, rank ^ 3) * rows + jnp.where(home, n, n - own_blocks) * QB
        base = pl.multiple_of(base, QB)
        last_seg = seg[base + QB - 1]
        first_seg = seg[base]
        end = (base + QB - 1) // KB + 1
        clear_end = base // KB
        begin = jnp.int32(0)
        clear = jnp.int32(0)
        for t in range(seq_len // KB):
            begin = begin + (seg[t * KB + KB - 1] < first_seg).astype(i32)
            outside = (seg[t * KB] != last_seg) | (base + QB - 1 - t * KB >= WINDOW)
            clear = clear + (outside & (t < clear_end)).astype(i32)
        begin = jnp.maximum(begin, jnp.maximum(base - (WINDOW - 1), 0) // KB)
        begin = jnp.minimum(begin, clear_end)
        clear = jnp.clip(clear, begin, clear_end)

        q_at = pl.ds(pl.multiple_of(n * QB, QB), QB)
        nothing = jnp.zeros((QB, half), bf16)
        q = []
        for h in range(heads):
            x = q_all[q_at, h * HD : (h + 1) * HD]
            q.append(jnp.concatenate([x[:, :half], nothing, x[:, half:], nothing], 1))
        low = [starts[pl.ds(base // LANES + g, 1), :] for g in range(QB // LANES)]
        low = jnp.concatenate(low, 1)
        i_pos = base + lax.broadcasted_iota(i32, (1, QB), 1)
        if seq_len > WINDOW:
            low = jnp.maximum(low, i_pos - (WINDOW - 1))

        def score(masked, size, kb, carry):
            start = pl.multiple_of(kb * KB, KB)
            rows_kb = kv[pl.ds(start, size), :]
            if masked:
                j_pos = start + lax.broadcasted_iota(i32, (size, QB), 0)
                allowed = (j_pos <= i_pos) & (j_pos >= low)
            result = []
            for h in range(heads):
                top, total = carry[h]
                lanes = slice(h * QB, (h + 1) * QB)
                s = lax.dot_general(
                    rows_kb, q[h], (((1,), (1,)), ((), ())), preferred_element_type=f32
                )
                if masked:
                    s = jnp.where(allowed, s, -1e30)
                new_top = jnp.maximum(top, jnp.max(s, axis=0, keepdims=True))
                p = jnp.exp2(s - new_top)
                weights[pl.ds(start, size), lanes] = p.astype(bf16)
                tops[pl.ds(kb, 1), lanes] = new_top
                p = jnp.sum(p.reshape(size // 8, 8, QB), axis=0)
                result.append((new_top, total * jnp.exp2(top - new_top) + p))
            return tuple(result)

        state = (jnp.full((1, QB), -1e30, f32), jnp.zeros((8, QB), f32))
        state = (state,) * heads
        pairs = (clear_end - clear) // 2
        single = clear + 2 * pairs
        state = lax.fori_loop(begin, clear, lambda kb, c: score(True, KB, kb, c), state)
        state = lax.fori_loop(
            0, pairs, lambda t, c: score(False, 2 * KB, clear + 2 * t, c), state
        )
        state = lax.fori_loop(single, clear_end, lambda kb, c: score(False, KB, kb, c), state)
        state = lax.fori_loop(clear_end, end, lambda kb, c: score(True, KB, kb, c), state)
        top = jnp.concatenate([t for t, _ in state], 1)
        total = jnp.concatenate([t for _, t in state], 1)
        share = 1.0 / jnp.sum(total, axis=0, keepdims=True)
        row = lax.broadcasted_iota(i32, (16, wide), 0)
        head = lax.broadcasted_iota(i32, (16, wide), 1) // QB

        def gather(size, kb, carry):
            start = pl.multiple_of(kb * KB, KB)
            r = share * jnp.exp2(tops[pl.ds(kb, 1), :] - top)
            high = r.astype(bf16).astype(f32)
            r = jnp.where(row == head, high, jnp.where(row == heads + head, r - high, 0.0))
            at = pl.ds(start, size)
            contract = (((1,), (1,)), ((), ()))
            w = weights[at, :]
            r = r.astype(bf16)
            if COLUMNS_AS_ROWS:
                add = lax.dot_general(r, w, contract, preferred_element_type=f32)
                col[:16, at] = col[:16, at] + add
            else:
                add = lax.dot_general(w, r, contract, preferred_element_type=f32)
                col[at, :16] = col[at, :16] + add
            return carry

        lax.fori_loop(begin, clear, lambda kb, c: gather(KB, kb, c), 0)
        lax.fori_loop(0, pairs, lambda t, c: gather(2 * KB, clear + 2 * t, c), 0)
        lax.fori_loop(single, end, lambda kb, c: gather(KB, kb, c), 0)
        return carry

    if balanced:
        low_n = jnp.where(rank == 3, 2, jnp.where(rank == 2, 1, 0))
        high_n = own_blocks + jnp.where(rank == 0, 2, jnp.where(rank == 1, 1, 0))
    else:
        low_n = 0
        high_n = own_blocks
    lax.fori_loop(low_n, high_n, q_step, 0)

    number = jnp.zeros((seg_total, LANES), f32)
    for g in range(seq_len // LANES):
        at = slice(g * LANES, (g + 1) * LANES)
        member = ids[g : g + 1, :] == lax.broadcasted_iota(i32, (seg_total, LANES), 0)
        number = number + member.astype(f32)
        turned = col[:16, at] if COLUMNS_AS_ROWS else col[at, :].T
        for h in range(heads):
            w = turned[h : h + 1] + turned[heads + h : heads + h + 1]
            w = jnp.where(member, w, 0.0)
            high = w.astype(bf16)
            lhs[h * seg_total : (h + 1) * seg_total, at] = high
            rest = (w - high.astype(f32)).astype(bf16)
            lhs[(heads + h) * seg_total : (heads + h + 1) * seg_total, at] = rest
    sums = token_sums[0][...]
    for t in token_sums[1:]:
        sums = sums + t[...]
    tokens_out[...] = sums
    counts[...] = jnp.broadcast_to(jnp.sum(number, axis=1, keepdims=True), counts.shape)
    pooled = jnp.dot(lhs[...], kv[...], preferred_element_type=f32)
    pooled = jnp.concatenate([pooled[:, half:HD], pooled[:, HD + half :]], 1)
    for h in range(heads):
        x = pooled[h * seg_total : (h + 1) * seg_total]
        x = x + pooled[(heads + h) * seg_total : (heads + h + 1) * seg_total]
        out[:, h * HD : (h + 1) * HD] = jnp.where(upper, pltpu.roll(x, half, 1), x)


def attend(seg_ids, ids, queries, own, other, token_sums, seg_total, balanced):
    q_rows, cols = queries[0].shape
    rows = own[0].shape[0]
    seq_len = seg_ids.shape[0]
    pieces = len(own)
    heads = cols // HD
    whole = pl.BlockSpec(memory_space=pltpu.VMEM)
    anywhere = pl.BlockSpec(memory_space=pl.ANY)
    inputs = len(queries) + 2 * pieces

    def body(*refs):
        attend_body(pieces, seg_total, balanced, *refs)

    return pl.pallas_call(
        body,
        in_specs=[pl.BlockSpec(memory_space=pltpu.SMEM), whole]
        + [anywhere] * inputs
        + [whole] * pieces,
        out_specs=[whole, whole, whole],
        out_shape=[
            jax.ShapeDtypeStruct((seg_total, cols), f32),
            jax.ShapeDtypeStruct((seg_total, LANES), f32),
            jax.ShapeDtypeStruct(token_sums[0].shape, f32),
        ],
        scratch_shapes=[
            pltpu.VMEM((len(queries) * q_rows, cols), bf16),
            pltpu.VMEM((seq_len, 2 * HD), bf16),
            pltpu.VMEM((seq_len // LANES, LANES), i32),
            pltpu.VMEM((seq_len, heads * QB), bf16),
            pltpu.VMEM((max(8, seq_len // KB), heads * QB), f32),
            pltpu.VMEM((16, seq_len) if COLUMNS_AS_ROWS else (seq_len, LANES), f32),
            pltpu.VMEM((2 * heads * seg_total, seq_len), bf16),
            pltpu.SemaphoreType.DMA((inputs,)),
        ],
        compiler_params=pltpu.CompilerParams(vmem_limit_bytes=24 * MIB),
        name="attend",
    )(seg_ids, ids, *queries, *own, *other, *token_sums)


def mix_body(pieces, *refs):
    parts = refs[:pieces]
    norms, w_out, keep, send = refs[pieces:]
    groups, _, feat = keep.shape
    seg_total = parts[0].shape[0]
    mixed = parts[0][...]
    for p in parts[1:]:
        mixed = mixed + p[...]
    high = mixed.astype(bf16)
    low = (mixed - high.astype(f32)).astype(bf16)
    lhs = jnp.concatenate([high, low], 0)
    rank = lax.axis_index("tp")
    for k, target in enumerate((keep, send)):
        for m in range(groups):
            owner = rank ^ (2 * m + k)
            cols = pl.ds(pl.multiple_of(owner * feat, feat), feat)
            y = jnp.dot(lhs, w_out[:, cols], preferred_element_type=f32)
            target[m, :seg_total, :] = y[:seg_total] + y[seg_total:]
            target[m, seg_total:, :] = norms[...]


def mix(parts, norms, w_out, feat, groups):
    seg_total = parts[0].shape[0]
    whole = pl.BlockSpec(memory_space=pltpu.VMEM)
    out = jax.ShapeDtypeStruct((groups, seg_total + 8, feat), f32)

    def body(*refs):
        mix_body(len(parts), *refs)

    return pl.pallas_call(
        body,
        in_specs=[whole] * (len(parts) + 2),
        out_specs=[whole, whole],
        out_shape=[out, out],
        compiler_params=pltpu.CompilerParams(vmem_limit_bytes=16 * MIB),
        name="mix",
    )(*parts, norms, w_out)


def fold_body(groups, keep, received, own, *sends):
    rows = keep.shape[-1]
    own[...] = keep[0] + received[0]
    for m in range(1, groups):
        total = keep[m] + received[m]
        target = sends[m - 1]
        if target.dtype == f32:
            target[...] = total
        else:
            last = total[:, rows - LANES :]
            high = last.astype(bf16)
            target[:, : rows - LANES] = total[:, : rows - LANES].astype(bf16)
            target[:, rows - LANES : rows] = high
            target[:, rows:] = (last - high.astype(f32)).astype(bf16)


def fold(keep, received, kind):
    groups, rows, cols = keep.shape
    whole = pl.BlockSpec(memory_space=pltpu.VMEM)
    sent = jax.ShapeDtypeStruct((rows, cols if kind == f32 else cols + LANES), kind)

    def body(*refs):
        fold_body(groups, *refs)

    result = pl.pallas_call(
        body,
        in_specs=[whole, whole],
        out_specs=[whole] * groups,
        out_shape=[jax.ShapeDtypeStruct((rows, cols), f32)] + [sent] * (groups - 1),
        compiler_params=pltpu.CompilerParams(vmem_limit_bytes=12 * MIB),
        name="fold",
    )(keep, received)
    return [result[0]] + [swapped(result[m], "tp", 2 * m) for m in range(1, groups)]


def owner_span(owner_counts, owner):
    start = jnp.int32(0)
    for o in range(owner_counts.shape[0]):
        start = start + jnp.where(o < owner, owner_counts[o], 0)
    return start, owner_counts[owner]


def cross_body(groups, chunks, model_width, *refs):
    mixed = refs[:groups]
    token_sums, counts, gain, chosen, cent = refs[groups : groups + 5]
    keep, send, emb, norms, lhs = refs[groups + 5 :]
    seg_total, feat = emb.shape
    rows = cent.shape[0]
    slots = keep.shape[1]
    per_side = groups * slots

    total = mixed[0][...]
    for p in mixed[1:]:
        total = total + p[...]
    norms[...] = total[seg_total:]
    pooled = (total[:seg_total] + token_sums[...]) / counts[:, :1]
    square = jnp.sum(pooled * pooled, axis=1, keepdims=True)
    row = lax.broadcasted_iota(i32, (seg_total, LANES), 0)
    lane = lax.broadcasted_iota(i32, (seg_total, LANES), 1)
    square = jnp.sum(jnp.where(row == lane, square, 0.0), axis=0, keepdims=True)
    square = jnp.broadcast_to(square, (slots, LANES))
    scaled = pooled * gain[...]
    emb[...] = scaled
    high = scaled.astype(bf16)
    low = (scaled - high.astype(f32)).astype(bf16)
    picks = chosen[...].astype(bf16)
    factor = -2.0 / model_width**0.5
    lhs[: 2 * per_side] = (jnp.dot(picks, high, preferred_element_type=f32) * factor).astype(bf16)
    lhs[2 * per_side :] = (jnp.dot(picks, low, preferred_element_type=f32) * factor).astype(bf16)
    for target in (keep, send):
        for m in range(groups):
            target[m, :, rows:] = square

    size = rows // chunks
    for i in range(chunks):
        at = slice(i * size, (i + 1) * size)
        y = lax.dot_general(
            cent[at, :], lhs[...], (((1,), (1,)), ((), ())), preferred_element_type=f32
        ).T
        y = y[: 2 * per_side] + y[2 * per_side :]
        for k, target in enumerate((keep, send)):
            for m in range(groups):
                first = k * per_side + m * slots
                target[m, :, at] = y[first : first + slots]


def cross(mixed, token_sums, counts, gain, chosen, centroids, slots, model_width):
    rows, feat = centroids.shape
    groups = len(mixed)
    seg_total = counts.shape[0]
    whole = pl.BlockSpec(memory_space=pltpu.VMEM)
    side = jax.ShapeDtypeStruct((groups, slots, rows + LANES), f32)

    def body(*refs):
        cross_body(groups, 4, model_width, *refs)

    return pl.pallas_call(
        body,
        in_specs=[whole] * (groups + 5),
        out_specs=[whole] * 4,
        out_shape=[
            side,
            side,
            jax.ShapeDtypeStruct((seg_total, feat), f32),
            jax.ShapeDtypeStruct((8, rows // 8), f32),
        ],
        scratch_shapes=[pltpu.VMEM((4 * groups * slots, feat), bf16)],
        compiler_params=pltpu.CompilerParams(vmem_limit_bytes=16 * MIB),
        name="cross",
    )(*mixed, token_sums, counts, gain, chosen, centroids)


def finish_body(groups, model_width, place, *refs):
    terms = refs[:groups]
    norms, emb, hit, match, picked, wide_in, dist, wide, moved, sems = refs[groups:]
    seg_total, feat = emb.shape
    block = norms.shape[1]
    rows = dist.shape[1]
    total = terms[0][:, rows:]
    for t in terms[1:]:
        total = total + t[:, rows : rows + LANES].astype(f32)
        total = total + t[:, rows + LANES :].astype(f32)
    scale = lax.rsqrt(total / model_width + norm_eps)

    spread = jnp.broadcast_to(scale[:1], (seg_total, LANES))
    r_row = lax.broadcasted_iota(i32, (seg_total, LANES), 0)
    r_lane = lax.broadcasted_iota(i32, (seg_total, LANES), 1)
    row_scale = jnp.sum(jnp.where(r_row == r_lane, spread, 0.0), axis=1, keepdims=True)
    value = emb[...] * row_scale
    high = value.astype(bf16)
    rest = value - high.astype(f32)
    middle = rest.astype(bf16)
    low = (rest - middle.astype(f32)).astype(bf16)
    stacked = jnp.concatenate([high, middle, low], 0)
    once = lax.broadcasted_iota(i32, (3 * seg_total, LANES), 0) < seg_total
    stacked = jnp.concatenate([stacked, jnp.where(once, 1.0, 0.0).astype(bf16)], 1)
    added = jnp.dot(match[...], stacked, preferred_element_type=f32)
    shrink = 1.0 / (1.0 + added[:, feat:])
    for g in range(feat // LANES):
        at = slice(g * LANES, (g + 1) * LANES)
        moved[:, at] = (picked[:, at].astype(f32) + added[:, at]) * shrink

    def write(r):
        first = pl.multiple_of(place[0, r], GROUP)
        return pltpu.make_async_copy(
            moved.at[pl.ds(r * GROUP, GROUP), :], wide.at[pl.ds(first, GROUP), :], sems.at[r]
        )

    for r in range(seg_total):
        pl.when(place[2, r] == 1)(lambda r=r: write(r).start())

    own_scale = jnp.sum(hit[...] * scale, axis=1, keepdims=True)
    valid = jnp.sum(hit[...], axis=1, keepdims=True) > 0.0
    for g in range(rows // block):
        at = slice(g * block, (g + 1) * block)
        y = terms[0][:, at]
        for t in terms[1:]:
            y = y + t[:, at].astype(f32)
        y = norms[g : g + 1, :] * (1.0 / model_width**0.5) + y * own_scale
        dist[:, at] = jnp.where(valid, y, 0.0)

    for r in range(seg_total):
        pl.when(place[2, r] == 1)(lambda r=r: write(r).wait())


def finish(place, terms, norms, emb, hit, match, picked, wide, model_width):
    groups = len(terms)
    seg_total = emb.shape[0]
    slots, rows = terms[0].shape
    rows = rows - LANES
    whole = pl.BlockSpec(memory_space=pltpu.VMEM)
    in_hbm = pl.BlockSpec(memory_space=pltpu.HBM)
    scalar = pl.BlockSpec(memory_space=pltpu.SMEM)

    def body(*refs):
        finish_body(groups, model_width, *refs)

    return pl.pallas_call(
        body,
        in_specs=[scalar] + [whole] * (groups + 5) + [in_hbm],
        out_specs=[whole, in_hbm],
        out_shape=[
            jax.ShapeDtypeStruct((slots, rows), f32),
            jax.ShapeDtypeStruct(wide.shape, f32),
        ],
        scratch_shapes=[
            pltpu.VMEM((seg_total * GROUP, emb.shape[1]), f32),
            pltpu.SemaphoreType.DMA((seg_total,)),
        ],
        input_output_aliases={1 + groups + 5: 1},
        compiler_params=pltpu.CompilerParams(vmem_limit_bytes=16 * MIB),
        name="finish",
    )(place, *terms, norms, emb, hit, match, picked, wide)


def shards(
    tokens, w_query, w_key, w_value, w_out, seg_ids, owner_counts, centroids, pool_gain, assign
):
    tok_rows, model_width = tokens.shape
    seq_len = seg_ids.shape[0]
    seg_total = assign.shape[0]
    rank_seq = lax.axis_index("seq")
    seq_total = lax.axis_size("seq")
    tp_total = lax.axis_size("tp")
    groups = tp_total // 2
    feat = model_width // tp_total
    cent_rows = centroids.shape[0]
    slots = 2 * seg_total // owner_counts.shape[0]
    fine_np, coarse_np = angle_tables(seq_len)
    fine = jnp.asarray(fine_np)
    coarse = jnp.asarray(coarse_np)

    ids = seg_ids.reshape(seq_len // LANES, LANES)
    masks = range(1, seq_total)

    own, pooled, tables = project_kv(
        tokens, w_key, w_value, fine, coarse, ids, seg_total, model_width // tp_total
    )
    own = [own] + [swapped(own, "seq", m) for m in masks]
    other = [swapped(x, "tp", 1) for x in own]

    queries = list(project_q(tokens, w_query, tables))
    balanced = seq_total == 4 and seq_len <= WINDOW and tok_rows == 4 * QB
    if balanced:
        queries = queries + [lax.ppermute(queries[0], "seq", [(3, 0), (2, 1)])]

    local = assign - rank_seq * cent_rows
    mine = (local >= 0) & (local < cent_rows)
    first_row = jnp.where(mine, local // GROUP * GROUP, 0)
    line = assign // GROUP
    order = jnp.arange(seg_total, dtype=i32)
    repeat = jnp.any((line[:, None] == line[None, :]) & (order[None, :] < order[:, None]), axis=1)
    place = jnp.stack([first_row, line * GROUP, (mine & ~repeat).astype(i32), assign])
    wide, norms, picked, gain, chosen, hit, match = widen_centroids(
        place, owner_counts, pool_gain.reshape(1, feat), centroids, groups, slots
    )

    pooled_tokens = [pooled] + [swapped(pooled, "seq", m) for m in masks]

    queries, wide, norms, picked, gain, chosen, hit, match, pooled_tokens = lax.optimization_barrier(
        (queries, wide, norms, picked, gain, chosen, hit, match, pooled_tokens)
    )
    attended, counts, token_sums = attend(
        seg_ids, ids, queries, own, other, pooled_tokens, seg_total, balanced
    )
    attended = [attended] + [swapped(attended, "seq", m) for m in masks]

    keep, send = mix(attended, norms, w_out, feat, groups)
    mixed = fold(keep, swapped(send, "tp", 1), f32)

    keep, send, emb, norms = cross(
        mixed, token_sums, counts, gain, chosen, centroids, slots, model_width
    )
    terms = fold(keep, swapped(send, "tp", 1), bf16)
    distances, updated = finish(
        place, terms, norms, emb, hit, match, picked, wide, model_width
    )
    return (distances, updated)


def solution(mesh):
    in_specs = (
        P("seq", None),
        P(None, "tp"),
        P(None, "tp"),
        P(None, "tp"),
        P("tp", None),
        P(),
        P(),
        P("seq", "tp"),
        P("tp"),
        P(),
    )
    out_specs = (P("tp", "seq"), P("seq", "tp"))
    return jax.shard_map(shards, mesh=mesh, in_specs=in_specs, out_specs=out_specs, check_vma=False)
```

```python
import math

import jax
import jax.numpy as jnp
import numpy as np
from jax import lax
from jax.experimental import pallas as pl
from jax.experimental.pallas import tpu as pltpu
from jax.sharding import PartitionSpec as P

HD = 128
WINDOW = 4096
QB = 256
KB = 512
LANES = 128
GROUP = 16
TOKEN_CHUNKS = 8
AHEAD = 3
COLUMNS_AS_ROWS = True

rope_theta = 10000.0
norm_eps = 1e-06
MIB = 1024 * 1024

f32 = jnp.float32
bf16 = jnp.bfloat16
i32 = jnp.int32


def swapped(x, axis, mask):
    count = lax.axis_size(axis)
    return lax.ppermute(x, axis, [(i, i ^ mask) for i in range(count)])


def angle_tables(seq_len):
    inverse = np.exp(-(2.0 * np.arange(HD // 2) / HD) * math.log(rope_theta))
    inverse = np.repeat(inverse, 2)[None, :]
    fine = np.arange(LANES)[:, None] * inverse
    coarse = LANES * np.arange(seq_len // LANES)[:, None] * inverse
    fine_tab = np.stack([np.cos(fine), np.sin(fine)]).astype(np.float32)
    coarse_tab = np.stack([np.cos(coarse), np.sin(coarse)]).astype(np.float32)
    return fine_tab, coarse_tab


def turn(fine, coarse, which):
    ca = coarse[0, pl.ds(which, 1), :]
    sa = coarse[1, pl.ds(which, 1), :]
    cb = fine[0]
    sb = fine[1]
    return ca * cb - sa * sb, sa * cb + ca * sb


def pair_swap(x, even):
    up = pltpu.roll(x, x.shape[1] - 1, 1)
    down = pltpu.roll(x, 1, 1)
    return jnp.where(even, up, down)


def far(x):
    return pltpu.with_memory_space_constraint(x, pltpu.HBM)


def near(x):
    return pltpu.with_memory_space_constraint(x, pltpu.VMEM)


def stream(source, buffer, sems, chunks, axis):
    size = source.shape[axis] // chunks
    result = []
    for i in range(chunks):
        part = pl.ds(i * size, size)
        at = (part, slice(None)) if axis == 0 else (slice(None), part)
        result.append(pltpu.make_async_copy(source.at[at], buffer.at[at], sems.at[i]))
    return result


def kv_body(chunks, seg_total, *refs):
    ids_in, wk_in, wv_in, fine_in, coarse_in, tok_in = refs[:6]
    out, tables, tok, key_tables, weight, ids, fine, coarse, acc, small, sems = refs[6:]
    rows, width = tok.shape
    half = wk_in.shape[0]
    subs = rows // LANES
    size = width // chunks
    rest = [
        pltpu.make_async_copy(wk_in, weight.at[pl.ds(0, half), :], small.at[0]),
        pltpu.make_async_copy(wv_in, weight.at[pl.ds(half, half), :], small.at[1]),
        pltpu.make_async_copy(fine_in, fine, small.at[2]),
        pltpu.make_async_copy(coarse_in, coarse, small.at[3]),
        pltpu.make_async_copy(ids_in, ids, small.at[4]),
    ]
    for c in rest:
        c.start()
    copies = stream(tok_in, tok, sems, chunks, 1)
    for c in copies[:AHEAD]:
        c.start()
    for c in rest:
        c.wait()
    lane = lax.broadcasted_iota(i32, (LANES, LANES), 1)
    even = lane % 2 == 0
    upper = lax.axis_index("tp") % 2 == 1
    first = lax.axis_index("seq") * subs
    members = []
    for sub in range(subs):
        at = slice(sub * LANES, (sub + 1) * LANES)
        cos, sin = turn(fine, coarse, first + sub)
        sin = jnp.where(even, -sin, sin)
        tables[0, at, :] = cos
        tables[1, at, :] = sin
        cos = jnp.where(upper, pltpu.roll(cos, half, 1), cos)
        sin = jnp.where(upper, pltpu.roll(sin, half, 1), sin)
        key_tables[0, at, :] = jnp.where(lane < half, cos, 1.0)
        key_tables[1, at, :] = jnp.where(lane < half, sin, 0.0)
        member = ids[pl.ds(first + sub, 1), :] == lax.broadcasted_iota(i32, (seg_total, LANES), 0)
        members.append(jnp.where(member, 1.0, 0.0))
    for i in range(chunks):
        at = slice(i * size, (i + 1) * size)
        copies[i].wait()
        if i + AHEAD < chunks:
            copies[i + AHEAD].start()
        part = lax.dot_general(
            tok[:, at], weight[:, at], (((1,), (1,)), ((), ())), preferred_element_type=f32
        )
        acc[...] = part if i == 0 else acc[...] + part
    for sub in range(subs):
        at = slice(sub * LANES, (sub + 1) * LANES)
        x = acc[at]
        x = x * key_tables[0, at, :] + pair_swap(x, even) * key_tables[1, at, :]
        out[at, :] = x.astype(bf16)
    feat = (out.shape[0] - rows) // 2 // seg_total * LANES
    cols = pl.ds(pl.multiple_of(lax.axis_index("tp") * feat, feat), feat)
    member = jnp.concatenate(members, 1).astype(bf16)
    pooled = jnp.dot(member, tok[:, cols], preferred_element_type=f32)
    high = pooled.astype(bf16)
    low = (pooled - high.astype(f32)).astype(bf16)
    row = rows
    for part in (high, low):
        for g in range(feat // LANES):
            out[row : row + seg_total, :] = part[:, g * LANES : (g + 1) * LANES]
            row = row + seg_total


def project_kv(tokens, w_key, w_value, fine, coarse, ids, seg_total, feat):
    rows, width = tokens.shape
    half = w_key.shape[1]
    whole = pl.BlockSpec(memory_space=pltpu.VMEM)

    def body(*refs):
        kv_body(TOKEN_CHUNKS, seg_total, *refs)

    return pl.pallas_call(
        body,
        in_specs=[pl.BlockSpec(memory_space=pltpu.HBM)] * 6,
        out_specs=[whole] * 2,
        out_shape=[
            jax.ShapeDtypeStruct((rows + 2 * seg_total * feat // LANES, 2 * half), bf16),
            jax.ShapeDtypeStruct((2, rows, LANES), f32),
        ],
        scratch_shapes=[
            pltpu.VMEM((rows, width), bf16),
            pltpu.VMEM((2, rows, LANES), f32),
            pltpu.VMEM((2 * half, width), bf16),
            pltpu.VMEM(ids.shape, i32),
            pltpu.VMEM(fine.shape, f32),
            pltpu.VMEM(coarse.shape, f32),
            pltpu.VMEM((rows, 2 * half), f32),
            pltpu.SemaphoreType.DMA((5,)),
            pltpu.SemaphoreType.DMA((TOKEN_CHUNKS,)),
        ],
        compiler_params=pltpu.CompilerParams(vmem_limit_bytes=20 * MIB),
        cost_estimate=pl.CostEstimate(flops=2 * rows * width * 2 * half, bytes_accessed=2 * rows * width, transcendentals=0),
        name="project_kv",
    )(*[far(x) for x in (ids, w_key.T, w_value.T, fine, coarse, tokens)])


def q_body(tok, weight, tables, *refs):
    outs = refs[:2]
    acc = refs[2]
    rows = tok.shape[0]
    subs = rows // LANES
    per_out = subs // len(outs)
    heads = weight.shape[1] // HD
    acc[...] = jnp.dot(tok[...], weight[...], preferred_element_type=f32)
    even = lax.broadcasted_iota(i32, (LANES, LANES), 1) % 2 == 0
    upper = lax.axis_index("tp") % 2 == 1
    scale = HD ** (-0.5) * math.log2(math.e)
    for sub in range(subs):
        at = slice(sub * LANES, (sub + 1) * LANES)
        cos = tables[0, at, :] * scale
        sin = tables[1, at, :] * scale
        out = outs[sub // per_out]
        row = (sub % per_out) * LANES
        for h in range(heads):
            x = acc[at, h * HD : (h + 1) * HD]
            x = x * cos + pair_swap(x, even) * sin
            x = jnp.where(upper, pltpu.roll(x, HD // 2, 1), x)
            out[row : row + LANES, h * HD : (h + 1) * HD] = x.astype(bf16)


def project_q(tokens, w_query, tables):
    rows, width = tokens.shape
    cols = w_query.shape[1]
    whole = pl.BlockSpec(memory_space=pltpu.VMEM)
    out = jax.ShapeDtypeStruct((rows // 2, cols), bf16)
    return pl.pallas_call(
        q_body,
        in_specs=[whole] * 3,
        out_specs=[whole, whole],
        out_shape=[out, out],
        scratch_shapes=[pltpu.VMEM((rows, cols), f32)],
        compiler_params=pltpu.CompilerParams(vmem_limit_bytes=20 * MIB),
        cost_estimate=pl.CostEstimate(flops=2 * rows * width * cols, bytes_accessed=2 * rows * width + 2 * width * cols, transcendentals=0),
        name="project_q",
    )(near(tokens), near(w_query), near(tables))


def cent_body(chunks, groups, place, owner_counts, gain_in, cent_in, *refs):
    wide, norms, picked, gain, chosen, hit, match = refs[:7]
    cent, wide_buf, in_sems, out_sems = refs[7:]
    rows, feat = cent.shape
    size = rows // chunks
    block = norms.shape[1]
    loads = stream(cent_in, cent, in_sems, chunks, 0)
    stores = []
    for i in range(chunks):
        at = pl.ds(i * size, size)
        stores.append(pltpu.make_async_copy(wide_buf.at[at, :], wide.at[at, :], out_sems.at[i]))
    for c in loads:
        c.start()
    gain[...] = gain_in[...]
    slots = hit.shape[0]
    seg_total = chosen.shape[1]
    rank = lax.axis_index("tp")
    slot = lax.broadcasted_iota(i32, (slots, seg_total), 0)
    column = lax.broadcasted_iota(i32, (slots, seg_total), 1)
    for k in range(2):
        for m in range(groups):
            start, number = owner_span(owner_counts, rank ^ (2 * m + k))
            row = (k * groups + m) * slots
            taken = (slot + start == column) & (slot < number)
            chosen[row : row + slots, :] = jnp.where(taken, 1.0, 0.0)
    start, number = owner_span(owner_counts, rank)
    slot = lax.broadcasted_iota(i32, (slots, LANES), 0)
    column = lax.broadcasted_iota(i32, (slots, LANES), 1)
    hit[...] = jnp.where((slot + start == column) & (slot < number), 1.0, 0.0)
    third = lax.broadcasted_iota(i32, (1, match.shape[1]), 1) % seg_total
    assigned = jnp.zeros((1, match.shape[1]), i32)
    for r in range(seg_total):
        assigned = jnp.where(third == r, place[3, r], assigned)
    member = lax.broadcasted_iota(i32, (GROUP, match.shape[1]), 0)
    for r in range(seg_total):
        same = jnp.where(assigned == member + place[1, r], 1.0, 0.0)
        match[r * GROUP : (r + 1) * GROUP, :] = same.astype(bf16)

    def widen(b, carry):
        at = pl.ds(pl.multiple_of(b * block, block), block)
        c = cent[at, :].astype(f32)
        wide_buf[at, :] = c
        square = c * c
        part = square[:, :LANES]
        for g in range(1, feat // LANES):
            part = part + square[:, g * LANES : (g + 1) * LANES]
        norms[pl.ds(b, 1), :] = jnp.sum(part.T, axis=0, keepdims=True)
        return carry

    per_chunk = size // block
    for i in range(chunks):
        loads[i].wait()
        lax.fori_loop(i * per_chunk, (i + 1) * per_chunk, widen, 0)
        stores[i].start()
    for r in range(seg_total):
        first = pl.multiple_of(place[0, r], GROUP)
        picked[r * GROUP : (r + 1) * GROUP, :] = cent[pl.ds(first, GROUP), :]
    for c in stores:
        c.wait()


def widen_centroids(place, owner_counts, gain, centroids, groups, slots):
    rows, feat = centroids.shape
    count = place.shape[1]
    chunks = 4
    whole = pl.BlockSpec(memory_space=pltpu.VMEM)
    scalar = pl.BlockSpec(memory_space=pltpu.SMEM)
    in_hbm = pl.BlockSpec(memory_space=pltpu.HBM)

    def body(*refs):
        cent_body(chunks, groups, *refs)

    return pl.pallas_call(
        body,
        in_specs=[scalar, scalar, whole, in_hbm],
        out_specs=[in_hbm] + [whole] * 6,
        out_shape=[
            jax.ShapeDtypeStruct((rows, feat), f32),
            jax.ShapeDtypeStruct((8, rows // 8), f32),
            jax.ShapeDtypeStruct((count * GROUP, feat), bf16),
            jax.ShapeDtypeStruct((1, feat), f32),
            jax.ShapeDtypeStruct((2 * groups * slots, count), f32),
            jax.ShapeDtypeStruct((slots, LANES), f32),
            jax.ShapeDtypeStruct((count * GROUP, 3 * count), bf16),
        ],
        scratch_shapes=[
            pltpu.VMEM((rows, feat), bf16),
            pltpu.VMEM((rows, feat), f32),
            pltpu.SemaphoreType.DMA((chunks,)),
            pltpu.SemaphoreType.DMA((chunks,)),
        ],
        compiler_params=pltpu.CompilerParams(vmem_limit_bytes=24 * MIB),
        cost_estimate=pl.CostEstimate(flops=4 * rows * feat, bytes_accessed=6 * rows * feat, transcendentals=0),
        name="widen_centroids",
    )(place, owner_counts, gain, far(centroids))


def segment_starts(ids):
    rows = ids.shape[0]
    row = lax.broadcasted_iota(i32, ids.shape, 0)
    lane = lax.broadcasted_iota(i32, ids.shape, 1)
    left = pltpu.roll(ids, 1, 1)
    left = jnp.where(lane == 0, pltpu.roll(left, 1, 0), left)
    token = row * LANES + lane
    first = jnp.where((ids != left) & (token > 0), token, 0)
    shift = 1
    while shift < LANES:
        first = jnp.maximum(first, jnp.where(lane >= shift, pltpu.roll(first, shift, 1), 0))
        shift = shift * 2
    above = jnp.broadcast_to(jnp.max(first, axis=1, keepdims=True), ids.shape)
    above = jnp.where(row >= 1, pltpu.roll(above, 1, 0), 0)
    shift = 1
    while shift < rows:
        above = jnp.maximum(above, jnp.where(row >= shift, pltpu.roll(above, shift, 0), 0))
        shift = shift * 2
    return jnp.maximum(first, above)


def attend_body(pieces, seg_total, balanced, seg, ids, *refs):
    queries = refs[: 3 if balanced else 2]
    refs = refs[len(queries) :]
    own_in = refs[:pieces]
    other_in = refs[pieces : 2 * pieces]
    out, counts, tokens_out, tails, q_all, kv, starts, weights, tops, col, lhs, sems = refs[
        2 * pieces :
    ]
    q_rows, q_cols = queries[0].shape
    rows = own_in[0].shape[0] - tails.shape[1]
    heads = q_cols // HD
    half = HD // 2
    seq_len = kv.shape[0]
    wide = heads * QB
    own_blocks = rows // QB
    rank = lax.axis_index("seq")
    upper = lax.axis_index("tp") % 2 == 1

    copies = []
    for k, source in enumerate(queries):
        target = q_all.at[pl.ds(k * q_rows, q_rows), :]
        copies.append(pltpu.make_async_copy(source, target, sems.at[len(copies)]))
    for k, sources in enumerate((own_in, other_in)):
        for m in range(pieces):
            row0 = pl.multiple_of((rank ^ m) * rows, rows)
            place = kv.at[pl.ds(row0, rows), pl.ds(k * HD, HD)]
            source = sources[m].at[pl.ds(0, rows), :]
            copies.append(pltpu.make_async_copy(source, place, sems.at[len(copies)]))
    for m in range(pieces):
        source = own_in[m].at[pl.ds(rows, tails.shape[1]), :]
        copies.append(pltpu.make_async_copy(source, tails.at[m], sems.at[len(copies)]))
    for c in copies:
        c.start()
    col[...] = jnp.zeros(col.shape, f32)
    starts[...] = segment_starts(ids[...])
    for c in copies:
        c.wait()

    def q_step(n, carry):
        home = n < own_blocks
        base = jnp.where(home, rank, rank ^ 3) * rows + jnp.where(home, n, n - own_blocks) * QB
        base = pl.multiple_of(base, QB)
        last_seg = seg[base + QB - 1]
        first_seg = seg[base]
        end = (base + QB - 1) // KB + 1
        clear_end = base // KB
        begin = jnp.int32(0)
        clear = jnp.int32(0)
        for t in range(seq_len // KB):
            begin = begin + (seg[t * KB + KB - 1] < first_seg).astype(i32)
            outside = (seg[t * KB] != last_seg) | (base + QB - 1 - t * KB >= WINDOW)
            clear = clear + (outside & (t < clear_end)).astype(i32)
        begin = jnp.maximum(begin, jnp.maximum(base - (WINDOW - 1), 0) // KB)
        begin = jnp.minimum(begin, clear_end)
        clear = jnp.clip(clear, begin, clear_end)

        q_at = pl.ds(pl.multiple_of(n * QB, QB), QB)
        nothing = jnp.zeros((QB, half), bf16)
        q = []
        for h in range(heads):
            x = q_all[q_at, h * HD : (h + 1) * HD]
            q.append(jnp.concatenate([x[:, :half], nothing, x[:, half:], nothing], 1))
        low = [starts[pl.ds(base // LANES + g, 1), :] for g in range(QB // LANES)]
        low = jnp.concatenate(low, 1)
        i_pos = base + lax.broadcasted_iota(i32, (1, QB), 1)
        if seq_len > WINDOW:
            low = jnp.maximum(low, i_pos - (WINDOW - 1))

        def score(masked, size, kb, carry):
            start = pl.multiple_of(kb * KB, KB)
            rows_kb = kv[pl.ds(start, size), :]
            if masked:
                j_pos = start + lax.broadcasted_iota(i32, (size, QB), 0)
                allowed = (j_pos <= i_pos) & (j_pos >= low)
            result = []
            for h in range(heads):
                top, total = carry[h]
                lanes = slice(h * QB, (h + 1) * QB)
                s = lax.dot_general(
                    rows_kb, q[h], (((1,), (1,)), ((), ())), preferred_element_type=f32
                )
                if masked:
                    s = jnp.where(allowed, s, -1e30)
                new_top = jnp.maximum(top, jnp.max(s, axis=0, keepdims=True))
                p = jnp.exp2(s - new_top)
                weights[pl.ds(start, size), lanes] = p.astype(bf16)
                tops[pl.ds(kb, 1), lanes] = new_top
                p = jnp.sum(p.reshape(size // 8, 8, QB), axis=0)
                result.append((new_top, total * jnp.exp2(top - new_top) + p))
            return tuple(result)

        state = (jnp.full((1, QB), -1e30, f32), jnp.zeros((8, QB), f32))
        state = (state,) * heads
        pairs = (clear_end - clear) // 2
        single = clear + 2 * pairs
        state = lax.fori_loop(begin, clear, lambda kb, c: score(True, KB, kb, c), state)
        state = lax.fori_loop(
            0, pairs, lambda t, c: score(False, 2 * KB, clear + 2 * t, c), state
        )
        state = lax.fori_loop(single, clear_end, lambda kb, c: score(False, KB, kb, c), state)
        state = lax.fori_loop(clear_end, end, lambda kb, c: score(True, KB, kb, c), state)
        top = jnp.concatenate([t for t, _ in state], 1)
        total = jnp.concatenate([t for _, t in state], 1)
        share = 1.0 / jnp.sum(total, axis=0, keepdims=True)
        row = lax.broadcasted_iota(i32, (16, wide), 0)
        head = lax.broadcasted_iota(i32, (16, wide), 1) // QB

        def gather(size, kb, carry):
            start = pl.multiple_of(kb * KB, KB)
            r = share * jnp.exp2(tops[pl.ds(kb, 1), :] - top)
            high = r.astype(bf16).astype(f32)
            r = jnp.where(row == head, high, jnp.where(row == heads + head, r - high, 0.0))
            at = pl.ds(start, size)
            contract = (((1,), (1,)), ((), ()))
            w = weights[at, :]
            r = r.astype(bf16)
            if COLUMNS_AS_ROWS:
                add = lax.dot_general(r, w, contract, preferred_element_type=f32)
                col[:16, at] = col[:16, at] + add
            else:
                add = lax.dot_general(w, r, contract, preferred_element_type=f32)
                col[at, :16] = col[at, :16] + add
            return carry

        lax.fori_loop(begin, clear, lambda kb, c: gather(KB, kb, c), 0)
        lax.fori_loop(0, pairs, lambda t, c: gather(2 * KB, clear + 2 * t, c), 0)
        lax.fori_loop(single, end, lambda kb, c: gather(KB, kb, c), 0)
        return carry

    if balanced:
        low_n = jnp.where(rank == 3, 2, jnp.where(rank == 2, 1, 0))
        high_n = own_blocks + jnp.where(rank == 0, 2, jnp.where(rank == 1, 1, 0))
    else:
        low_n = 0
        high_n = own_blocks
    lax.fori_loop(low_n, high_n, q_step, 0)

    number = jnp.zeros((seg_total, LANES), f32)
    for g in range(seq_len // LANES):
        at = slice(g * LANES, (g + 1) * LANES)
        member = ids[g : g + 1, :] == lax.broadcasted_iota(i32, (seg_total, LANES), 0)
        number = number + member.astype(f32)
        turned = col[:16, at] if COLUMNS_AS_ROWS else col[at, :].T
        for h in range(heads):
            w = turned[h : h + 1] + turned[heads + h : heads + h + 1]
            w = jnp.where(member, w, 0.0)
            high = w.astype(bf16)
            lhs[h * seg_total : (h + 1) * seg_total, at] = high
            rest = (w - high.astype(f32)).astype(bf16)
            lhs[(heads + h) * seg_total : (heads + h + 1) * seg_total, at] = rest
    parts = tokens_out.shape[1] // LANES
    for g in range(parts):
        sums = jnp.zeros((seg_total, LANES), f32)
        for m in range(pieces):
            for first in (g * seg_total, (parts + g) * seg_total):
                sums = sums + tails[m, first : first + seg_total, :].astype(f32)
        tokens_out[:, g * LANES : (g + 1) * LANES] = sums
    counts[...] = jnp.broadcast_to(jnp.sum(number, axis=1, keepdims=True), counts.shape)
    pooled = jnp.dot(lhs[...], kv[...], preferred_element_type=f32)
    pooled = jnp.concatenate([pooled[:, half:HD], pooled[:, HD + half :]], 1)
    for h in range(heads):
        x = pooled[h * seg_total : (h + 1) * seg_total]
        x = x + pooled[(heads + h) * seg_total : (heads + h + 1) * seg_total]
        out[:, h * HD : (h + 1) * HD] = jnp.where(upper, pltpu.roll(x, half, 1), x)


def attend(seg_ids, ids, queries, own, other, feat, seg_total, balanced):
    q_rows, cols = queries[0].shape
    tail = 2 * seg_total * feat // LANES
    seq_len = seg_ids.shape[0]
    pieces = len(own)
    heads = cols // HD
    whole = pl.BlockSpec(memory_space=pltpu.VMEM)
    anywhere = pl.BlockSpec(memory_space=pl.ANY)
    inputs = len(queries) + 2 * pieces

    def body(*refs):
        attend_body(pieces, seg_total, balanced, *refs)

    return pl.pallas_call(
        body,
        in_specs=[pl.BlockSpec(memory_space=pltpu.SMEM), whole]
        + [anywhere] * inputs,
        out_specs=[whole, whole, whole],
        out_shape=[
            jax.ShapeDtypeStruct((seg_total, cols), f32),
            jax.ShapeDtypeStruct((seg_total, LANES), f32),
            jax.ShapeDtypeStruct((seg_total, feat), f32),
        ],
        scratch_shapes=[
            pltpu.VMEM((pieces, tail, HD), bf16),
            pltpu.VMEM((len(queries) * q_rows, cols), bf16),
            pltpu.VMEM((seq_len, 2 * HD), bf16),
            pltpu.VMEM((seq_len // LANES, LANES), i32),
            pltpu.VMEM((seq_len, heads * QB), bf16),
            pltpu.VMEM((max(8, seq_len // KB), heads * QB), f32),
            pltpu.VMEM((16, seq_len) if COLUMNS_AS_ROWS else (seq_len, LANES), f32),
            pltpu.VMEM((2 * heads * seg_total, seq_len), bf16),
            pltpu.SemaphoreType.DMA((inputs + pieces,)),
        ],
        compiler_params=pltpu.CompilerParams(vmem_limit_bytes=24 * MIB),
        cost_estimate=pl.CostEstimate(flops=8 * q_rows * cols * seq_len, bytes_accessed=4 * seq_len * HD, transcendentals=0),
        name="attend",
    )(seg_ids, ids, *queries, *own, *other)


def mix_body(pieces, *refs):
    parts = refs[:pieces]
    norms, w_out, keep, send = refs[pieces:]
    groups, _, feat = keep.shape
    seg_total = parts[0].shape[0]
    mixed = parts[0][...]
    for p in parts[1:]:
        mixed = mixed + p[...]
    high = mixed.astype(bf16)
    low = (mixed - high.astype(f32)).astype(bf16)
    lhs = jnp.concatenate([high, low], 0)
    rank = lax.axis_index("tp")
    for k, target in enumerate((keep, send)):
        for m in range(groups):
            owner = rank ^ (2 * m + k)
            cols = pl.ds(pl.multiple_of(owner * feat, feat), feat)
            y = jnp.dot(lhs, w_out[:, cols], preferred_element_type=f32)
            target[m, :seg_total, :] = y[:seg_total] + y[seg_total:]
            target[m, seg_total:, :] = norms[...]


def mix(parts, norms, w_out, feat, groups):
    seg_total = parts[0].shape[0]
    whole = pl.BlockSpec(memory_space=pltpu.VMEM)
    out = jax.ShapeDtypeStruct((groups, seg_total + 8, feat), f32)

    def body(*refs):
        mix_body(len(parts), *refs)

    return pl.pallas_call(
        body,
        in_specs=[whole] * (len(parts) + 2),
        out_specs=[whole, whole],
        out_shape=[out, out],
        compiler_params=pltpu.CompilerParams(vmem_limit_bytes=16 * MIB),
        name="mix",
    )(*parts, norms, w_out)


def fold_body(groups, edge, keep, received, own, *sends):
    _, rows, cols = keep.shape
    own[...] = keep[0] + received[0]
    for m in range(1, groups):
        total = keep[m] + received[m]
        target = sends[m - 1]
        if edge == "rows":
            inner = rows - 8
            last = total[inner:]
            high = last.astype(bf16).astype(f32)
            target[:inner, :] = total[:inner].astype(bf16)
            target[inner:, :] = jnp.concatenate([high, last - high], 0).astype(bf16)
        else:
            inner = cols - LANES
            last = total[:, inner:]
            high = last.astype(bf16)
            target[:, :inner] = total[:, :inner].astype(bf16)
            target[:, inner:cols] = high
            target[:, cols:] = (last - high.astype(f32)).astype(bf16)


def fold(keep, received, edge):
    groups, rows, cols = keep.shape
    whole = pl.BlockSpec(memory_space=pltpu.VMEM)
    shape = (rows + 8, cols) if edge == "rows" else (rows, cols + LANES)

    def body(*refs):
        fold_body(groups, edge, *refs)

    result = pl.pallas_call(
        body,
        in_specs=[whole, whole],
        out_specs=[whole] * groups,
        out_shape=[jax.ShapeDtypeStruct((rows, cols), f32)]
        + [jax.ShapeDtypeStruct(shape, bf16)] * (groups - 1),
        compiler_params=pltpu.CompilerParams(vmem_limit_bytes=12 * MIB),
        name="fold",
    )(keep, received)
    return [result[0]] + [swapped(result[m], "tp", 2 * m) for m in range(1, groups)]


def owner_span(owner_counts, owner):
    start = jnp.int32(0)
    for o in range(owner_counts.shape[0]):
        start = start + jnp.where(o < owner, owner_counts[o], 0)
    return start, owner_counts[owner]


def cross_body(groups, chunks, model_width, *refs):
    mixed = refs[:groups]
    token_sums, counts, gain, chosen, cent = refs[groups : groups + 5]
    keep, send, emb, norms, lhs = refs[groups + 5 :]
    seg_total, feat = emb.shape
    rows = cent.shape[0]
    slots = keep.shape[1]
    per_side = groups * slots

    total = mixed[0][:seg_total, :] + token_sums[...]
    square = mixed[0][seg_total:, :]
    for p in mixed[1:]:
        total = total + p[:seg_total, :].astype(f32)
        terms = p[seg_total:, :].astype(f32)
        square = square + (terms[:8] + terms[8:])
    norms[...] = square
    pooled = total / counts[:, :1]
    square = jnp.sum(pooled * pooled, axis=1, keepdims=True)
    row = lax.broadcasted_iota(i32, (seg_total, LANES), 0)
    lane = lax.broadcasted_iota(i32, (seg_total, LANES), 1)
    square = jnp.sum(jnp.where(row == lane, square, 0.0), axis=0, keepdims=True)
    square = jnp.broadcast_to(square, (slots, LANES))
    scaled = pooled * gain[...]
    emb[...] = scaled
    high = scaled.astype(bf16)
    low = (scaled - high.astype(f32)).astype(bf16)
    picks = chosen[...].astype(bf16)
    factor = -2.0 / model_width**0.5
    lhs[: 2 * per_side] = (jnp.dot(picks, high, preferred_element_type=f32) * factor).astype(bf16)
    lhs[2 * per_side :] = (jnp.dot(picks, low, preferred_element_type=f32) * factor).astype(bf16)
    for target in (keep, send):
        for m in range(groups):
            target[m, :, rows:] = square

    size = rows // chunks
    for i in range(chunks):
        at = slice(i * size, (i + 1) * size)
        y = lax.dot_general(
            cent[at, :], lhs[...], (((1,), (1,)), ((), ())), preferred_element_type=f32
        ).T
        y = y[: 2 * per_side] + y[2 * per_side :]
        for k, target in enumerate((keep, send)):
            for m in range(groups):
                first = k * per_side + m * slots
                target[m, :, at] = y[first : first + slots]


def cross(mixed, token_sums, counts, gain, chosen, centroids, slots, model_width):
    rows, feat = centroids.shape
    groups = len(mixed)
    seg_total = counts.shape[0]
    whole = pl.BlockSpec(memory_space=pltpu.VMEM)
    side = jax.ShapeDtypeStruct((groups, slots, rows + LANES), f32)

    def body(*refs):
        cross_body(groups, 4, model_width, *refs)

    return pl.pallas_call(
        body,
        in_specs=[whole] * (groups + 5),
        out_specs=[whole] * 4,
        out_shape=[
            side,
            side,
            jax.ShapeDtypeStruct((seg_total, feat), f32),
            jax.ShapeDtypeStruct((8, rows // 8), f32),
        ],
        scratch_shapes=[pltpu.VMEM((4 * groups * slots, feat), bf16)],
        compiler_params=pltpu.CompilerParams(vmem_limit_bytes=16 * MIB),
        name="cross",
    )(*mixed, token_sums, counts, gain, chosen, centroids)


def finish_body(groups, model_width, place, *refs):
    terms = refs[:groups]
    norms, emb, hit, match, picked, wide_in, dist, wide, moved, sems = refs[groups:]
    seg_total, feat = emb.shape
    block = norms.shape[1]
    rows = dist.shape[1]
    total = terms[0][:, rows:]
    for t in terms[1:]:
        total = total + t[:, rows : rows + LANES].astype(f32)
        total = total + t[:, rows + LANES :].astype(f32)
    scale = lax.rsqrt(total / model_width + norm_eps)

    spread = jnp.broadcast_to(scale[:1], (seg_total, LANES))
    r_row = lax.broadcasted_iota(i32, (seg_total, LANES), 0)
    r_lane = lax.broadcasted_iota(i32, (seg_total, LANES), 1)
    row_scale = jnp.sum(jnp.where(r_row == r_lane, spread, 0.0), axis=1, keepdims=True)
    value = emb[...] * row_scale
    high = value.astype(bf16)
    rest = value - high.astype(f32)
    middle = rest.astype(bf16)
    low = (rest - middle.astype(f32)).astype(bf16)
    stacked = jnp.concatenate([high, middle, low], 0)
    once = lax.broadcasted_iota(i32, (3 * seg_total, LANES), 0) < seg_total
    stacked = jnp.concatenate([stacked, jnp.where(once, 1.0, 0.0).astype(bf16)], 1)
    added = jnp.dot(match[...], stacked, preferred_element_type=f32)
    shrink = 1.0 / (1.0 + added[:, feat:])
    for g in range(feat // LANES):
        at = slice(g * LANES, (g + 1) * LANES)
        moved[:, at] = (picked[:, at].astype(f32) + added[:, at]) * shrink

    def write(r):
        first = pl.multiple_of(place[0, r], GROUP)
        return pltpu.make_async_copy(
            moved.at[pl.ds(r * GROUP, GROUP), :], wide.at[pl.ds(first, GROUP), :], sems.at[r]
        )

    for r in range(seg_total):
        pl.when(place[2, r] == 1)(lambda r=r: write(r).start())

    own_scale = jnp.sum(hit[...] * scale, axis=1, keepdims=True)
    valid = jnp.sum(hit[...], axis=1, keepdims=True) > 0.0
    for g in range(rows // block):
        at = slice(g * block, (g + 1) * block)
        y = terms[0][:, at]
        for t in terms[1:]:
            y = y + t[:, at].astype(f32)
        y = norms[g : g + 1, :] * (1.0 / model_width**0.5) + y * own_scale
        dist[:, at] = jnp.where(valid, y, 0.0)

    for r in range(seg_total):
        pl.when(place[2, r] == 1)(lambda r=r: write(r).wait())


def finish(place, terms, norms, emb, hit, match, picked, wide, model_width):
    groups = len(terms)
    seg_total = emb.shape[0]
    slots, rows = terms[0].shape
    rows = rows - LANES
    whole = pl.BlockSpec(memory_space=pltpu.VMEM)
    in_hbm = pl.BlockSpec(memory_space=pltpu.HBM)
    scalar = pl.BlockSpec(memory_space=pltpu.SMEM)

    def body(*refs):
        finish_body(groups, model_width, *refs)

    return pl.pallas_call(
        body,
        in_specs=[scalar] + [whole] * (groups + 5) + [in_hbm],
        out_specs=[whole, in_hbm],
        out_shape=[
            jax.ShapeDtypeStruct((slots, rows), f32),
            jax.ShapeDtypeStruct(wide.shape, f32),
        ],
        scratch_shapes=[
            pltpu.VMEM((seg_total * GROUP, emb.shape[1]), f32),
            pltpu.SemaphoreType.DMA((seg_total,)),
        ],
        input_output_aliases={1 + groups + 5: 1},
        compiler_params=pltpu.CompilerParams(vmem_limit_bytes=16 * MIB),
        name="finish",
    )(place, *terms, norms, emb, hit, match, picked, wide)


def shards(
    tokens, w_query, w_key, w_value, w_out, seg_ids, owner_counts, centroids, pool_gain, assign
):
    tok_rows, model_width = tokens.shape
    seq_len = seg_ids.shape[0]
    seg_total = assign.shape[0]
    rank_seq = lax.axis_index("seq")
    seq_total = lax.axis_size("seq")
    tp_total = lax.axis_size("tp")
    groups = tp_total // 2
    feat = model_width // tp_total
    cent_rows = centroids.shape[0]
    slots = 2 * seg_total // owner_counts.shape[0]
    fine_np, coarse_np = angle_tables(seq_len)
    fine = jnp.asarray(fine_np)
    coarse = jnp.asarray(coarse_np)

    ids = seg_ids.reshape(seq_len // LANES, LANES)
    masks = range(1, seq_total)

    own, tables = project_kv(
        tokens, w_key, w_value, fine, coarse, ids, seg_total, model_width // tp_total
    )
    own = [own] + [swapped(own, "seq", m) for m in masks]
    other = [swapped(x, "tp", 1) for x in own]

    queries = list(project_q(tokens, w_query, tables))
    balanced = seq_total == 4 and seq_len <= WINDOW and tok_rows == 4 * QB
    if balanced:
        queries = queries + [lax.ppermute(queries[0], "seq", [(3, 0), (2, 1)])]

    local = assign - rank_seq * cent_rows
    mine = (local >= 0) & (local < cent_rows)
    first_row = jnp.where(mine, local // GROUP * GROUP, 0)
    line = assign // GROUP
    order = jnp.arange(seg_total, dtype=i32)
    repeat = jnp.any((line[:, None] == line[None, :]) & (order[None, :] < order[:, None]), axis=1)
    place = jnp.stack([first_row, line * GROUP, (mine & ~repeat).astype(i32), assign])
    wide, norms, picked, gain, chosen, hit, match = widen_centroids(
        place, owner_counts, pool_gain.reshape(1, feat), centroids, groups, slots
    )

    queries, wide, norms, picked, gain, chosen, hit, match = lax.optimization_barrier(
        (queries, wide, norms, picked, gain, chosen, hit, match)
    )
    attended, counts, token_sums = attend(
        seg_ids, ids, queries, own, other, feat, seg_total, balanced
    )
    attended = [attended] + [swapped(attended, "seq", m) for m in masks]

    keep, send = mix(attended, norms, w_out, feat, groups)
    mixed = fold(keep, swapped(send, "tp", 1), "rows")

    keep, send, emb, norms = cross(
        mixed, token_sums, counts, gain, chosen, centroids, slots, model_width
    )
    terms = fold(keep, swapped(send, "tp", 1), "columns")
    distances, updated = finish(
        place, terms, norms, emb, hit, match, picked, wide, model_width
    )
    return (distances, updated)


def solution(mesh):
    in_specs = (
        P("seq", None),
        P(None, "tp"),
        P(None, "tp"),
        P(None, "tp"),
        P("tp", None),
        P(),
        P(),
        P("seq", "tp"),
        P("tp"),
        P(),
    )
    out_specs = (P("tp", "seq"), P("seq", "tp"))
    return jax.shard_map(shards, mesh=mesh, in_specs=in_specs, out_specs=out_specs, check_vma=False)
```

```python
import math

import jax
import jax.numpy as jnp
import numpy as np
from jax import lax
from jax.experimental import pallas as pl
from jax.experimental.pallas import tpu as pltpu
from jax.sharding import PartitionSpec as P

HD = 128
WINDOW = 4096
QB = 256
KB = 512
LANES = 128
GROUP = 16
COLUMNS_AS_ROWS = True

rope_theta = 10000.0
norm_eps = 1e-06
MIB = 1024 * 1024

f32 = jnp.float32
bf16 = jnp.bfloat16
i32 = jnp.int32


def swapped(x, axis, mask):
    count = lax.axis_size(axis)
    return lax.ppermute(x, axis, [(i, i ^ mask) for i in range(count)])


def angle_tables(seq_len):
    inverse = np.exp(-(2.0 * np.arange(HD // 2) / HD) * math.log(rope_theta))
    inverse = np.repeat(inverse, 2)[None, :]
    fine = np.arange(LANES)[:, None] * inverse
    coarse = LANES * np.arange(seq_len // LANES)[:, None] * inverse
    fine_tab = np.stack([np.cos(fine), np.sin(fine)]).astype(np.float32)
    coarse_tab = np.stack([np.cos(coarse), np.sin(coarse)]).astype(np.float32)
    return fine_tab, coarse_tab


def turn(fine, coarse, which):
    ca = coarse[0, pl.ds(which, 1), :]
    sa = coarse[1, pl.ds(which, 1), :]
    cb = fine[0]
    sb = fine[1]
    return ca * cb - sa * sb, sa * cb + ca * sb


def pair_swap(x, even):
    up = pltpu.roll(x, x.shape[1] - 1, 1)
    down = pltpu.roll(x, 1, 1)
    return jnp.where(even, up, down)


def far(x):
    return pltpu.with_memory_space_constraint(x, pltpu.HBM)


def near(x):
    return pltpu.with_memory_space_constraint(x, pltpu.VMEM)


def stream(source, buffer, sems, chunks, axis):
    size = source.shape[axis] // chunks
    result = []
    for i in range(chunks):
        part = pl.ds(i * size, size)
        at = (part, slice(None)) if axis == 0 else (slice(None), part)
        result.append(pltpu.make_async_copy(source.at[at], buffer.at[at], sems.at[i]))
    return result


def kv_body(seg_total, *refs):
    ids_in, wk_in, wv_in, fine_in, coarse_in, tok = refs[:6]
    out, tables, key_tables, weight, ids, fine, coarse, acc, small = refs[6:]
    rows, _ = tok.shape
    half = wk_in.shape[0]
    subs = rows // LANES
    rest = [
        pltpu.make_async_copy(wk_in, weight.at[pl.ds(0, half), :], small.at[0]),
        pltpu.make_async_copy(wv_in, weight.at[pl.ds(half, half), :], small.at[1]),
        pltpu.make_async_copy(fine_in, fine, small.at[2]),
        pltpu.make_async_copy(coarse_in, coarse, small.at[3]),
        pltpu.make_async_copy(ids_in, ids, small.at[4]),
    ]
    for c in rest:
        c.start()
    for c in rest:
        c.wait()
    lane = lax.broadcasted_iota(i32, (LANES, LANES), 1)
    even = lane % 2 == 0
    upper = lax.axis_index("tp") % 2 == 1
    first = lax.axis_index("seq") * subs
    members = []
    for sub in range(subs):
        at = slice(sub * LANES, (sub + 1) * LANES)
        cos, sin = turn(fine, coarse, first + sub)
        sin = jnp.where(even, -sin, sin)
        tables[0, at, :] = cos
        tables[1, at, :] = sin
        cos = jnp.where(upper, pltpu.roll(cos, half, 1), cos)
        sin = jnp.where(upper, pltpu.roll(sin, half, 1), sin)
        key_tables[0, at, :] = jnp.where(lane < half, cos, 1.0)
        key_tables[1, at, :] = jnp.where(lane < half, sin, 0.0)
        member = ids[pl.ds(first + sub, 1), :] == lax.broadcasted_iota(i32, (seg_total, LANES), 0)
        members.append(jnp.where(member, 1.0, 0.0))
    acc[...] = lax.dot_general(
        tok[...], weight[...], (((1,), (1,)), ((), ())), preferred_element_type=f32
    )
    for sub in range(subs):
        at = slice(sub * LANES, (sub + 1) * LANES)
        x = acc[at]
        x = x * key_tables[0, at, :] + pair_swap(x, even) * key_tables[1, at, :]
        out[at, :] = x.astype(bf16)
    feat = (out.shape[0] - rows) // 2 // seg_total * LANES
    cols = pl.ds(pl.multiple_of(lax.axis_index("tp") * feat, feat), feat)
    member = jnp.concatenate(members, 1).astype(bf16)
    pooled = jnp.dot(member, tok[:, cols], preferred_element_type=f32)
    high = pooled.astype(bf16)
    low = (pooled - high.astype(f32)).astype(bf16)
    row = rows
    for part in (high, low):
        for g in range(feat // LANES):
            out[row : row + seg_total, :] = part[:, g * LANES : (g + 1) * LANES]
            row = row + seg_total


def project_kv(tokens, w_key, w_value, fine, coarse, ids, seg_total, feat):
    rows, width = tokens.shape
    half = w_key.shape[1]
    whole = pl.BlockSpec(memory_space=pltpu.VMEM)

    def body(*refs):
        kv_body(seg_total, *refs)

    return pl.pallas_call(
        body,
        in_specs=[pl.BlockSpec(memory_space=pltpu.HBM)] * 5 + [whole],
        out_specs=[whole] * 2,
        out_shape=[
            jax.ShapeDtypeStruct((rows + 2 * seg_total * feat // LANES, 2 * half), bf16),
            jax.ShapeDtypeStruct((2, rows, LANES), f32),
        ],
        scratch_shapes=[
            pltpu.VMEM((2, rows, LANES), f32),
            pltpu.VMEM((2 * half, width), bf16),
            pltpu.VMEM(ids.shape, i32),
            pltpu.VMEM(fine.shape, f32),
            pltpu.VMEM(coarse.shape, f32),
            pltpu.VMEM((rows, 2 * half), f32),
            pltpu.SemaphoreType.DMA((5,)),
        ],
        compiler_params=pltpu.CompilerParams(vmem_limit_bytes=20 * MIB),
        cost_estimate=pl.CostEstimate(flops=2 * rows * width * 2 * half, bytes_accessed=2 * rows * width, transcendentals=0),
        name="project_kv",
    )(*[far(x) for x in (ids, w_key.T, w_value.T, fine, coarse)], near(tokens))


def q_body(tok, weight, tables, *refs):
    outs = refs[:2]
    acc = refs[2]
    rows = tok.shape[0]
    subs = rows // LANES
    per_out = subs // len(outs)
    heads = weight.shape[1] // HD
    acc[...] = jnp.dot(tok[...], weight[...], preferred_element_type=f32)
    even = lax.broadcasted_iota(i32, (LANES, LANES), 1) % 2 == 0
    upper = lax.axis_index("tp") % 2 == 1
    scale = HD ** (-0.5) * math.log2(math.e)
    for sub in range(subs):
        at = slice(sub * LANES, (sub + 1) * LANES)
        cos = tables[0, at, :] * scale
        sin = tables[1, at, :] * scale
        out = outs[sub // per_out]
        row = (sub % per_out) * LANES
        for h in range(heads):
            x = acc[at, h * HD : (h + 1) * HD]
            x = x * cos + pair_swap(x, even) * sin
            x = jnp.where(upper, pltpu.roll(x, HD // 2, 1), x)
            out[row : row + LANES, h * HD : (h + 1) * HD] = x.astype(bf16)


def project_q(tokens, w_query, tables):
    rows, width = tokens.shape
    cols = w_query.shape[1]
    whole = pl.BlockSpec(memory_space=pltpu.VMEM)
    out = jax.ShapeDtypeStruct((rows // 2, cols), bf16)
    return pl.pallas_call(
        q_body,
        in_specs=[whole] * 3,
        out_specs=[whole, whole],
        out_shape=[out, out],
        scratch_shapes=[pltpu.VMEM((rows, cols), f32)],
        compiler_params=pltpu.CompilerParams(vmem_limit_bytes=20 * MIB),
        cost_estimate=pl.CostEstimate(flops=2 * rows * width * cols, bytes_accessed=2 * rows * width + 2 * width * cols, transcendentals=0),
        name="project_q",
    )(near(tokens), near(w_query), near(tables))


def cent_body(chunks, groups, place, owner_counts, gain_in, cent_in, *refs):
    wide, norms, picked, gain, chosen, hit, match = refs[:7]
    cent, wide_buf, in_sems, out_sems = refs[7:]
    rows, feat = cent.shape
    size = rows // chunks
    block = norms.shape[1]
    loads = stream(cent_in, cent, in_sems, chunks, 0)
    stores = []
    for i in range(chunks):
        at = pl.ds(i * size, size)
        stores.append(pltpu.make_async_copy(wide_buf.at[at, :], wide.at[at, :], out_sems.at[i]))
    for c in loads:
        c.start()
    gain[...] = gain_in[...]
    slots = hit.shape[0]
    seg_total = chosen.shape[1]
    rank = lax.axis_index("tp")
    slot = lax.broadcasted_iota(i32, (slots, seg_total), 0)
    column = lax.broadcasted_iota(i32, (slots, seg_total), 1)
    for k in range(2):
        for m in range(groups):
            start, number = owner_span(owner_counts, rank ^ (2 * m + k))
            row = (k * groups + m) * slots
            taken = (slot + start == column) & (slot < number)
            chosen[row : row + slots, :] = jnp.where(taken, 1.0, 0.0)
    start, number = owner_span(owner_counts, rank)
    slot = lax.broadcasted_iota(i32, (slots, LANES), 0)
    column = lax.broadcasted_iota(i32, (slots, LANES), 1)
    hit[...] = jnp.where((slot + start == column) & (slot < number), 1.0, 0.0)
    third = lax.broadcasted_iota(i32, (1, match.shape[1]), 1) % seg_total
    assigned = jnp.zeros((1, match.shape[1]), i32)
    for r in range(seg_total):
        assigned = jnp.where(third == r, place[3, r], assigned)
    member = lax.broadcasted_iota(i32, (GROUP, match.shape[1]), 0)
    for r in range(seg_total):
        same = jnp.where(assigned == member + place[1, r], 1.0, 0.0)
        match[r * GROUP : (r + 1) * GROUP, :] = same.astype(bf16)

    def widen(b, carry):
        at = pl.ds(pl.multiple_of(b * block, block), block)
        c = cent[at, :].astype(f32)
        wide_buf[at, :] = c
        square = c * c
        part = square[:, :LANES]
        for g in range(1, feat // LANES):
            part = part + square[:, g * LANES : (g + 1) * LANES]
        norms[pl.ds(b, 1), :] = jnp.sum(part.T, axis=0, keepdims=True)
        return carry

    per_chunk = size // block
    for i in range(chunks):
        loads[i].wait()
        lax.fori_loop(i * per_chunk, (i + 1) * per_chunk, widen, 0)
        stores[i].start()
    for r in range(seg_total):
        first = pl.multiple_of(place[0, r], GROUP)
        picked[r * GROUP : (r + 1) * GROUP, :] = cent[pl.ds(first, GROUP), :]
    for c in stores:
        c.wait()


def widen_centroids(place, owner_counts, gain, centroids, groups, slots):
    rows, feat = centroids.shape
    count = place.shape[1]
    chunks = 4
    whole = pl.BlockSpec(memory_space=pltpu.VMEM)
    scalar = pl.BlockSpec(memory_space=pltpu.SMEM)
    in_hbm = pl.BlockSpec(memory_space=pltpu.HBM)

    def body(*refs):
        cent_body(chunks, groups, *refs)

    return pl.pallas_call(
        body,
        in_specs=[scalar, scalar, whole, in_hbm],
        out_specs=[in_hbm] + [whole] * 6,
        out_shape=[
            jax.ShapeDtypeStruct((rows, feat), f32),
            jax.ShapeDtypeStruct((8, rows // 8), f32),
            jax.ShapeDtypeStruct((count * GROUP, feat), bf16),
            jax.ShapeDtypeStruct((1, feat), f32),
            jax.ShapeDtypeStruct((2 * groups * slots, count), f32),
            jax.ShapeDtypeStruct((slots, LANES), f32),
            jax.ShapeDtypeStruct((count * GROUP, 3 * count), bf16),
        ],
        scratch_shapes=[
            pltpu.VMEM((rows, feat), bf16),
            pltpu.VMEM((rows, feat), f32),
            pltpu.SemaphoreType.DMA((chunks,)),
            pltpu.SemaphoreType.DMA((chunks,)),
        ],
        compiler_params=pltpu.CompilerParams(vmem_limit_bytes=24 * MIB),
        cost_estimate=pl.CostEstimate(flops=4 * rows * feat, bytes_accessed=6 * rows * feat, transcendentals=0),
        name="widen_centroids",
    )(place, owner_counts, gain, far(centroids))


def segment_starts(ids):
    rows = ids.shape[0]
    row = lax.broadcasted_iota(i32, ids.shape, 0)
    lane = lax.broadcasted_iota(i32, ids.shape, 1)
    left = pltpu.roll(ids, 1, 1)
    left = jnp.where(lane == 0, pltpu.roll(left, 1, 0), left)
    token = row * LANES + lane
    first = jnp.where((ids != left) & (token > 0), token, 0)
    shift = 1
    while shift < LANES:
        first = jnp.maximum(first, jnp.where(lane >= shift, pltpu.roll(first, shift, 1), 0))
        shift = shift * 2
    above = jnp.broadcast_to(jnp.max(first, axis=1, keepdims=True), ids.shape)
    above = jnp.where(row >= 1, pltpu.roll(above, 1, 0), 0)
    shift = 1
    while shift < rows:
        above = jnp.maximum(above, jnp.where(row >= shift, pltpu.roll(above, shift, 0), 0))
        shift = shift * 2
    return jnp.maximum(first, above)


def attend_body(pieces, seg_total, balanced, seg, ids, *refs):
    queries = refs[: 3 if balanced else 2]
    refs = refs[len(queries) :]
    own_in = refs[:pieces]
    other_in = refs[pieces : 2 * pieces]
    out, counts, tokens_out, tails, q_all, kv, starts, weights, tops, col, lhs, sems = refs[
        2 * pieces :
    ]
    q_rows, q_cols = queries[0].shape
    rows = own_in[0].shape[0] - tails.shape[1]
    heads = q_cols // HD
    half = HD // 2
    seq_len = kv.shape[0]
    wide = heads * QB
    own_blocks = rows // QB
    rank = lax.axis_index("seq")
    upper = lax.axis_index("tp") % 2 == 1

    copies = []
    for k, source in enumerate(queries):
        target = q_all.at[pl.ds(k * q_rows, q_rows), :]
        copies.append(pltpu.make_async_copy(source, target, sems.at[len(copies)]))
    for k, sources in enumerate((own_in, other_in)):
        for m in range(pieces):
            row0 = pl.multiple_of((rank ^ m) * rows, rows)
            place = kv.at[pl.ds(row0, rows), pl.ds(k * HD, HD)]
            source = sources[m].at[pl.ds(0, rows), :]
            copies.append(pltpu.make_async_copy(source, place, sems.at[len(copies)]))
    for m in range(pieces):
        source = own_in[m].at[pl.ds(rows, tails.shape[1]), :]
        copies.append(pltpu.make_async_copy(source, tails.at[m], sems.at[len(copies)]))
    for c in copies:
        c.start()
    col[...] = jnp.zeros(col.shape, f32)
    starts[...] = segment_starts(ids[...])
    for c in copies:
        c.wait()

    def q_step(n, carry):
        home = n < own_blocks
        base = jnp.where(home, rank, rank ^ 3) * rows + jnp.where(home, n, n - own_blocks) * QB
        base = pl.multiple_of(base, QB)
        last_seg = seg[base + QB - 1]
        first_seg = seg[base]
        clear_end = base // KB
        short = (base % KB + QB <= QB).astype(i32)
        begin = jnp.int32(0)
        clear = jnp.int32(0)
        for t in range(seq_len // KB):
            begin = begin + (seg[t * KB + KB - 1] < first_seg).astype(i32)
            outside = (seg[t * KB] != last_seg) | (base + QB - 1 - t * KB >= WINDOW)
            clear = clear + (outside & (t < clear_end)).astype(i32)
        begin = jnp.maximum(begin, jnp.maximum(base - (WINDOW - 1), 0) // KB)
        begin = jnp.minimum(begin, clear_end)
        clear = jnp.clip(clear, begin, clear_end)

        q_at = pl.ds(pl.multiple_of(n * QB, QB), QB)
        nothing = jnp.zeros((QB, half), bf16)
        q = []
        for h in range(heads):
            x = q_all[q_at, h * HD : (h + 1) * HD]
            q.append(jnp.concatenate([x[:, :half], nothing, x[:, half:], nothing], 1))
        low = [starts[pl.ds(base // LANES + g, 1), :] for g in range(QB // LANES)]
        low = jnp.concatenate(low, 1)
        i_pos = base + lax.broadcasted_iota(i32, (1, QB), 1)
        if seq_len > WINDOW:
            low = jnp.maximum(low, i_pos - (WINDOW - 1))

        def score(masked, size, kb, carry):
            start = pl.multiple_of(kb * KB, KB)
            rows_kb = kv[pl.ds(start, size), :]
            if masked:
                j_pos = start + lax.broadcasted_iota(i32, (size, QB), 0)
                allowed = (j_pos <= i_pos) & (j_pos >= low)
            result = []
            for h in range(heads):
                top, total = carry[h]
                lanes = slice(h * QB, (h + 1) * QB)
                s = lax.dot_general(
                    rows_kb, q[h], (((1,), (1,)), ((), ())), preferred_element_type=f32
                )
                if masked:
                    s = jnp.where(allowed, s, -1e30)
                new_top = jnp.maximum(top, jnp.max(s, axis=0, keepdims=True))
                p = jnp.exp2(s - new_top)
                weights[pl.ds(start, size), lanes] = p.astype(bf16)
                tops[pl.ds(kb, 1), lanes] = new_top
                p = jnp.sum(p.reshape(size // 8, 8, QB), axis=0)
                result.append((new_top, total * jnp.exp2(top - new_top) + p))
            return tuple(result)

        state = (jnp.full((1, QB), -1e30, f32), jnp.zeros((8, QB), f32))
        state = (state,) * heads
        pairs = (clear_end - clear) // 2
        single = clear + 2 * pairs
        state = lax.fori_loop(begin, clear, lambda kb, c: score(True, KB, kb, c), state)
        state = lax.fori_loop(
            0, pairs, lambda t, c: score(False, 2 * KB, clear + 2 * t, c), state
        )
        state = lax.fori_loop(single, clear_end, lambda kb, c: score(False, KB, kb, c), state)
        state = lax.fori_loop(0, short, lambda t, c: score(True, QB, clear_end, c), state)
        state = lax.fori_loop(short, 1, lambda t, c: score(True, KB, clear_end, c), state)
        top = jnp.concatenate([t for t, _ in state], 1)
        total = jnp.concatenate([t for _, t in state], 1)
        share = 1.0 / jnp.sum(total, axis=0, keepdims=True)
        row = lax.broadcasted_iota(i32, (16, wide), 0)
        head = lax.broadcasted_iota(i32, (16, wide), 1) // QB

        def gather(size, kb, carry):
            start = pl.multiple_of(kb * KB, KB)
            r = share * jnp.exp2(tops[pl.ds(kb, 1), :] - top)
            high = r.astype(bf16).astype(f32)
            r = jnp.where(row == head, high, jnp.where(row == heads + head, r - high, 0.0))
            at = pl.ds(start, size)
            contract = (((1,), (1,)), ((), ()))
            w = weights[at, :]
            r = r.astype(bf16)
            if COLUMNS_AS_ROWS:
                add = lax.dot_general(r, w, contract, preferred_element_type=f32)
                col[:16, at] = col[:16, at] + add
            else:
                add = lax.dot_general(w, r, contract, preferred_element_type=f32)
                col[at, :16] = col[at, :16] + add
            return carry

        lax.fori_loop(begin, clear, lambda kb, c: gather(KB, kb, c), 0)
        lax.fori_loop(0, pairs, lambda t, c: gather(2 * KB, clear + 2 * t, c), 0)
        lax.fori_loop(single, clear_end, lambda kb, c: gather(KB, kb, c), 0)
        lax.fori_loop(0, short, lambda t, c: gather(QB, clear_end, c), 0)
        lax.fori_loop(short, 1, lambda t, c: gather(KB, clear_end, c), 0)
        return carry

    if balanced:
        low_n = jnp.where(rank == 3, 2, jnp.where(rank == 2, 1, 0))
        high_n = own_blocks + jnp.where(rank == 0, 2, jnp.where(rank == 1, 1, 0))
    else:
        low_n = 0
        high_n = own_blocks
    lax.fori_loop(low_n, high_n, q_step, 0)

    number = jnp.zeros((seg_total, LANES), f32)
    for g in range(seq_len // LANES):
        at = slice(g * LANES, (g + 1) * LANES)
        member = ids[g : g + 1, :] == lax.broadcasted_iota(i32, (seg_total, LANES), 0)
        number = number + member.astype(f32)
        turned = col[:16, at] if COLUMNS_AS_ROWS else col[at, :].T
        for h in range(heads):
            w = turned[h : h + 1] + turned[heads + h : heads + h + 1]
            w = jnp.where(member, w, 0.0)
            high = w.astype(bf16)
            lhs[h * seg_total : (h + 1) * seg_total, at] = high
            rest = (w - high.astype(f32)).astype(bf16)
            lhs[(heads + h) * seg_total : (heads + h + 1) * seg_total, at] = rest
    parts = tokens_out.shape[1] // LANES
    for g in range(parts):
        sums = jnp.zeros((seg_total, LANES), f32)
        for m in range(pieces):
            for first in (g * seg_total, (parts + g) * seg_total):
                sums = sums + tails[m, first : first + seg_total, :].astype(f32)
        tokens_out[:, g * LANES : (g + 1) * LANES] = sums
    counts[...] = jnp.broadcast_to(jnp.sum(number, axis=1, keepdims=True), counts.shape)
    pooled = jnp.dot(lhs[...], kv[...], preferred_element_type=f32)
    pooled = jnp.concatenate([pooled[:, half:HD], pooled[:, HD + half :]], 1)
    for h in range(heads):
        x = pooled[h * seg_total : (h + 1) * seg_total]
        x = x + pooled[(heads + h) * seg_total : (heads + h + 1) * seg_total]
        out[:, h * HD : (h + 1) * HD] = jnp.where(upper, pltpu.roll(x, half, 1), x)


def attend(seg_ids, ids, queries, own, other, feat, seg_total, balanced):
    q_rows, cols = queries[0].shape
    tail = 2 * seg_total * feat // LANES
    seq_len = seg_ids.shape[0]
    pieces = len(own)
    heads = cols // HD
    whole = pl.BlockSpec(memory_space=pltpu.VMEM)
    anywhere = pl.BlockSpec(memory_space=pl.ANY)
    inputs = len(queries) + 2 * pieces

    def body(*refs):
        attend_body(pieces, seg_total, balanced, *refs)

    return pl.pallas_call(
        body,
        in_specs=[pl.BlockSpec(memory_space=pltpu.SMEM), whole]
        + [anywhere] * inputs,
        out_specs=[whole, whole, whole],
        out_shape=[
            jax.ShapeDtypeStruct((seg_total, cols), f32),
            jax.ShapeDtypeStruct((seg_total, LANES), f32),
            jax.ShapeDtypeStruct((seg_total, feat), f32),
        ],
        scratch_shapes=[
            pltpu.VMEM((pieces, tail, HD), bf16),
            pltpu.VMEM((len(queries) * q_rows, cols), bf16),
            pltpu.VMEM((seq_len, 2 * HD), bf16),
            pltpu.VMEM((seq_len // LANES, LANES), i32),
            pltpu.VMEM((seq_len, heads * QB), bf16),
            pltpu.VMEM((max(8, seq_len // KB), heads * QB), f32),
            pltpu.VMEM((16, seq_len) if COLUMNS_AS_ROWS else (seq_len, LANES), f32),
            pltpu.VMEM((2 * heads * seg_total, seq_len), bf16),
            pltpu.SemaphoreType.DMA((inputs + pieces,)),
        ],
        compiler_params=pltpu.CompilerParams(vmem_limit_bytes=24 * MIB),
        cost_estimate=pl.CostEstimate(flops=8 * q_rows * cols * seq_len, bytes_accessed=4 * seq_len * HD, transcendentals=0),
        name="attend",
    )(seg_ids, ids, *queries, *own, *other)


def mix_body(pieces, *refs):
    parts = refs[:pieces]
    norms, w_out, keep, send = refs[pieces:]
    groups, _, feat = keep.shape
    seg_total = parts[0].shape[0]
    mixed = parts[0][...]
    for p in parts[1:]:
        mixed = mixed + p[...]
    high = mixed.astype(bf16)
    low = (mixed - high.astype(f32)).astype(bf16)
    lhs = jnp.concatenate([high, low], 0)
    rank = lax.axis_index("tp")
    for k, target in enumerate((keep, send)):
        for m in range(groups):
            owner = rank ^ (2 * m + k)
            cols = pl.ds(pl.multiple_of(owner * feat, feat), feat)
            y = jnp.dot(lhs, w_out[:, cols], preferred_element_type=f32)
            target[m, :seg_total, :] = y[:seg_total] + y[seg_total:]
            target[m, seg_total:, :] = norms[...]


def mix(parts, norms, w_out, feat, groups):
    seg_total = parts[0].shape[0]
    whole = pl.BlockSpec(memory_space=pltpu.VMEM)
    out = jax.ShapeDtypeStruct((groups, seg_total + 8, feat), f32)

    def body(*refs):
        mix_body(len(parts), *refs)

    return pl.pallas_call(
        body,
        in_specs=[whole] * (len(parts) + 2),
        out_specs=[whole, whole],
        out_shape=[out, out],
        compiler_params=pltpu.CompilerParams(vmem_limit_bytes=16 * MIB),
        name="mix",
    )(*parts, norms, w_out)


def fold_body(groups, edge, keep, received, own, *sends):
    _, rows, cols = keep.shape
    own[...] = keep[0] + received[0]
    for m in range(1, groups):
        total = keep[m] + received[m]
        target = sends[m - 1]
        if edge == "rows":
            inner = rows - 8
            last = total[inner:]
            high = last.astype(bf16).astype(f32)
            target[:inner, :] = total[:inner].astype(bf16)
            target[inner:, :] = jnp.concatenate([high, last - high], 0).astype(bf16)
        else:
            inner = cols - LANES
            last = total[:, inner:]
            high = last.astype(bf16)
            target[:, :inner] = total[:, :inner].astype(bf16)
            target[:, inner:cols] = high
            target[:, cols:] = (last - high.astype(f32)).astype(bf16)


def fold(keep, received, edge):
    groups, rows, cols = keep.shape
    whole = pl.BlockSpec(memory_space=pltpu.VMEM)
    shape = (rows + 8, cols) if edge == "rows" else (rows, cols + LANES)

    def body(*refs):
        fold_body(groups, edge, *refs)

    result = pl.pallas_call(
        body,
        in_specs=[whole, whole],
        out_specs=[whole] * groups,
        out_shape=[jax.ShapeDtypeStruct((rows, cols), f32)]
        + [jax.ShapeDtypeStruct(shape, bf16)] * (groups - 1),
        compiler_params=pltpu.CompilerParams(vmem_limit_bytes=12 * MIB),
        name="fold",
    )(keep, received)
    return [result[0]] + [swapped(result[m], "tp", 2 * m) for m in range(1, groups)]


def owner_span(owner_counts, owner):
    start = jnp.int32(0)
    for o in range(owner_counts.shape[0]):
        start = start + jnp.where(o < owner, owner_counts[o], 0)
    return start, owner_counts[owner]


def cross_body(groups, chunks, model_width, *refs):
    mixed = refs[:groups]
    token_sums, counts, gain, chosen, cent = refs[groups : groups + 5]
    keep, send, emb, norms, lhs = refs[groups + 5 :]
    seg_total, feat = emb.shape
    rows = cent.shape[0]
    slots = keep.shape[1]
    per_side = groups * slots

    total = mixed[0][:seg_total, :] + token_sums[...]
    square = mixed[0][seg_total:, :]
    for p in mixed[1:]:
        total = total + p[:seg_total, :].astype(f32)
        terms = p[seg_total:, :].astype(f32)
        square = square + (terms[:8] + terms[8:])
    norms[...] = square
    pooled = total / counts[:, :1]
    square = jnp.sum(pooled * pooled, axis=1, keepdims=True)
    row = lax.broadcasted_iota(i32, (seg_total, LANES), 0)
    lane = lax.broadcasted_iota(i32, (seg_total, LANES), 1)
    square = jnp.sum(jnp.where(row == lane, square, 0.0), axis=0, keepdims=True)
    square = jnp.broadcast_to(square, (slots, LANES))
    scaled = pooled * gain[...]
    emb[...] = scaled
    high = scaled.astype(bf16)
    low = (scaled - high.astype(f32)).astype(bf16)
    picks = chosen[...].astype(bf16)
    factor = -2.0 / model_width**0.5
    lhs[: 2 * per_side] = (jnp.dot(picks, high, preferred_element_type=f32) * factor).astype(bf16)
    lhs[2 * per_side :] = (jnp.dot(picks, low, preferred_element_type=f32) * factor).astype(bf16)
    for target in (keep, send):
        for m in range(groups):
            target[m, :, rows:] = square

    size = rows // chunks
    for i in range(chunks):
        at = slice(i * size, (i + 1) * size)
        y = lax.dot_general(
            cent[at, :], lhs[...], (((1,), (1,)), ((), ())), preferred_element_type=f32
        ).T
        y = y[: 2 * per_side] + y[2 * per_side :]
        for k, target in enumerate((keep, send)):
            for m in range(groups):
                first = k * per_side + m * slots
                target[m, :, at] = y[first : first + slots]


def cross(mixed, token_sums, counts, gain, chosen, centroids, slots, model_width):
    rows, feat = centroids.shape
    groups = len(mixed)
    seg_total = counts.shape[0]
    whole = pl.BlockSpec(memory_space=pltpu.VMEM)
    side = jax.ShapeDtypeStruct((groups, slots, rows + LANES), f32)

    def body(*refs):
        cross_body(groups, 4, model_width, *refs)

    return pl.pallas_call(
        body,
        in_specs=[whole] * (groups + 5),
        out_specs=[whole] * 4,
        out_shape=[
            side,
            side,
            jax.ShapeDtypeStruct((seg_total, feat), f32),
            jax.ShapeDtypeStruct((8, rows // 8), f32),
        ],
        scratch_shapes=[pltpu.VMEM((4 * groups * slots, feat), bf16)],
        compiler_params=pltpu.CompilerParams(vmem_limit_bytes=16 * MIB),
        name="cross",
    )(*mixed, token_sums, counts, gain, chosen, centroids)


def finish_body(groups, model_width, place, *refs):
    terms = refs[:groups]
    norms, emb, hit, match, picked, wide_in, dist, wide, moved, sems = refs[groups:]
    seg_total, feat = emb.shape
    block = norms.shape[1]
    rows = dist.shape[1]
    total = terms[0][:, rows:]
    for t in terms[1:]:
        total = total + t[:, rows : rows + LANES].astype(f32)
        total = total + t[:, rows + LANES :].astype(f32)
    scale = lax.rsqrt(total / model_width + norm_eps)

    spread = jnp.broadcast_to(scale[:1], (seg_total, LANES))
    r_row = lax.broadcasted_iota(i32, (seg_total, LANES), 0)
    r_lane = lax.broadcasted_iota(i32, (seg_total, LANES), 1)
    row_scale = jnp.sum(jnp.where(r_row == r_lane, spread, 0.0), axis=1, keepdims=True)
    value = emb[...] * row_scale
    high = value.astype(bf16)
    rest = value - high.astype(f32)
    middle = rest.astype(bf16)
    low = (rest - middle.astype(f32)).astype(bf16)
    stacked = jnp.concatenate([high, middle, low], 0)
    once = lax.broadcasted_iota(i32, (3 * seg_total, LANES), 0) < seg_total
    stacked = jnp.concatenate([stacked, jnp.where(once, 1.0, 0.0).astype(bf16)], 1)
    added = jnp.dot(match[...], stacked, preferred_element_type=f32)
    shrink = 1.0 / (1.0 + added[:, feat:])
    for g in range(feat // LANES):
        at = slice(g * LANES, (g + 1) * LANES)
        moved[:, at] = (picked[:, at].astype(f32) + added[:, at]) * shrink

    def write(r):
        first = pl.multiple_of(place[0, r], GROUP)
        return pltpu.make_async_copy(
            moved.at[pl.ds(r * GROUP, GROUP), :], wide.at[pl.ds(first, GROUP), :], sems.at[r]
        )

    for r in range(seg_total):
        pl.when(place[2, r] == 1)(lambda r=r: write(r).start())

    own_scale = jnp.sum(hit[...] * scale, axis=1, keepdims=True)
    valid = jnp.sum(hit[...], axis=1, keepdims=True) > 0.0
    for g in range(rows // block):
        at = slice(g * block, (g + 1) * block)
        y = terms[0][:, at]
        for t in terms[1:]:
            y = y + t[:, at].astype(f32)
        y = norms[g : g + 1, :] * (1.0 / model_width**0.5) + y * own_scale
        dist[:, at] = jnp.where(valid, y, 0.0)

    for r in range(seg_total):
        pl.when(place[2, r] == 1)(lambda r=r: write(r).wait())


def finish(place, terms, norms, emb, hit, match, picked, wide, model_width):
    groups = len(terms)
    seg_total = emb.shape[0]
    slots, rows = terms[0].shape
    rows = rows - LANES
    whole = pl.BlockSpec(memory_space=pltpu.VMEM)
    in_hbm = pl.BlockSpec(memory_space=pltpu.HBM)
    scalar = pl.BlockSpec(memory_space=pltpu.SMEM)

    def body(*refs):
        finish_body(groups, model_width, *refs)

    return pl.pallas_call(
        body,
        in_specs=[scalar] + [whole] * (groups + 5) + [in_hbm],
        out_specs=[whole, in_hbm],
        out_shape=[
            jax.ShapeDtypeStruct((slots, rows), f32),
            jax.ShapeDtypeStruct(wide.shape, f32),
        ],
        scratch_shapes=[
            pltpu.VMEM((seg_total * GROUP, emb.shape[1]), f32),
            pltpu.SemaphoreType.DMA((seg_total,)),
        ],
        input_output_aliases={1 + groups + 5: 1},
        compiler_params=pltpu.CompilerParams(vmem_limit_bytes=16 * MIB),
        name="finish",
    )(place, *terms, norms, emb, hit, match, picked, wide)


def shards(
    tokens, w_query, w_key, w_value, w_out, seg_ids, owner_counts, centroids, pool_gain, assign
):
    tok_rows, model_width = tokens.shape
    seq_len = seg_ids.shape[0]
    seg_total = assign.shape[0]
    rank_seq = lax.axis_index("seq")
    seq_total = lax.axis_size("seq")
    tp_total = lax.axis_size("tp")
    groups = tp_total // 2
    feat = model_width // tp_total
    cent_rows = centroids.shape[0]
    slots = 2 * seg_total // owner_counts.shape[0]
    fine_np, coarse_np = angle_tables(seq_len)
    fine = jnp.asarray(fine_np)
    coarse = jnp.asarray(coarse_np)

    ids = seg_ids.reshape(seq_len // LANES, LANES)
    masks = range(1, seq_total)

    own, tables = project_kv(
        tokens, w_key, w_value, fine, coarse, ids, seg_total, model_width // tp_total
    )
    own = [own] + [swapped(own, "seq", m) for m in masks]
    other = [swapped(x, "tp", 1) for x in own]

    queries = list(project_q(tokens, w_query, tables))
    balanced = seq_total == 4 and seq_len <= WINDOW and tok_rows == 4 * QB
    if balanced:
        queries = queries + [lax.ppermute(queries[0], "seq", [(3, 0), (2, 1)])]

    local = assign - rank_seq * cent_rows
    mine = (local >= 0) & (local < cent_rows)
    first_row = jnp.where(mine, local // GROUP * GROUP, 0)
    line = assign // GROUP
    order = jnp.arange(seg_total, dtype=i32)
    repeat = jnp.any((line[:, None] == line[None, :]) & (order[None, :] < order[:, None]), axis=1)
    place = jnp.stack([first_row, line * GROUP, (mine & ~repeat).astype(i32), assign])
    wide, norms, picked, gain, chosen, hit, match = widen_centroids(
        place, owner_counts, pool_gain.reshape(1, feat), centroids, groups, slots
    )

    queries, wide, norms, picked, gain, chosen, hit, match = lax.optimization_barrier(
        (queries, wide, norms, picked, gain, chosen, hit, match)
    )
    attended, counts, token_sums = attend(
        seg_ids, ids, queries, own, other, feat, seg_total, balanced
    )
    attended = [attended] + [swapped(attended, "seq", m) for m in masks]

    keep, send = mix(attended, norms, w_out, feat, groups)
    mixed = fold(keep, swapped(send, "tp", 1), "rows")

    keep, send, emb, norms = cross(
        mixed, token_sums, counts, gain, chosen, centroids, slots, model_width
    )
    terms = fold(keep, swapped(send, "tp", 1), "columns")
    distances, updated = finish(
        place, terms, norms, emb, hit, match, picked, wide, model_width
    )
    return (distances, updated)


def solution(mesh):
    in_specs = (
        P("seq", None),
        P(None, "tp"),
        P(None, "tp"),
        P(None, "tp"),
        P("tp", None),
        P(),
        P(),
        P("seq", "tp"),
        P("tp"),
        P(),
    )
    out_specs = (P("tp", "seq"), P("seq", "tp"))
    return jax.shard_map(shards, mesh=mesh, in_specs=in_specs, out_specs=out_specs, check_vma=False)
```

```python
import math

import jax
import jax.numpy as jnp
import numpy as np
from jax import lax
from jax.experimental import pallas as pl
from jax.experimental.pallas import tpu as pltpu
from jax.sharding import PartitionSpec as P

HD = 128
WINDOW = 4096
QB = 256
KB = 512
LANES = 128
GROUP = 16
COLUMNS_AS_ROWS = True

rope_theta = 10000.0
norm_eps = 1e-06
MIB = 1024 * 1024

f32 = jnp.float32
bf16 = jnp.bfloat16
i32 = jnp.int32


def swapped(x, axis, mask):
    count = lax.axis_size(axis)
    return lax.ppermute(x, axis, [(i, i ^ mask) for i in range(count)])


def angle_tables(seq_len):
    inverse = np.exp(-(2.0 * np.arange(HD // 2) / HD) * math.log(rope_theta))
    inverse = np.repeat(inverse, 2)[None, :]
    fine = np.arange(LANES)[:, None] * inverse
    coarse = LANES * np.arange(seq_len // LANES)[:, None] * inverse
    fine_tab = np.stack([np.cos(fine), np.sin(fine)]).astype(np.float32)
    coarse_tab = np.stack([np.cos(coarse), np.sin(coarse)]).astype(np.float32)
    return fine_tab, coarse_tab


def turn(fine, coarse, which):
    ca = coarse[0, pl.ds(which, 1), :]
    sa = coarse[1, pl.ds(which, 1), :]
    cb = fine[0]
    sb = fine[1]
    return ca * cb - sa * sb, sa * cb + ca * sb


def pair_swap(x, even):
    up = pltpu.roll(x, x.shape[1] - 1, 1)
    down = pltpu.roll(x, 1, 1)
    return jnp.where(even, up, down)


def far(x):
    return pltpu.with_memory_space_constraint(x, pltpu.HBM)


def near(x):
    return pltpu.with_memory_space_constraint(x, pltpu.VMEM)


def stream(source, buffer, sems, chunks, axis):
    size = source.shape[axis] // chunks
    result = []
    for i in range(chunks):
        part = pl.ds(i * size, size)
        at = (part, slice(None)) if axis == 0 else (slice(None), part)
        result.append(pltpu.make_async_copy(source.at[at], buffer.at[at], sems.at[i]))
    return result


def kv_body(seg_total, *refs):
    ids_in, wk_in, wv_in, fine_in, coarse_in, tok = refs[:6]
    out, tables, key_tables, weight, ids, fine, coarse, acc, small = refs[6:]
    rows, _ = tok.shape
    half = wk_in.shape[0]
    subs = rows // LANES
    rest = [
        pltpu.make_async_copy(wk_in, weight.at[pl.ds(0, half), :], small.at[0]),
        pltpu.make_async_copy(wv_in, weight.at[pl.ds(half, half), :], small.at[1]),
        pltpu.make_async_copy(fine_in, fine, small.at[2]),
        pltpu.make_async_copy(coarse_in, coarse, small.at[3]),
        pltpu.make_async_copy(ids_in, ids, small.at[4]),
    ]
    for c in rest:
        c.start()
    for c in rest:
        c.wait()
    lane = lax.broadcasted_iota(i32, (LANES, LANES), 1)
    even = lane % 2 == 0
    upper = lax.axis_index("tp") % 2 == 1
    first = lax.axis_index("seq") * subs
    members = []
    for sub in range(subs):
        at = slice(sub * LANES, (sub + 1) * LANES)
        cos, sin = turn(fine, coarse, first + sub)
        sin = jnp.where(even, -sin, sin)
        tables[0, at, :] = cos
        tables[1, at, :] = sin
        cos = jnp.where(upper, pltpu.roll(cos, half, 1), cos)
        sin = jnp.where(upper, pltpu.roll(sin, half, 1), sin)
        key_tables[0, at, :] = jnp.where(lane < half, cos, 1.0)
        key_tables[1, at, :] = jnp.where(lane < half, sin, 0.0)
        member = ids[pl.ds(first + sub, 1), :] == lax.broadcasted_iota(i32, (seg_total, LANES), 0)
        members.append(jnp.where(member, 1.0, 0.0))
    acc[...] = lax.dot_general(
        tok[...], weight[...], (((1,), (1,)), ((), ())), preferred_element_type=f32
    )
    for sub in range(subs):
        at = slice(sub * LANES, (sub + 1) * LANES)
        x = acc[at]
        x = x * key_tables[0, at, :] + pair_swap(x, even) * key_tables[1, at, :]
        out[at, :] = x.astype(bf16)
    feat = (out.shape[0] - rows) // 2 // seg_total * LANES
    cols = pl.ds(pl.multiple_of(lax.axis_index("tp") * feat, feat), feat)
    member = jnp.concatenate(members, 1).astype(bf16)
    pooled = jnp.dot(member, tok[:, cols], preferred_element_type=f32)
    high = pooled.astype(bf16)
    low = (pooled - high.astype(f32)).astype(bf16)
    row = rows
    for part in (high, low):
        for g in range(feat // LANES):
            out[row : row + seg_total, :] = part[:, g * LANES : (g + 1) * LANES]
            row = row + seg_total


def project_kv(tokens, w_key, w_value, fine, coarse, ids, seg_total, feat):
    rows, width = tokens.shape
    half = w_key.shape[1]
    whole = pl.BlockSpec(memory_space=pltpu.VMEM)

    def body(*refs):
        kv_body(seg_total, *refs)

    return pl.pallas_call(
        body,
        in_specs=[pl.BlockSpec(memory_space=pltpu.HBM)] * 5 + [whole],
        out_specs=[whole] * 2,
        out_shape=[
            jax.ShapeDtypeStruct((rows + 2 * seg_total * feat // LANES, 2 * half), bf16),
            jax.ShapeDtypeStruct((2, rows, LANES), f32),
        ],
        scratch_shapes=[
            pltpu.VMEM((2, rows, LANES), f32),
            pltpu.VMEM((2 * half, width), bf16),
            pltpu.VMEM(ids.shape, i32),
            pltpu.VMEM(fine.shape, f32),
            pltpu.VMEM(coarse.shape, f32),
            pltpu.VMEM((rows, 2 * half), f32),
            pltpu.SemaphoreType.DMA((5,)),
        ],
        compiler_params=pltpu.CompilerParams(vmem_limit_bytes=20 * MIB),
        cost_estimate=pl.CostEstimate(flops=2 * rows * width * 2 * half, bytes_accessed=2 * rows * width, transcendentals=0),
        name="project_kv",
    )(*[far(x) for x in (ids, w_key.T, w_value.T, fine, coarse)], near(tokens))


def q_body(tok, weight, tables, *refs):
    outs = refs[:2]
    acc = refs[2]
    rows = tok.shape[0]
    subs = rows // LANES
    per_out = subs // len(outs)
    heads = weight.shape[1] // HD
    acc[...] = jnp.dot(tok[...], weight[...], preferred_element_type=f32)
    even = lax.broadcasted_iota(i32, (LANES, LANES), 1) % 2 == 0
    upper = lax.axis_index("tp") % 2 == 1
    scale = HD ** (-0.5) * math.log2(math.e)
    for sub in range(subs):
        at = slice(sub * LANES, (sub + 1) * LANES)
        cos = tables[0, at, :] * scale
        sin = tables[1, at, :] * scale
        out = outs[sub // per_out]
        row = (sub % per_out) * LANES
        for h in range(heads):
            x = acc[at, h * HD : (h + 1) * HD]
            x = x * cos + pair_swap(x, even) * sin
            x = jnp.where(upper, pltpu.roll(x, HD // 2, 1), x)
            out[row : row + LANES, h * HD : (h + 1) * HD] = x.astype(bf16)


def project_q(tokens, w_query, tables):
    rows, width = tokens.shape
    cols = w_query.shape[1]
    whole = pl.BlockSpec(memory_space=pltpu.VMEM)
    out = jax.ShapeDtypeStruct((rows // 2, cols), bf16)
    return pl.pallas_call(
        q_body,
        in_specs=[whole] * 3,
        out_specs=[whole, whole],
        out_shape=[out, out],
        scratch_shapes=[pltpu.VMEM((rows, cols), f32)],
        compiler_params=pltpu.CompilerParams(vmem_limit_bytes=20 * MIB),
        cost_estimate=pl.CostEstimate(flops=2 * rows * width * cols, bytes_accessed=2 * rows * width + 2 * width * cols, transcendentals=0),
        name="project_q",
    )(near(tokens), near(w_query), near(tables))


def cent_body(chunks, groups, place, owner_counts, gain_in, cent_in, *refs):
    wide, norms, picked, gain, chosen, hit, match = refs[:7]
    cent, wide_buf, in_sems, out_sems = refs[7:]
    rows, feat = cent.shape
    size = rows // chunks
    block = norms.shape[1]
    loads = stream(cent_in, cent, in_sems, chunks, 0)
    stores = []
    for i in range(chunks):
        at = pl.ds(i * size, size)
        stores.append(pltpu.make_async_copy(wide_buf.at[at, :], wide.at[at, :], out_sems.at[i]))
    for c in loads:
        c.start()
    gain[...] = gain_in[...]
    slots = hit.shape[0]
    seg_total = chosen.shape[1]
    rank = lax.axis_index("tp")
    slot = lax.broadcasted_iota(i32, (slots, seg_total), 0)
    column = lax.broadcasted_iota(i32, (slots, seg_total), 1)
    for k in range(2):
        for m in range(groups):
            start, number = owner_span(owner_counts, rank ^ (2 * m + k))
            row = (k * groups + m) * slots
            taken = (slot + start == column) & (slot < number)
            chosen[row : row + slots, :] = jnp.where(taken, 1.0, 0.0)
    start, number = owner_span(owner_counts, rank)
    slot = lax.broadcasted_iota(i32, (slots, LANES), 0)
    column = lax.broadcasted_iota(i32, (slots, LANES), 1)
    hit[...] = jnp.where((slot + start == column) & (slot < number), 1.0, 0.0)
    third = lax.broadcasted_iota(i32, (1, match.shape[1]), 1) % seg_total
    assigned = jnp.zeros((1, match.shape[1]), i32)
    for r in range(seg_total):
        assigned = jnp.where(third == r, place[3, r], assigned)
    member = lax.broadcasted_iota(i32, (GROUP, match.shape[1]), 0)
    for r in range(seg_total):
        same = jnp.where(assigned == member + place[1, r], 1.0, 0.0)
        match[r * GROUP : (r + 1) * GROUP, :] = same.astype(bf16)

    def widen(b, carry):
        at = pl.ds(pl.multiple_of(b * block, block), block)
        c = cent[at, :].astype(f32)
        wide_buf[at, :] = c
        square = c * c
        part = square[:, :LANES]
        for g in range(1, feat // LANES):
            part = part + square[:, g * LANES : (g + 1) * LANES]
        norms[pl.ds(b, 1), :] = jnp.sum(part.T, axis=0, keepdims=True)
        return carry

    per_chunk = size // block
    for i in range(chunks):
        loads[i].wait()
        lax.fori_loop(i * per_chunk, (i + 1) * per_chunk, widen, 0)
        stores[i].start()
    for r in range(seg_total):
        first = pl.multiple_of(place[0, r], GROUP)
        picked[r * GROUP : (r + 1) * GROUP, :] = cent[pl.ds(first, GROUP), :]
    for c in stores:
        c.wait()


def widen_centroids(place, owner_counts, gain, centroids, groups, slots):
    rows, feat = centroids.shape
    count = place.shape[1]
    chunks = 8
    whole = pl.BlockSpec(memory_space=pltpu.VMEM)
    scalar = pl.BlockSpec(memory_space=pltpu.SMEM)
    in_hbm = pl.BlockSpec(memory_space=pltpu.HBM)

    def body(*refs):
        cent_body(chunks, groups, *refs)

    return pl.pallas_call(
        body,
        in_specs=[scalar, scalar, whole, in_hbm],
        out_specs=[in_hbm] + [whole] * 6,
        out_shape=[
            jax.ShapeDtypeStruct((rows, feat), f32),
            jax.ShapeDtypeStruct((8, rows // 8), f32),
            jax.ShapeDtypeStruct((count * GROUP, feat), bf16),
            jax.ShapeDtypeStruct((1, feat), f32),
            jax.ShapeDtypeStruct((2 * groups * slots, count), f32),
            jax.ShapeDtypeStruct((slots, LANES), f32),
            jax.ShapeDtypeStruct((count * GROUP, 3 * count), bf16),
        ],
        scratch_shapes=[
            pltpu.VMEM((rows, feat), bf16),
            pltpu.VMEM((rows, feat), f32),
            pltpu.SemaphoreType.DMA((chunks,)),
            pltpu.SemaphoreType.DMA((chunks,)),
        ],
        compiler_params=pltpu.CompilerParams(vmem_limit_bytes=24 * MIB),
        cost_estimate=pl.CostEstimate(flops=4 * rows * feat, bytes_accessed=6 * rows * feat, transcendentals=0),
        name="widen_centroids",
    )(place, owner_counts, gain, far(centroids))


def segment_starts(ids):
    rows = ids.shape[0]
    row = lax.broadcasted_iota(i32, ids.shape, 0)
    lane = lax.broadcasted_iota(i32, ids.shape, 1)
    left = pltpu.roll(ids, 1, 1)
    left = jnp.where(lane == 0, pltpu.roll(left, 1, 0), left)
    token = row * LANES + lane
    first = jnp.where((ids != left) & (token > 0), token, 0)
    shift = 1
    while shift < LANES:
        first = jnp.maximum(first, jnp.where(lane >= shift, pltpu.roll(first, shift, 1), 0))
        shift = shift * 2
    above = jnp.broadcast_to(jnp.max(first, axis=1, keepdims=True), ids.shape)
    above = jnp.where(row >= 1, pltpu.roll(above, 1, 0), 0)
    shift = 1
    while shift < rows:
        above = jnp.maximum(above, jnp.where(row >= shift, pltpu.roll(above, shift, 0), 0))
        shift = shift * 2
    return jnp.maximum(first, above)


def attend_body(pieces, seg_total, balanced, seg, ids, *refs):
    queries = refs[: 3 if balanced else 2]
    refs = refs[len(queries) :]
    own_in = refs[:pieces]
    other_in = refs[pieces : 2 * pieces]
    out, counts, tokens_out, tails, q_all, kv, starts, weights, tops, col, lhs, sems = refs[
        2 * pieces :
    ]
    q_rows, q_cols = queries[0].shape
    rows = own_in[0].shape[0] - tails.shape[1]
    heads = q_cols // HD
    half = HD // 2
    seq_len = kv.shape[0]
    wide = heads * QB
    own_blocks = rows // QB
    rank = lax.axis_index("seq")
    upper = lax.axis_index("tp") % 2 == 1

    copies = []
    for k, source in enumerate(queries):
        target = q_all.at[pl.ds(k * q_rows, q_rows), :]
        copies.append(pltpu.make_async_copy(source, target, sems.at[len(copies)]))
    for k, sources in enumerate((own_in, other_in)):
        for m in range(pieces):
            row0 = pl.multiple_of((rank ^ m) * rows, rows)
            place = kv.at[pl.ds(row0, rows), pl.ds(k * HD, HD)]
            source = sources[m].at[pl.ds(0, rows), :]
            copies.append(pltpu.make_async_copy(source, place, sems.at[len(copies)]))
    for m in range(pieces):
        source = own_in[m].at[pl.ds(rows, tails.shape[1]), :]
        copies.append(pltpu.make_async_copy(source, tails.at[m], sems.at[len(copies)]))
    for c in copies:
        c.start()
    col[...] = jnp.zeros(col.shape, f32)
    starts[...] = segment_starts(ids[...])
    for c in copies:
        c.wait()

    def q_step(n, carry):
        home = n < own_blocks
        base = jnp.where(home, rank, rank ^ 3) * rows + jnp.where(home, n, n - own_blocks) * QB
        base = pl.multiple_of(base, QB)
        last_seg = seg[base + QB - 1]
        first_seg = seg[base]
        clear_end = base // KB
        short = (base % KB + QB <= QB).astype(i32)
        begin = jnp.int32(0)
        clear = jnp.int32(0)
        for t in range(seq_len // KB):
            begin = begin + (seg[t * KB + KB - 1] < first_seg).astype(i32)
            outside = (seg[t * KB] != last_seg) | (base + QB - 1 - t * KB >= WINDOW)
            clear = clear + (outside & (t < clear_end)).astype(i32)
        begin = jnp.maximum(begin, jnp.maximum(base - (WINDOW - 1), 0) // KB)
        begin = jnp.minimum(begin, clear_end)
        clear = jnp.clip(clear, begin, clear_end)

        q_at = pl.ds(pl.multiple_of(n * QB, QB), QB)
        nothing = jnp.zeros((QB, half), bf16)
        q = []
        for h in range(heads):
            x = q_all[q_at, h * HD : (h + 1) * HD]
            q.append(jnp.concatenate([x[:, :half], nothing, x[:, half:], nothing], 1))
        low = [starts[pl.ds(base // LANES + g, 1), :] for g in range(QB // LANES)]
        low = jnp.concatenate(low, 1)
        i_pos = base + lax.broadcasted_iota(i32, (1, QB), 1)
        if seq_len > WINDOW:
            low = jnp.maximum(low, i_pos - (WINDOW - 1))

        def score(masked, size, kb, carry):
            start = pl.multiple_of(kb * KB, KB)
            rows_kb = kv[pl.ds(start, size), :]
            if masked:
                j_pos = start + lax.broadcasted_iota(i32, (size, QB), 0)
                allowed = (j_pos <= i_pos) & (j_pos >= low)
            result = []
            for h in range(heads):
                top, total = carry[h]
                lanes = slice(h * QB, (h + 1) * QB)
                s = lax.dot_general(
                    rows_kb, q[h], (((1,), (1,)), ((), ())), preferred_element_type=f32
                )
                if masked:
                    s = jnp.where(allowed, s, -1e30)
                new_top = jnp.maximum(top, jnp.max(s, axis=0, keepdims=True))
                p = jnp.exp2(s - new_top)
                weights[pl.ds(start, size), lanes] = p.astype(bf16)
                tops[pl.ds(kb, 1), lanes] = new_top
                p = jnp.sum(p.reshape(size // 8, 8, QB), axis=0)
                result.append((new_top, total * jnp.exp2(top - new_top) + p))
            return tuple(result)

        state = (jnp.full((1, QB), -1e30, f32), jnp.zeros((8, QB), f32))
        state = (state,) * heads
        pairs = (clear_end - clear) // 2
        single = clear + 2 * pairs
        state = lax.fori_loop(begin, clear, lambda kb, c: score(True, KB, kb, c), state)
        state = lax.fori_loop(
            0, pairs, lambda t, c: score(False, 2 * KB, clear + 2 * t, c), state
        )
        state = lax.fori_loop(single, clear_end, lambda kb, c: score(False, KB, kb, c), state)
        state = lax.fori_loop(0, short, lambda t, c: score(True, QB, clear_end, c), state)
        state = lax.fori_loop(short, 1, lambda t, c: score(True, KB, clear_end, c), state)
        top = jnp.concatenate([t for t, _ in state], 1)
        total = jnp.concatenate([t for _, t in state], 1)
        share = 1.0 / jnp.sum(total, axis=0, keepdims=True)
        row = lax.broadcasted_iota(i32, (16, wide), 0)
        head = lax.broadcasted_iota(i32, (16, wide), 1) // QB

        def gather(size, kb, carry):
            start = pl.multiple_of(kb * KB, KB)
            r = share * jnp.exp2(tops[pl.ds(kb, 1), :] - top)
            high = r.astype(bf16).astype(f32)
            r = jnp.where(row == head, high, jnp.where(row == heads + head, r - high, 0.0))
            at = pl.ds(start, size)
            contract = (((1,), (1,)), ((), ()))
            w = weights[at, :]
            r = r.astype(bf16)
            if COLUMNS_AS_ROWS:
                add = lax.dot_general(r, w, contract, preferred_element_type=f32)
                col[:16, at] = col[:16, at] + add
            else:
                add = lax.dot_general(w, r, contract, preferred_element_type=f32)
                col[at, :16] = col[at, :16] + add
            return carry

        lax.fori_loop(begin, clear, lambda kb, c: gather(KB, kb, c), 0)
        lax.fori_loop(0, pairs, lambda t, c: gather(2 * KB, clear + 2 * t, c), 0)
        lax.fori_loop(single, clear_end, lambda kb, c: gather(KB, kb, c), 0)
        lax.fori_loop(0, short, lambda t, c: gather(QB, clear_end, c), 0)
        lax.fori_loop(short, 1, lambda t, c: gather(KB, clear_end, c), 0)
        return carry

    if balanced:
        low_n = jnp.where(rank == 3, 2, jnp.where(rank == 2, 1, 0))
        high_n = own_blocks + jnp.where(rank == 0, 2, jnp.where(rank == 1, 1, 0))
    else:
        low_n = 0
        high_n = own_blocks
    lax.fori_loop(low_n, high_n, q_step, 0)

    number = jnp.zeros((seg_total, LANES), f32)
    for g in range(seq_len // LANES):
        at = slice(g * LANES, (g + 1) * LANES)
        member = ids[g : g + 1, :] == lax.broadcasted_iota(i32, (seg_total, LANES), 0)
        number = number + member.astype(f32)
        turned = col[:16, at] if COLUMNS_AS_ROWS else col[at, :].T
        for h in range(heads):
            w = turned[h : h + 1] + turned[heads + h : heads + h + 1]
            w = jnp.where(member, w, 0.0)
            high = w.astype(bf16)
            lhs[h * seg_total : (h + 1) * seg_total, at] = high
            rest = (w - high.astype(f32)).astype(bf16)
            lhs[(heads + h) * seg_total : (heads + h + 1) * seg_total, at] = rest
    parts = tokens_out.shape[1] // LANES
    for g in range(parts):
        sums = jnp.zeros((seg_total, LANES), f32)
        for m in range(pieces):
            for first in (g * seg_total, (parts + g) * seg_total):
                sums = sums + tails[m, first : first + seg_total, :].astype(f32)
        tokens_out[:, g * LANES : (g + 1) * LANES] = sums
    counts[...] = jnp.broadcast_to(jnp.sum(number, axis=1, keepdims=True), counts.shape)
    pooled = jnp.dot(lhs[...], kv[...], preferred_element_type=f32)
    pooled = jnp.concatenate([pooled[:, half:HD], pooled[:, HD + half :]], 1)
    for h in range(heads):
        x = pooled[h * seg_total : (h + 1) * seg_total]
        x = x + pooled[(heads + h) * seg_total : (heads + h + 1) * seg_total]
        out[:, h * HD : (h + 1) * HD] = jnp.where(upper, pltpu.roll(x, half, 1), x)


def attend(seg_ids, ids, queries, own, other, feat, seg_total, balanced):
    q_rows, cols = queries[0].shape
    tail = 2 * seg_total * feat // LANES
    seq_len = seg_ids.shape[0]
    pieces = len(own)
    heads = cols // HD
    whole = pl.BlockSpec(memory_space=pltpu.VMEM)
    anywhere = pl.BlockSpec(memory_space=pl.ANY)
    inputs = len(queries) + 2 * pieces

    def body(*refs):
        attend_body(pieces, seg_total, balanced, *refs)

    return pl.pallas_call(
        body,
        in_specs=[pl.BlockSpec(memory_space=pltpu.SMEM), whole]
        + [anywhere] * inputs,
        out_specs=[whole, whole, whole],
        out_shape=[
            jax.ShapeDtypeStruct((seg_total, cols), f32),
            jax.ShapeDtypeStruct((seg_total, LANES), f32),
            jax.ShapeDtypeStruct((seg_total, feat), f32),
        ],
        scratch_shapes=[
            pltpu.VMEM((pieces, tail, HD), bf16),
            pltpu.VMEM((len(queries) * q_rows, cols), bf16),
            pltpu.VMEM((seq_len, 2 * HD), bf16),
            pltpu.VMEM((seq_len // LANES, LANES), i32),
            pltpu.VMEM((seq_len, heads * QB), bf16),
            pltpu.VMEM((max(8, seq_len // KB), heads * QB), f32),
            pltpu.VMEM((16, seq_len) if COLUMNS_AS_ROWS else (seq_len, LANES), f32),
            pltpu.VMEM((2 * heads * seg_total, seq_len), bf16),
            pltpu.SemaphoreType.DMA((inputs + pieces,)),
        ],
        compiler_params=pltpu.CompilerParams(vmem_limit_bytes=24 * MIB),
        cost_estimate=pl.CostEstimate(flops=8 * q_rows * cols * seq_len, bytes_accessed=4 * seq_len * HD, transcendentals=0),
        name="attend",
    )(seg_ids, ids, *queries, *own, *other)


def mix_body(pieces, *refs):
    parts = refs[:pieces]
    norms, w_out, keep, send = refs[pieces:]
    groups, _, feat = keep.shape
    seg_total = parts[0].shape[0]
    mixed = parts[0][...]
    for p in parts[1:]:
        mixed = mixed + p[...]
    high = mixed.astype(bf16)
    low = (mixed - high.astype(f32)).astype(bf16)
    lhs = jnp.concatenate([high, low], 0)
    rank = lax.axis_index("tp")
    for k, target in enumerate((keep, send)):
        for m in range(groups):
            owner = rank ^ (2 * m + k)
            cols = pl.ds(pl.multiple_of(owner * feat, feat), feat)
            y = jnp.dot(lhs, w_out[:, cols], preferred_element_type=f32)
            target[m, :seg_total, :] = y[:seg_total] + y[seg_total:]
            target[m, seg_total:, :] = norms[...]


def mix(parts, norms, w_out, feat, groups):
    seg_total = parts[0].shape[0]
    whole = pl.BlockSpec(memory_space=pltpu.VMEM)
    out = jax.ShapeDtypeStruct((groups, seg_total + 8, feat), f32)

    def body(*refs):
        mix_body(len(parts), *refs)

    return pl.pallas_call(
        body,
        in_specs=[whole] * (len(parts) + 2),
        out_specs=[whole, whole],
        out_shape=[out, out],
        compiler_params=pltpu.CompilerParams(vmem_limit_bytes=16 * MIB),
        name="mix",
    )(*parts, norms, w_out)


def fold_body(groups, edge, keep, received, own, *sends):
    _, rows, cols = keep.shape
    own[...] = keep[0] + received[0]
    for m in range(1, groups):
        total = keep[m] + received[m]
        target = sends[m - 1]
        if edge == "rows":
            inner = rows - 8
            last = total[inner:]
            high = last.astype(bf16).astype(f32)
            target[:inner, :] = total[:inner].astype(bf16)
            target[inner:, :] = jnp.concatenate([high, last - high], 0).astype(bf16)
        else:
            inner = cols - LANES
            last = total[:, inner:]
            high = last.astype(bf16)
            target[:, :inner] = total[:, :inner].astype(bf16)
            target[:, inner:cols] = high
            target[:, cols:] = (last - high.astype(f32)).astype(bf16)


def fold(keep, received, edge):
    groups, rows, cols = keep.shape
    whole = pl.BlockSpec(memory_space=pltpu.VMEM)
    shape = (rows + 8, cols) if edge == "rows" else (rows, cols + LANES)

    def body(*refs):
        fold_body(groups, edge, *refs)

    result = pl.pallas_call(
        body,
        in_specs=[whole, whole],
        out_specs=[whole] * groups,
        out_shape=[jax.ShapeDtypeStruct((rows, cols), f32)]
        + [jax.ShapeDtypeStruct(shape, bf16)] * (groups - 1),
        compiler_params=pltpu.CompilerParams(vmem_limit_bytes=12 * MIB),
        name="fold",
    )(keep, received)
    return [result[0]] + [swapped(result[m], "tp", 2 * m) for m in range(1, groups)]


def owner_span(owner_counts, owner):
    start = jnp.int32(0)
    for o in range(owner_counts.shape[0]):
        start = start + jnp.where(o < owner, owner_counts[o], 0)
    return start, owner_counts[owner]


def cross_body(groups, chunks, model_width, *refs):
    mixed = refs[:groups]
    token_sums, counts, gain, chosen, cent = refs[groups : groups + 5]
    keep, send, emb, norms, lhs = refs[groups + 5 :]
    seg_total, feat = emb.shape
    rows = cent.shape[0]
    slots = keep.shape[1]
    per_side = groups * slots

    total = mixed[0][:seg_total, :] + token_sums[...]
    square = mixed[0][seg_total:, :]
    for p in mixed[1:]:
        total = total + p[:seg_total, :].astype(f32)
        terms = p[seg_total:, :].astype(f32)
        square = square + (terms[:8] + terms[8:])
    norms[...] = square
    pooled = total / counts[:, :1]
    square = jnp.sum(pooled * pooled, axis=1, keepdims=True)
    row = lax.broadcasted_iota(i32, (seg_total, LANES), 0)
    lane = lax.broadcasted_iota(i32, (seg_total, LANES), 1)
    square = jnp.sum(jnp.where(row == lane, square, 0.0), axis=0, keepdims=True)
    square = jnp.broadcast_to(square, (slots, LANES))
    scaled = pooled * gain[...]
    emb[...] = scaled
    high = scaled.astype(bf16)
    low = (scaled - high.astype(f32)).astype(bf16)
    picks = chosen[...].astype(bf16)
    factor = -2.0 / model_width**0.5
    lhs[: 2 * per_side] = (jnp.dot(picks, high, preferred_element_type=f32) * factor).astype(bf16)
    lhs[2 * per_side :] = (jnp.dot(picks, low, preferred_element_type=f32) * factor).astype(bf16)
    for target in (keep, send):
        for m in range(groups):
            target[m, :, rows:] = square

    size = rows // chunks
    for i in range(chunks):
        at = slice(i * size, (i + 1) * size)
        y = lax.dot_general(
            cent[at, :], lhs[...], (((1,), (1,)), ((), ())), preferred_element_type=f32
        ).T
        y = y[: 2 * per_side] + y[2 * per_side :]
        for k, target in enumerate((keep, send)):
            for m in range(groups):
                first = k * per_side + m * slots
                target[m, :, at] = y[first : first + slots]


def cross(mixed, token_sums, counts, gain, chosen, centroids, slots, model_width):
    rows, feat = centroids.shape
    groups = len(mixed)
    seg_total = counts.shape[0]
    whole = pl.BlockSpec(memory_space=pltpu.VMEM)
    side = jax.ShapeDtypeStruct((groups, slots, rows + LANES), f32)

    def body(*refs):
        cross_body(groups, 4, model_width, *refs)

    return pl.pallas_call(
        body,
        in_specs=[whole] * (groups + 5),
        out_specs=[whole] * 4,
        out_shape=[
            side,
            side,
            jax.ShapeDtypeStruct((seg_total, feat), f32),
            jax.ShapeDtypeStruct((8, rows // 8), f32),
        ],
        scratch_shapes=[pltpu.VMEM((4 * groups * slots, feat), bf16)],
        compiler_params=pltpu.CompilerParams(vmem_limit_bytes=16 * MIB),
        name="cross",
    )(*mixed, token_sums, counts, gain, chosen, centroids)


def finish_body(groups, model_width, place, *refs):
    terms = refs[:groups]
    norms, emb, hit, match, picked, wide_in, dist, wide, moved, sems = refs[groups:]
    seg_total, feat = emb.shape
    block = norms.shape[1]
    rows = dist.shape[1]
    total = terms[0][:, rows:]
    for t in terms[1:]:
        total = total + t[:, rows : rows + LANES].astype(f32)
        total = total + t[:, rows + LANES :].astype(f32)
    scale = lax.rsqrt(total / model_width + norm_eps)

    spread = jnp.broadcast_to(scale[:1], (seg_total, LANES))
    r_row = lax.broadcasted_iota(i32, (seg_total, LANES), 0)
    r_lane = lax.broadcasted_iota(i32, (seg_total, LANES), 1)
    row_scale = jnp.sum(jnp.where(r_row == r_lane, spread, 0.0), axis=1, keepdims=True)
    value = emb[...] * row_scale
    high = value.astype(bf16)
    rest = value - high.astype(f32)
    middle = rest.astype(bf16)
    low = (rest - middle.astype(f32)).astype(bf16)
    stacked = jnp.concatenate([high, middle, low], 0)
    once = lax.broadcasted_iota(i32, (3 * seg_total, LANES), 0) < seg_total
    stacked = jnp.concatenate([stacked, jnp.where(once, 1.0, 0.0).astype(bf16)], 1)
    added = jnp.dot(match[...], stacked, preferred_element_type=f32)
    shrink = 1.0 / (1.0 + added[:, feat:])
    for g in range(feat // LANES):
        at = slice(g * LANES, (g + 1) * LANES)
        moved[:, at] = (picked[:, at].astype(f32) + added[:, at]) * shrink

    def write(r):
        first = pl.multiple_of(place[0, r], GROUP)
        return pltpu.make_async_copy(
            moved.at[pl.ds(r * GROUP, GROUP), :], wide.at[pl.ds(first, GROUP), :], sems.at[r]
        )

    for r in range(seg_total):
        pl.when(place[2, r] == 1)(lambda r=r: write(r).start())

    own_scale = jnp.sum(hit[...] * scale, axis=1, keepdims=True)
    valid = jnp.sum(hit[...], axis=1, keepdims=True) > 0.0
    for g in range(rows // block):
        at = slice(g * block, (g + 1) * block)
        y = terms[0][:, at]
        for t in terms[1:]:
            y = y + t[:, at].astype(f32)
        y = norms[g : g + 1, :] * (1.0 / model_width**0.5) + y * own_scale
        dist[:, at] = jnp.where(valid, y, 0.0)

    for r in range(seg_total):
        pl.when(place[2, r] == 1)(lambda r=r: write(r).wait())


def finish(place, terms, norms, emb, hit, match, picked, wide, model_width):
    groups = len(terms)
    seg_total = emb.shape[0]
    slots, rows = terms[0].shape
    rows = rows - LANES
    whole = pl.BlockSpec(memory_space=pltpu.VMEM)
    in_hbm = pl.BlockSpec(memory_space=pltpu.HBM)
    scalar = pl.BlockSpec(memory_space=pltpu.SMEM)

    def body(*refs):
        finish_body(groups, model_width, *refs)

    return pl.pallas_call(
        body,
        in_specs=[scalar] + [whole] * (groups + 5) + [in_hbm],
        out_specs=[whole, in_hbm],
        out_shape=[
            jax.ShapeDtypeStruct((slots, rows), f32),
            jax.ShapeDtypeStruct(wide.shape, f32),
        ],
        scratch_shapes=[
            pltpu.VMEM((seg_total * GROUP, emb.shape[1]), f32),
            pltpu.SemaphoreType.DMA((seg_total,)),
        ],
        input_output_aliases={1 + groups + 5: 1},
        compiler_params=pltpu.CompilerParams(vmem_limit_bytes=16 * MIB),
        name="finish",
    )(place, *terms, norms, emb, hit, match, picked, wide)


def shards(
    tokens, w_query, w_key, w_value, w_out, seg_ids, owner_counts, centroids, pool_gain, assign
):
    tok_rows, model_width = tokens.shape
    seq_len = seg_ids.shape[0]
    seg_total = assign.shape[0]
    rank_seq = lax.axis_index("seq")
    seq_total = lax.axis_size("seq")
    tp_total = lax.axis_size("tp")
    groups = tp_total // 2
    feat = model_width // tp_total
    cent_rows = centroids.shape[0]
    slots = 2 * seg_total // owner_counts.shape[0]
    fine_np, coarse_np = angle_tables(seq_len)
    fine = jnp.asarray(fine_np)
    coarse = jnp.asarray(coarse_np)

    ids = seg_ids.reshape(seq_len // LANES, LANES)
    masks = range(1, seq_total)

    own, tables = project_kv(
        tokens, w_key, w_value, fine, coarse, ids, seg_total, model_width // tp_total
    )
    own = [own] + [swapped(own, "seq", m) for m in masks]
    other = [swapped(x, "tp", 1) for x in own]

    queries = list(project_q(tokens, w_query, tables))
    balanced = seq_total == 4 and seq_len <= WINDOW and tok_rows == 4 * QB
    if balanced:
        queries = queries + [lax.ppermute(queries[0], "seq", [(3, 0), (2, 1)])]

    local = assign - rank_seq * cent_rows
    mine = (local >= 0) & (local < cent_rows)
    first_row = jnp.where(mine, local // GROUP * GROUP, 0)
    line = assign // GROUP
    order = jnp.arange(seg_total, dtype=i32)
    repeat = jnp.any((line[:, None] == line[None, :]) & (order[None, :] < order[:, None]), axis=1)
    place = jnp.stack([first_row, line * GROUP, (mine & ~repeat).astype(i32), assign])
    wide, norms, picked, gain, chosen, hit, match = widen_centroids(
        place, owner_counts, pool_gain.reshape(1, feat), centroids, groups, slots
    )

    queries, wide, norms, picked, gain, chosen, hit, match = lax.optimization_barrier(
        (queries, wide, norms, picked, gain, chosen, hit, match)
    )
    attended, counts, token_sums = attend(
        seg_ids, ids, queries, own, other, feat, seg_total, balanced
    )
    attended = [attended] + [swapped(attended, "seq", m) for m in masks]

    keep, send = mix(attended, norms, w_out, feat, groups)
    mixed = fold(keep, swapped(send, "tp", 1), "rows")

    keep, send, emb, norms = cross(
        mixed, token_sums, counts, gain, chosen, centroids, slots, model_width
    )
    terms = fold(keep, swapped(send, "tp", 1), "columns")
    distances, updated = finish(
        place, terms, norms, emb, hit, match, picked, wide, model_width
    )
    return (distances, updated)


def solution(mesh):
    in_specs = (
        P("seq", None),
        P(None, "tp"),
        P(None, "tp"),
        P(None, "tp"),
        P("tp", None),
        P(),
        P(),
        P("seq", "tp"),
        P("tp"),
        P(),
    )
    out_specs = (P("tp", "seq"), P("seq", "tp"))
    return jax.shard_map(shards, mesh=mesh, in_specs=in_specs, out_specs=out_specs, check_vma=False)
```
